32 devices in a mesh: samp: 4 (over y, x), gx: 2 (over core), gy: 4 (over z).
Axes of the slice: x: 2, y: 2, z: 4, core: 2. Of those that a mesh axis runs over, the one named last changes fastest.
Arguments:
- load: float32 [4, 2, 256, 2048], P('samp', None, 'gx', 'gy'), parts along dimension 0, may hold values from -6 to 6
- material: int32 [4, 32, 256], P('samp', 'gx', 'gy'), parts along dimension 0, may hold values from 0 to 7
- lame_table: float32 [2, 8], replicated, may hold values from 0.3 to 6
Outputs:
- solution: float32 [4, 2, 256, 2048], P('samp', None, 'gx', 'gy'), parts along dimension 0
- residual: float32 [4, 2, 256, 2048], P('samp', None, 'gx', 'gy'), parts along dimension 0
The draws below stay inside these ranges and needn't reach their ends.
There are 4 independent parts, one for each index of `samp`. The reference program is written for one: setup_inputs(seed, part) draws one part's arguments, and reference() takes and returns one part's arrays. A program takes and returns all parts, laid end to end along the dimension named above; an argument that names none is the same for every part. Nothing has to cross between parts.
All inputs are finite; a program needn't handle non-finite values.
Results may differ from the reference program's by a relative error of at most 0.0003.
Values sent between devices are 32-bit elements; how exact they have to be, the bound alone decides.
No kernel may reach another device: no remote copies, remote signals or barrier semaphores. Data moves between devices by JAX's collectives and lax.ppermute only.
A program may use at most 64 MiB of HBM per device.

```python
import math
import jax
import jax.numpy as jnp

SAMPLES = 1
TILE = 8
CLASSES = 8
ITERS = 4
NX = 256
NY = 2048


def plant(result, stream_key, low, top_value):
    spot = [jax.random.randint(jax.random.fold_in(stream_key, axis), (), 0, length) for axis, length in enumerate(result.shape)]
    longest = result.shape.index(max(result.shape))
    beside = spot[:longest] + [(spot[longest] + 1) % result.shape[longest]] + spot[longest + 1:]
    return result.at[tuple(spot)].set(low).at[tuple(beside)].set(top_value)


def steps_of(own_key, shape, split, smallest, top_value):
    gain = 1.0
    for position, blocks in split:
        heights = jax.random.uniform(jax.random.fold_in(jax.random.fold_in(own_key, 6), position), (blocks,), jnp.float32, smallest / len(split), top_value / len(split))
        gain = gain * jnp.repeat(jnp.exp(heights), shape[position] // blocks).reshape((-1,) + (1,) * (len(shape) - 1 - position))
    return gain


def centred(stream_key, shape, deviation, most, cuts=(), kind=jnp.bfloat16):
    entries = deviation * jax.random.normal(stream_key, shape, jnp.float32)
    if cuts:
        entries = entries * steps_of(stream_key, shape, cuts, -0.22, 0.18)
    return jnp.clip(entries, -most, most).astype(kind)


def setup_inputs(seed: int = 0, part: int = 0) -> dict:
    key_of = jax.random.split(jax.random.key(seed), 4)
    part_splits = jax.random.split(jax.random.fold_in(key_of[3], part), 4)
    return {
        "load": centred(part_splits[0], (SAMPLES, 2, NX, NY), 1.0, 6.0, ((2, 2), (3, 4)), jnp.float32),
        "material": plant(jax.random.randint(part_splits[1], (SAMPLES, NX // TILE, NY // TILE), 0, CLASSES), jax.random.fold_in(part_splits[1], 1), 0, CLASSES - 1).astype(jnp.int32),
        "lame_table": jnp.clip(jnp.exp(jax.random.uniform(key_of[2], (2, CLASSES), jnp.float32, math.log(0.3), math.log(6.0))), 0.3, 6.0),
    }


def cell_moduli(material, lame_table):
    classes = jnp.arange(CLASSES, dtype=jnp.int32)
    match = (material[..., None] == classes).astype(jnp.float32)
    lam = jnp.sum(match * lame_table[0], axis=-1)
    mu = jnp.sum(match * lame_table[1], axis=-1)

    def expand(tiles):
        count, rows, cols = tiles.shape
        wide = jnp.broadcast_to(tiles[:, :, None, :, None], (count, rows, TILE, cols, TILE))
        return wide.reshape(count, rows * TILE, cols * TILE)

    return expand(lam), expand(mu)


def cell_terms(nodes, lam, mu):
    low_low = nodes[..., :-1, :-1]
    high_low = nodes[..., 1:, :-1]
    low_high = nodes[..., :-1, 1:]
    high_high = nodes[..., 1:, 1:]
    along_x = 0.5 * ((high_low + high_high) - (low_low + low_high))
    along_y = 0.5 * ((low_high + high_high) - (low_low + high_low))
    strain_xx = along_x[:, 0]
    strain_yy = along_y[:, 1]
    shear = along_y[:, 0] + along_x[:, 1]
    stiff = lam + 2.0 * mu
    stress_xx = stiff * strain_xx + lam * strain_yy
    stress_yy = lam * strain_xx + stiff * strain_yy
    stress_xy = mu * shear
    plus = 0.5 * jnp.stack([stress_xx + stress_xy, stress_xy + stress_yy], axis=1)
    minus = 0.5 * jnp.stack([stress_xx - stress_xy, stress_xy - stress_yy], axis=1)
    return plus, minus


def operate(field, lam_pad, mu_pad):
    padded = jnp.pad(field, ((0, 0), (0, 0), (1, 1), (1, 1)))
    plus, minus = cell_terms(padded, lam_pad, mu_pad)
    forces = plus[..., :-1, :-1] - plus[..., 1:, 1:] + minus[..., :-1, 1:] - minus[..., 1:, :-1]
    return 0.05 * field + forces


def reference(load, material, lame_table):
    lam, mu = cell_moduli(material, lame_table)
    lam_pad = jnp.pad(lam, ((0, 0), (1, 0), (1, 0)))
    mu_pad = jnp.pad(mu, ((0, 0), (1, 0), (1, 0)))
    solution = jnp.zeros_like(load)
    residual = load
    w_vec = operate(residual, lam_pad, mu_pad)
    z_vec = jnp.zeros_like(load)
    q_vec = jnp.zeros_like(load)
    p_vec = jnp.zeros_like(load)
    gamma_prev = jnp.ones((load.shape[0],), jnp.float32)
    alpha_prev = jnp.ones((load.shape[0],), jnp.float32)
    for step in range(ITERS):
        gamma = jnp.sum(residual * residual, axis=(1, 2, 3))
        delta = jnp.sum(w_vec * residual, axis=(1, 2, 3))
        if step == 0:
            beta = jnp.zeros_like(gamma)
            alpha = gamma / delta
        else:
            beta = gamma / gamma_prev
            alpha = gamma / (delta - beta * gamma / alpha_prev)
        beta_b = beta[:, None, None, None]
        alpha_b = alpha[:, None, None, None]
        if step + 1 < ITERS:
            n_vec = operate(w_vec, lam_pad, mu_pad)
            z_vec = n_vec + beta_b * z_vec
        q_vec = w_vec + beta_b * q_vec
        p_vec = residual + beta_b * p_vec
        solution = solution + alpha_b * p_vec
        residual = residual - alpha_b * q_vec
        if step + 1 < ITERS:
            w_vec = w_vec - alpha_b * z_vec
        gamma_prev = gamma
        alpha_prev = alpha
    return solution, residual
```

```python
import functools

import jax
import jax.numpy as jnp
from jax import lax
from jax.experimental import pallas as pl
from jax.experimental.pallas import tpu as pltpu
from jax.sharding import PartitionSpec as P

TILE = 8
CLASSES = 8
ITERS = 4
HALO = ITERS
LANES = 128
STRIP = 2 * TILE
F32 = jnp.float32


def iota(shape, dim):
    return lax.broadcasted_iota(jnp.int32, shape, dim)


def fast_two_sum(a, b):
    s = a + b
    return s, b - (s - a)


def two_sum(a, b):
    s = a + b
    t = s - a
    return s, (a - (s - t)) + (b - t)


def split(a):
    t = 4097.0 * a
    high = t - (t - a)
    return high, a - high


def two_prod(a, b):
    p = a * b
    ah, al = split(a)
    bh, bl = split(b)
    return p, ((ah * bh - p) + ah * bl + al * bh) + al * bl


def ds_add(x, y):
    s, e = two_sum(x[0], y[0])
    return fast_two_sum(s, e + (x[1] + y[1]))


def ds_mul(x, y):
    p, e = two_prod(x[0], y[0])
    return fast_two_sum(p, e + (x[0] * y[1] + x[1] * y[0]))


def ds_neg(x):
    return -x[0], -x[1]


def ds_div(x, y):
    inverse = 1.0 / y[0]
    first = x[0] * inverse
    p, e = two_prod(first, y[0])
    rest = ((x[0] - p) - e) + (x[1] - first * y[1])
    return fast_two_sum(first, rest * inverse)


def stress(c, n, lam, mu, right):
    rows = c[0][0].shape
    last = iota(rows, 0) == TILE - 1
    along_x, along_y = [], []
    for comp in range(2):
        tile, up = c[comp]
        down = jnp.where(last, n[comp][1], up)
        diff = down - tile
        total = down + tile
        along_x.append(diff + right(diff))
        along_y.append(right(total) - total)
    exx, eyy = along_x[0], along_y[1]
    trace = lam * (exx + eyy)
    two_mu = mu + mu
    return trace + two_mu * exx, trace + two_mu * eyy, mu * (along_y[0] + along_x[1])


def moved(s):
    return tuple(pltpu.roll(x, 1, 0) for x in s)


def forces(s, here, before, left):
    first = iota(s[0].shape, 0) == 0
    xx, yy, xy = s
    pxx, pyy, pxy = (jnp.where(first, b, h) for b, h in zip(before, here))
    dxx = pxx - xx
    sxy = pxy + xy
    dxy = pxy - xy
    syy = pyy + yy
    return left(dxx + sxy) + (dxx - sxy), left(dxy + syy) + (dxy - syy)


def apply(v, k, tiles, moduli, edge_moduli, edge_mask, right, left):
    def load(t):
        pair = [v[k, c, TILE * t : TILE * (t + 1), :] for c in range(2)]
        return [(x, pltpu.roll(x, TILE - 1, 0)) for x in pair]

    first = load(0)
    edge = load(tiles)
    edge_stress = stress(edge, first, *edge_moduli, right)
    edge_moved = moved(edge_stress)
    before = edge_moved
    here = first
    own = jnp.zeros(first[0][0].shape, F32)
    cross = own
    for t in range(tiles):
        after = load(t + 1)
        s = stress(here, after, *moduli(t), right)
        m = moved(s)
        push = forces(s, m, before, left)
        for c in range(2):
            old = here[c][0]
            new = 0.05 * old + push[c]
            v[k + 1, c, TILE * t : TILE * (t + 1), :] = new
            own = own + old * old
            cross = cross + old * new
        before = m
        here = after
    if k + 1 < ITERS:
        push = forces(edge_stress, edge_moved, before, left)
        for c in range(2):
            new = (0.05 * edge[c][0] + push[c]) * edge_mask
            v[k + 1, c, TILE * tiles : TILE * (tiles + 1), :] = new
    return own, cross


def moment_rows(parts, keep):
    row = iota((2 * ITERS, LANES), 0)
    result = jnp.zeros((2 * ITERS, LANES), F32)
    for index, part in enumerate(parts):
        part = jnp.where(keep, part, 0.0)
        folded = part[:, :LANES]
        for start in range(LANES, part.shape[1], LANES):
            folded = folded + part[:, start : start + LANES]
        total = jnp.sum(folded, axis=0, keepdims=True)
        result = jnp.where(row == index, total, result)
    return result


def prepare(table, top, bottom, material, moduli, *packets, gx):
    rows, cols = material.shape[1:]
    width = top.shape[3]
    spread = iota((cols, width), 1) // TILE == iota((cols, width), 0)
    kinds = jnp.dot(
        material[0].astype(F32).astype(jnp.bfloat16),
        spread.astype(F32).astype(jnp.bfloat16),
        preferred_element_type=F32,
    )
    for which in range(2):
        values = jnp.zeros((rows, width), F32)
        for k in range(CLASSES):
            values = jnp.where(kinds == float(k), 0.25 * table[which, k], values)
        moduli[which] = values
    place = lax.axis_index("gx")

    def fill(packet, down):
        for c in range(2):
            packet[c] = jnp.where(down, bottom[0, c], top[0, c])
            row = jnp.where(down, moduli[c, rows - 1 : rows, :], moduli[c, 0:1, :])
            packet[2, c : c + 1, :] = row
        packet[2, 2:, :] = jnp.zeros((TILE - 2, width), F32)

    if gx == 2:
        fill(packets[0], place == 0)
    else:
        fill(packets[0], True)
        fill(packets[1], False)


def block(load, moduli, above, below, v, packet, *, gx):
    rows, width = load.shape[2:]
    tiles = rows // TILE
    place = lax.axis_index("gx")
    has_above = place > 0
    has_below = place < gx - 1
    sub = iota((TILE, width), 0)
    low = sub < HALO

    def beside(a, b):
        return jnp.where(low, jnp.where(has_below, b, 0.0), jnp.where(has_above, a, 0.0))

    for c in range(2):
        v[0, c, :rows, :] = load[0, c]
        v[0, c, rows : rows + TILE, :] = beside(above[c], below[c])
    edge = [beside(above[2, c : c + 1, :], below[2, c : c + 1, :]) for c in range(2)]
    mask = jnp.where(low, jnp.where(has_below, 1.0, 0.0), 1.0)

    def row_of(t):
        return tuple(jnp.broadcast_to(moduli[c, t : t + 1, :], (TILE, width)) for c in range(2))

    right = lambda x: pltpu.roll(x, width - 1, 1)
    left = lambda x: pltpu.roll(x, 1, 1)
    parts = []
    for k in range(ITERS):
        parts += apply(v, k, tiles, row_of, edge, mask, right, left)
    lane = iota((TILE, width), 1)
    keep = (lane >= HALO) & (lane < width - HALO)
    packet_rows = packet.shape[0]
    packet[packet_rows - TILE :, :] = moment_rows(parts, keep)

    lane = iota((TILE, LANES), 1)
    short = iota((TILE, LANES), 0)
    tile_rows = moduli.shape[1]
    for group in range(packet_rows // TILE - 1):
        result = jnp.zeros((TILE, LANES), F32)
        for part in range(4):
            slot = 4 * group + part
            for c in range(2):
                offset = 32 * part + 16 * c
                if slot <= tiles:
                    ends = [v[0, c, TILE * slot : TILE * (slot + 1), s] for s in (slice(0, LANES), slice(width - LANES, width))]
                elif TILE * (slot - tiles - 1) < tile_rows:
                    first = TILE * (slot - tiles - 1)
                    ends = [moduli[c, first : first + TILE, s] for s in (slice(0, LANES), slice(width - LANES, width))]
                elif TILE * (slot - tiles - 1) == tile_rows:
                    ends = []
                    for s in (slice(0, LANES), slice(width - LANES, width)):
                        x = edge[c][:, s]
                        ends.append(jnp.where(short == 0, x[0:1, :], x[TILE - 1 :, :]))
                else:
                    continue
                first, final = ends
                first = pltpu.roll(first, offset, 1) if offset else first
                final = pltpu.roll(final, (offset + STRIP) % LANES, 1)
                result = jnp.where((lane >= offset) & (lane < offset + TILE), first, result)
                result = jnp.where((lane >= offset + TILE) & (lane < offset + STRIP), final, result)
        packet[TILE * group : TILE * (group + 1), :] = result


def interfaces(*refs, gx, gy, tiles, sources):
    packets = refs[:gy]
    v, moments, lam_rows = refs[gy:]
    mine = lax.axis_index("gy")
    place = lax.axis_index("gx")
    has_below = place < gx - 1
    groups = packets[0].shape[0] // TILE - 1

    def sort(rows):
        arrived = [p[rows, :] for p in packets]
        result = []
        for q in range(gy):
            chosen = arrived[0]
            for k in range(1, gy):
                chosen = jnp.where(sources(mine, k) == q, arrived[k], chosen)
            result.append(chosen)
        return result

    lane = iota((TILE, LANES), 1)
    sub = iota((TILE, LANES), 0)
    for group in range(groups):
        pieces = sort(slice(TILE * group, TILE * (group + 1)))
        for part in range(4):
            slot = 4 * group + part
            for c in range(2):
                result = jnp.zeros((TILE, LANES), F32)
                for q in range(gy):
                    shift = (STRIP * q - 32 * part - 16 * c) % LANES
                    piece = pltpu.roll(pieces[q], shift, 1) if shift else pieces[q]
                    result = jnp.where((lane >= STRIP * q) & (lane < STRIP * (q + 1)), piece, result)
                if slot <= tiles:
                    v[0, c, TILE * slot : TILE * (slot + 1), :] = result
                else:
                    first = TILE * (slot - tiles - 1)
                    if first + TILE <= lam_rows.shape[1]:
                        lam_rows[c, first : first + TILE, :] = result
    low = sub < HALO
    edge = [jnp.where(low, lam_rows[c, tiles : tiles + 1, :], lam_rows[c, tiles + 1 : tiles + 2, :]) for c in range(2)]
    mask = jnp.where(low, jnp.where(has_below, 1.0, 0.0), 1.0)

    def row_of(t):
        return tuple(jnp.broadcast_to(lam_rows[c, t : t + 1, :], (TILE, LANES)) for c in range(2))

    at_end = lane == STRIP * gy - 1
    at_start = lane == 0
    right = lambda x: jnp.where(at_end, 0.0, pltpu.roll(x, LANES - 1, 1))
    left = lambda x: jnp.where(at_start, 0.0, pltpu.roll(x, 1, 1))
    parts = []
    for k in range(ITERS):
        parts += apply(v, k, tiles, row_of, edge, mask, right, left)
    column = lane % STRIP
    keep = ((column < HALO) | (column >= STRIP - HALO)) & (lane < STRIP * gy)
    high = moment_rows(parts, keep)
    rest = jnp.zeros_like(high)
    for piece in sort(slice(TILE * groups, TILE * (groups + 1))):
        high, e = two_sum(high, piece)
        rest = rest + e
    moments[0] = high
    moments[1] = rest


def coefficients(moments):
    shape = moments[0].shape
    take = lambda x, l: jnp.broadcast_to(x[l : l + 1, :], shape)
    s = [(take(moments[0], l), take(moments[1], l)) for l in range(2 * ITERS)]
    q = list(s)
    zero = (jnp.zeros(shape, F32), jnp.zeros(shape, F32))
    one = (jnp.ones(shape, F32), zero[0])
    solution = []
    residual = [one]
    direction = []
    for k in range(ITERS):
        if k:
            beta = ds_neg(ds_div(ds_mul(alpha, s[k]), previous))
            q = [None] * k + [ds_add(s[l], ds_mul(beta, q[l])) if l < len(s) else None for l in range(k, len(q))]
            q = q[: len(s)]
            grown = [ds_mul(beta, x) for x in direction] + [None]
            direction = [ds_add(r, g) if g is not None else r for r, g in zip(residual, grown)]
        else:
            direction = [one]
        alpha = ds_div(s[k], q[k + 1])
        previous = s[k]
        if k + 1 < ITERS:
            s = [None] * (k + 1) + [ds_add(s[l], ds_neg(ds_mul(alpha, q[l + 1]))) for l in range(k + 1, len(s) - 1)]
        step = [ds_mul(alpha, x) for x in direction]
        solution = [ds_add(a, b) for a, b in zip(solution, step)] + [step[-1]]
        residual = [residual[0]] + [ds_add(r, ds_neg(b)) for r, b in zip(residual[1:], step)] + [ds_neg(step[-1])]
    return [x[0] for x in solution], [x[0] for x in residual]


def combine(*refs, gx):
    gathered = refs[:gx]
    v, strips, solution, residual = refs[gx:]
    rows, width = solution.shape[2:]
    total = (gathered[0][0], gathered[0][1])
    for other in gathered[1:]:
        total = ds_add(total, (other[0], other[1]))
    distance = LANES // 2
    while distance:
        total = ds_add(total, tuple(pltpu.roll(x, distance, 1) for x in total))
        distance //= 2
    weights = coefficients(total)
    mine = lax.axis_index("gy")
    lane = iota((TILE, LANES), 1)
    to_left = lax.rem(LANES - STRIP * mine, LANES)
    to_right = lax.rem(2 * LANES - STRIP - STRIP * mine, LANES)
    for t in range(rows // TILE):
        at = slice(TILE * t, TILE * (t + 1))
        for c in range(2):
            for out, w in zip((solution, residual), weights):
                edge = sum(w[k] * strips[k, c, at, :] for k in range(len(w)))
                for start in range(0, width, LANES):
                    value = sum(w[k] * v[k, c, at, start : start + LANES] for k in range(len(w)))
                    if start == 0:
                        value = jnp.where(lane < HALO, pltpu.roll(edge, to_left, 1), value)
                    if start + LANES == width:
                        value = jnp.where(lane >= LANES - HALO, pltpu.roll(edge, to_right, 1), value)
                    out[0, c, at, start : start + LANES] = value


def routes(n):
    if n & (n - 1) == 0:
        return [[(i, i ^ k) for i in range(n)] for k in range(1, n)]
    return [[(i, (i + k) % n) for i in range(n)] for k in range(1, n)]


def source_of(n):
    if n & (n - 1) == 0:
        return lambda mine, k: mine ^ k
    return lambda mine, k: lax.rem(mine - k + n, n)


def on_device(load, material, lame_table):
    gx, gy = lax.axis_size("gx"), lax.axis_size("gy")
    rows, width = load.shape[2:]
    tiles = rows // TILE
    tile_rows = material.shape[1]
    vmem = pl.BlockSpec(memory_space=pltpu.VMEM)
    shape = lambda *dims: jax.ShapeDtypeStruct(dims, F32)

    packets = 1 if gx == 2 else 2
    moduli, *sent = pl.pallas_call(
        functools.partial(prepare, gx=gx),
        grid=(1,),
        in_specs=[
            pl.BlockSpec(memory_space=pltpu.SMEM),
            pl.BlockSpec((1, 2, TILE, width), lambda i: (0, 0, 0, 0)),
            pl.BlockSpec((1, 2, TILE, width), lambda i: (0, 0, tiles - 1, 0)),
            pl.BlockSpec(material.shape, lambda i: (0, 0, 0)),
        ],
        out_specs=[pl.BlockSpec((2, tile_rows, width), lambda i: (0, 0, 0))]
        + [pl.BlockSpec((3, TILE, width), lambda i: (0, 0, 0))] * packets,
        out_shape=[shape(2, tile_rows, width)] + [shape(3, TILE, width)] * packets,
        name="prepare",
    )(lame_table, load, load, material)

    if gx == 2:
        above = below = lax.ppermute(sent[0], "gx", [(0, 1), (1, 0)])
    else:
        above = lax.ppermute(sent[0], "gx", [(i, i + 1) for i in range(gx - 1)])
        below = lax.ppermute(sent[1], "gx", [(i + 1, i) for i in range(gx - 1)])

    slots = tiles + 1 + -(-(tile_rows + 2) // TILE)
    packet_rows = TILE * (-(-slots // 4) + 1)
    v, packet = pl.pallas_call(
        functools.partial(block, gx=gx),
        in_specs=[vmem] * 4,
        out_specs=[vmem] * 2,
        out_shape=[shape(ITERS + 1, 2, rows + TILE, width), shape(packet_rows, LANES)],
        name="block",
    )(load, moduli, above, below)

    arrived = [packet] + [lax.ppermute(packet, "gy", route) for route in routes(gy)]
    strips, moments = pl.pallas_call(
        functools.partial(interfaces, gx=gx, gy=gy, tiles=tiles, sources=source_of(gy)),
        in_specs=[vmem] * gy,
        out_specs=[vmem] * 2,
        out_shape=[shape(ITERS + 1, 2, rows + TILE, LANES), shape(2, 2 * ITERS, LANES)],
        scratch_shapes=[pltpu.VMEM((2, tile_rows + TILE, LANES), F32)],
        name="interfaces",
    )(*arrived)

    gathered = [moments] + [lax.ppermute(moments, "gx", route) for route in routes(gx)]
    return pl.pallas_call(
        functools.partial(combine, gx=gx),
        in_specs=[vmem] * (gx + 2),
        out_specs=[vmem] * 2,
        out_shape=[shape(*load.shape)] * 2,
        name="combine",
    )(*gathered, v, strips)


def solution(mesh):
    return jax.shard_map(
        on_device,
        mesh=mesh,
        in_specs=(P("samp", None, "gx", "gy"), P("samp", "gx", "gy"), P()),
        out_specs=(P("samp", None, "gx", "gy"), P("samp", None, "gx", "gy")),
        check_vma=False,
    )
```

```python
import functools

import jax
import jax.numpy as jnp
from jax import lax
from jax.experimental import pallas as pl
from jax.experimental.pallas import tpu as pltpu
from jax.sharding import PartitionSpec as P

TILE = 8
CLASSES = 8
ITERS = 4
HALO = ITERS
LANES = 128
STRIP = 2 * TILE
VMEM_LIMIT = 16 << 20
F32 = jnp.float32


def iota(shape, dim):
    return lax.broadcasted_iota(jnp.int32, shape, dim)


def fast_two_sum(a, b):
    s = a + b
    return s, b - (s - a)


def two_sum(a, b):
    s = a + b
    t = s - a
    return s, (a - (s - t)) + (b - t)


def split(a):
    t = 4097.0 * a
    high = t - (t - a)
    return high, a - high


def two_prod(a, b):
    p = a * b
    ah, al = split(a)
    bh, bl = split(b)
    return p, ((ah * bh - p) + ah * bl + al * bh) + al * bl


def ds_add(x, y):
    s, e = two_sum(x[0], y[0])
    return fast_two_sum(s, e + (x[1] + y[1]))


def ds_mul(x, y):
    p, e = two_prod(x[0], y[0])
    return fast_two_sum(p, e + (x[0] * y[1] + x[1] * y[0]))


def ds_neg(x):
    return -x[0], -x[1]


def ds_div(x, y):
    inverse = 1.0 / y[0]
    first = x[0] * inverse
    p, e = two_prod(first, y[0])
    rest = ((x[0] - p) - e) + (x[1] - first * y[1])
    return fast_two_sum(first, rest * inverse)


def stress(c, n, lam, mu, right):
    rows = c[0][0].shape
    last = iota(rows, 0) == TILE - 1
    along_x, along_y = [], []
    for comp in range(2):
        tile, up = c[comp]
        down = jnp.where(last, n[comp][1], up)
        diff = down - tile
        total = down + tile
        along_x.append(diff + right(diff))
        along_y.append(right(total) - total)
    exx, eyy = along_x[0], along_y[1]
    trace = lam * (exx + eyy)
    two_mu = mu + mu
    return trace + two_mu * exx, trace + two_mu * eyy, mu * (along_y[0] + along_x[1])


def moved(s):
    return tuple(pltpu.roll(x, 1, 0) for x in s)


def forces(s, here, before, left):
    first = iota(s[0].shape, 0) == 0
    xx, yy, xy = s
    pxx, pyy, pxy = (jnp.where(first, b, h) for b, h in zip(before, here))
    dxx = pxx - xx
    sxy = pxy + xy
    dxy = pxy - xy
    syy = pyy + yy
    return left(dxx + sxy) + (dxx - sxy), left(dxy + syy) + (dxy - syy)


def apply(v, k, tiles, moduli, edge_moduli, edge_mask, right, left):
    def load(t):
        pair = [v[k, c, TILE * t : TILE * (t + 1), :] for c in range(2)]
        return [(x, pltpu.roll(x, TILE - 1, 0)) for x in pair]

    first = load(0)
    edge = load(tiles)
    edge_stress = stress(edge, first, *edge_moduli, right)
    edge_moved = moved(edge_stress)
    before = edge_moved
    here = first
    own = jnp.zeros(first[0][0].shape, F32)
    cross = own
    for t in range(tiles):
        after = load(t + 1)
        s = stress(here, after, *moduli(t), right)
        m = moved(s)
        push = forces(s, m, before, left)
        for c in range(2):
            old = here[c][0]
            new = 0.05 * old + push[c]
            v[k + 1, c, TILE * t : TILE * (t + 1), :] = new
            own = own + old * old
            cross = cross + old * new
        before = m
        here = after
    if k + 1 < ITERS:
        push = forces(edge_stress, edge_moved, before, left)
        for c in range(2):
            new = (0.05 * edge[c][0] + push[c]) * edge_mask
            v[k + 1, c, TILE * tiles : TILE * (tiles + 1), :] = new
    return own, cross


def moment_rows(parts, keep):
    row = iota((2 * ITERS, LANES), 0)
    result = jnp.zeros((2 * ITERS, LANES), F32)
    for index, part in enumerate(parts):
        part = jnp.where(keep, part, 0.0)
        folded = part[:, :LANES]
        for start in range(LANES, part.shape[1], LANES):
            folded = folded + part[:, start : start + LANES]
        total = jnp.sum(folded, axis=0, keepdims=True)
        result = jnp.where(row == index, total, result)
    return result


def prepare(table, top, bottom, material, moduli, *packets, gx):
    rows, cols = material.shape[1:]
    width = top.shape[3]
    spread = iota((cols, width), 1) // TILE == iota((cols, width), 0)
    kinds = jnp.dot(
        material[0].astype(F32).astype(jnp.bfloat16),
        spread.astype(F32).astype(jnp.bfloat16),
        preferred_element_type=F32,
    )
    for which in range(2):
        values = jnp.zeros((rows, width), F32)
        for k in range(CLASSES):
            values = jnp.where(kinds == float(k), 0.25 * table[which, k], values)
        moduli[which] = values
    place = lax.axis_index("gx")

    def fill(packet, down):
        for c in range(2):
            packet[c] = jnp.where(down, bottom[0, c], top[0, c])
            row = jnp.where(down, moduli[c, rows - 1 : rows, :], moduli[c, 0:1, :])
            packet[2, c : c + 1, :] = row
        packet[2, 2:, :] = jnp.zeros((TILE - 2, width), F32)

    if gx == 2:
        fill(packets[0], place == 0)
    else:
        fill(packets[0], True)
        fill(packets[1], False)


def block(load, moduli, above, below, v, packet, *, gx):
    rows, width = load.shape[2:]
    tiles = rows // TILE
    place = lax.axis_index("gx")
    has_above = place > 0
    has_below = place < gx - 1
    sub = iota((TILE, width), 0)
    low = sub < HALO

    def beside(a, b):
        return jnp.where(low, jnp.where(has_below, b, 0.0), jnp.where(has_above, a, 0.0))

    for c in range(2):
        v[0, c, :rows, :] = load[0, c]
        v[0, c, rows : rows + TILE, :] = beside(above[c], below[c])
    edge = [beside(above[2, c : c + 1, :], below[2, c : c + 1, :]) for c in range(2)]
    mask = jnp.where(low, jnp.where(has_below, 1.0, 0.0), 1.0)

    def row_of(t):
        return tuple(jnp.broadcast_to(moduli[c, t : t + 1, :], (TILE, width)) for c in range(2))

    right = lambda x: pltpu.roll(x, width - 1, 1)
    left = lambda x: pltpu.roll(x, 1, 1)
    parts = []
    for k in range(ITERS):
        parts += apply(v, k, tiles, row_of, edge, mask, right, left)
    lane = iota((TILE, width), 1)
    keep = (lane >= HALO) & (lane < width - HALO)
    packet_rows = packet.shape[0]
    packet[packet_rows - TILE :, :] = moment_rows(parts, keep)

    lane = iota((TILE, LANES), 1)
    short = iota((TILE, LANES), 0)
    tile_rows = moduli.shape[1]
    for group in range(packet_rows // TILE - 1):
        result = jnp.zeros((TILE, LANES), F32)
        for part in range(4):
            slot = 4 * group + part
            for c in range(2):
                offset = 32 * part + 16 * c
                if slot <= tiles:
                    ends = [v[0, c, TILE * slot : TILE * (slot + 1), s] for s in (slice(0, LANES), slice(width - LANES, width))]
                elif TILE * (slot - tiles - 1) < tile_rows:
                    first = TILE * (slot - tiles - 1)
                    ends = [moduli[c, first : first + TILE, s] for s in (slice(0, LANES), slice(width - LANES, width))]
                elif TILE * (slot - tiles - 1) == tile_rows:
                    ends = []
                    for s in (slice(0, LANES), slice(width - LANES, width)):
                        x = edge[c][:, s]
                        ends.append(jnp.where(short == 0, x[0:1, :], x[TILE - 1 :, :]))
                else:
                    continue
                first, final = ends
                first = pltpu.roll(first, offset, 1) if offset else first
                final = pltpu.roll(final, (offset + STRIP) % LANES, 1)
                result = jnp.where((lane >= offset) & (lane < offset + TILE), first, result)
                result = jnp.where((lane >= offset + TILE) & (lane < offset + STRIP), final, result)
        packet[TILE * group : TILE * (group + 1), :] = result


def interfaces(*refs, gx, gy, tiles, sources):
    packets = refs[:gy]
    v, moments, lam_rows = refs[gy:]
    mine = lax.axis_index("gy")
    place = lax.axis_index("gx")
    has_below = place < gx - 1
    groups = packets[0].shape[0] // TILE - 1

    def sort(rows):
        arrived = [p[rows, :] for p in packets]
        result = []
        for q in range(gy):
            chosen = arrived[0]
            for k in range(1, gy):
                chosen = jnp.where(sources(mine, k) == q, arrived[k], chosen)
            result.append(chosen)
        return result

    lane = iota((TILE, LANES), 1)
    sub = iota((TILE, LANES), 0)
    for group in range(groups):
        pieces = sort(slice(TILE * group, TILE * (group + 1)))
        for part in range(4):
            slot = 4 * group + part
            for c in range(2):
                result = jnp.zeros((TILE, LANES), F32)
                for q in range(gy):
                    shift = (STRIP * q - 32 * part - 16 * c) % LANES
                    piece = pltpu.roll(pieces[q], shift, 1) if shift else pieces[q]
                    result = jnp.where((lane >= STRIP * q) & (lane < STRIP * (q + 1)), piece, result)
                if slot <= tiles:
                    v[0, c, TILE * slot : TILE * (slot + 1), :] = result
                else:
                    first = TILE * (slot - tiles - 1)
                    if first + TILE <= lam_rows.shape[1]:
                        lam_rows[c, first : first + TILE, :] = result
    low = sub < HALO
    edge = [jnp.where(low, lam_rows[c, tiles : tiles + 1, :], lam_rows[c, tiles + 1 : tiles + 2, :]) for c in range(2)]
    mask = jnp.where(low, jnp.where(has_below, 1.0, 0.0), 1.0)

    def row_of(t):
        return tuple(jnp.broadcast_to(lam_rows[c, t : t + 1, :], (TILE, LANES)) for c in range(2))

    at_end = lane == STRIP * gy - 1
    at_start = lane == 0
    right = lambda x: jnp.where(at_end, 0.0, pltpu.roll(x, LANES - 1, 1))
    left = lambda x: jnp.where(at_start, 0.0, pltpu.roll(x, 1, 1))
    parts = []
    for k in range(ITERS):
        parts += apply(v, k, tiles, row_of, edge, mask, right, left)
    column = lane % STRIP
    keep = ((column < HALO) | (column >= STRIP - HALO)) & (lane < STRIP * gy)
    high = moment_rows(parts, keep)
    rest = jnp.zeros_like(high)
    for piece in sort(slice(TILE * groups, TILE * (groups + 1))):
        high, e = two_sum(high, piece)
        rest = rest + e
    moments[0] = high
    moments[1] = rest


def coefficients(moments):
    shape = moments[0].shape
    take = lambda x, l: jnp.broadcast_to(x[l : l + 1, :], shape)
    s = [(take(moments[0], l), take(moments[1], l)) for l in range(2 * ITERS)]
    q = list(s)
    zero = (jnp.zeros(shape, F32), jnp.zeros(shape, F32))
    one = (jnp.ones(shape, F32), zero[0])
    solution = []
    residual = [one]
    direction = []
    for k in range(ITERS):
        if k:
            beta = ds_neg(ds_div(ds_mul(alpha, s[k]), previous))
            q = [None] * k + [ds_add(s[l], ds_mul(beta, q[l])) if l < len(s) else None for l in range(k, len(q))]
            q = q[: len(s)]
            grown = [ds_mul(beta, x) for x in direction] + [None]
            direction = [ds_add(r, g) if g is not None else r for r, g in zip(residual, grown)]
        else:
            direction = [one]
        alpha = ds_div(s[k], q[k + 1])
        previous = s[k]
        if k + 1 < ITERS:
            s = [None] * (k + 1) + [ds_add(s[l], ds_neg(ds_mul(alpha, q[l + 1]))) for l in range(k + 1, len(s) - 1)]
        step = [ds_mul(alpha, x) for x in direction]
        solution = [ds_add(a, b) for a, b in zip(solution, step)] + [step[-1]]
        residual = [residual[0]] + [ds_add(r, ds_neg(b)) for r, b in zip(residual[1:], step)] + [ds_neg(step[-1])]
    return [x[0] for x in solution], [x[0] for x in residual]


def combine(*refs, gx):
    gathered = refs[:gx]
    v, strips, solution, residual = refs[gx:]
    rows, width = solution.shape[2:]
    total = (gathered[0][0], gathered[0][1])
    for other in gathered[1:]:
        total = ds_add(total, (other[0], other[1]))
    distance = LANES // 2
    while distance:
        total = ds_add(total, tuple(pltpu.roll(x, distance, 1) for x in total))
        distance //= 2
    weights = coefficients(total)
    mine = lax.axis_index("gy")
    lane = iota((TILE, LANES), 1)
    to_left = lax.rem(LANES - STRIP * mine, LANES)
    to_right = lax.rem(2 * LANES - STRIP - STRIP * mine, LANES)
    for t in range(rows // TILE):
        at = slice(TILE * t, TILE * (t + 1))
        for c in range(2):
            for out, w in zip((solution, residual), weights):
                edge = sum(w[k] * strips[k, c, at, :] for k in range(len(w)))
                for start in range(0, width, LANES):
                    value = sum(w[k] * v[k, c, at, start : start + LANES] for k in range(len(w)))
                    if start == 0:
                        value = jnp.where(lane < HALO, pltpu.roll(edge, to_left, 1), value)
                    if start + LANES == width:
                        value = jnp.where(lane >= LANES - HALO, pltpu.roll(edge, to_right, 1), value)
                    out[0, c, at, start : start + LANES] = value


def routes(n):
    if n & (n - 1) == 0:
        return [[(i, i ^ k) for i in range(n)] for k in range(1, n)]
    return [[(i, (i + k) % n) for i in range(n)] for k in range(1, n)]


def source_of(n):
    if n & (n - 1) == 0:
        return lambda mine, k: mine ^ k
    return lambda mine, k: lax.rem(mine - k + n, n)


def on_device(load, material, lame_table):
    gx, gy = lax.axis_size("gx"), lax.axis_size("gy")
    rows, width = load.shape[2:]
    tiles = rows // TILE
    tile_rows = material.shape[1]
    vmem = pl.BlockSpec(memory_space=pltpu.VMEM)
    shape = lambda *dims: pltpu.VMEM(dims, F32)
    params = pltpu.CompilerParams(vmem_limit_bytes=VMEM_LIMIT)
    pin = lambda x: pltpu.with_memory_space_constraint(x, pltpu.VMEM)

    packets = 1 if gx == 2 else 2
    moduli, *sent = pl.pallas_call(
        functools.partial(prepare, gx=gx),
        grid=(1,),
        in_specs=[
            pl.BlockSpec(memory_space=pltpu.SMEM),
            pl.BlockSpec((1, 2, TILE, width), lambda i: (0, 0, 0, 0)),
            pl.BlockSpec((1, 2, TILE, width), lambda i: (0, 0, tiles - 1, 0)),
            pl.BlockSpec(material.shape, lambda i: (0, 0, 0)),
        ],
        out_specs=[pl.BlockSpec((2, tile_rows, width), lambda i: (0, 0, 0))]
        + [pl.BlockSpec((3, TILE, width), lambda i: (0, 0, 0))] * packets,
        out_shape=[shape(2, tile_rows, width)] + [shape(3, TILE, width)] * packets,
        compiler_params=params,
        name="prepare",
    )(*(pltpu.with_memory_space_constraint(x, pltpu.HBM) for x in (lame_table, load, load, material)))

    if gx == 2:
        above = below = lax.ppermute(sent[0], "gx", [(0, 1), (1, 0)])
    else:
        above = lax.ppermute(sent[0], "gx", [(i, i + 1) for i in range(gx - 1)])
        below = lax.ppermute(sent[1], "gx", [(i + 1, i) for i in range(gx - 1)])

    slots = tiles + 1 + -(-(tile_rows + 2) // TILE)
    packet_rows = TILE * (-(-slots // 4) + 1)
    v, packet = pl.pallas_call(
        functools.partial(block, gx=gx),
        in_specs=[vmem] * 4,
        out_specs=[vmem] * 2,
        out_shape=[shape(ITERS + 1, 2, rows + TILE, width), shape(packet_rows, LANES)],
        compiler_params=params,
        name="block",
    )(pin(load), pin(moduli), pin(above), pin(below))

    arrived = [packet] + [lax.ppermute(packet, "gy", route) for route in routes(gy)]
    strips, moments = pl.pallas_call(
        functools.partial(interfaces, gx=gx, gy=gy, tiles=tiles, sources=source_of(gy)),
        in_specs=[vmem] * gy,
        out_specs=[vmem] * 2,
        out_shape=[shape(ITERS + 1, 2, rows + TILE, LANES), shape(2, 2 * ITERS, LANES)],
        scratch_shapes=[pltpu.VMEM((2, tile_rows + TILE, LANES), F32)],
        compiler_params=params,
        name="interfaces",
    )(*map(pin, arrived))

    gathered = [moments] + [lax.ppermute(moments, "gx", route) for route in routes(gx)]
    return pl.pallas_call(
        functools.partial(combine, gx=gx),
        in_specs=[vmem] * (gx + 2),
        out_specs=[vmem] * 2,
        out_shape=[jax.ShapeDtypeStruct(load.shape, F32)] * 2,
        compiler_params=params,
        name="combine",
    )(*map(pin, gathered), pin(v), pin(strips))


def solution(mesh):
    return jax.shard_map(
        on_device,
        mesh=mesh,
        in_specs=(P("samp", None, "gx", "gy"), P("samp", "gx", "gy"), P()),
        out_specs=(P("samp", None, "gx", "gy"), P("samp", None, "gx", "gy")),
        check_vma=False,
    )
```

```python
import functools

import jax
import jax.numpy as jnp
from jax import lax
from jax.experimental import pallas as pl
from jax.experimental.pallas import tpu as pltpu
from jax.sharding import PartitionSpec as P

TILE = 8
CLASSES = 8
ITERS = 4
HALO = ITERS
LANES = 128
STRIP = 2 * TILE
VMEM_LIMIT = 16 << 20
F32 = jnp.float32


def iota(shape, dim):
    return lax.broadcasted_iota(jnp.int32, shape, dim)


def fast_two_sum(a, b):
    s = a + b
    return s, b - (s - a)


def two_sum(a, b):
    s = a + b
    t = s - a
    return s, (a - (s - t)) + (b - t)


def split(a):
    t = 4097.0 * a
    high = t - (t - a)
    return high, a - high


def two_prod(a, b):
    p = a * b
    ah, al = split(a)
    bh, bl = split(b)
    return p, ((ah * bh - p) + ah * bl + al * bh) + al * bl


def ds_add(x, y):
    s, e = two_sum(x[0], y[0])
    return fast_two_sum(s, e + (x[1] + y[1]))


def ds_mul(x, y):
    p, e = two_prod(x[0], y[0])
    return fast_two_sum(p, e + (x[0] * y[1] + x[1] * y[0]))


def ds_neg(x):
    return -x[0], -x[1]


def ds_scale(c, x):
    p, e = two_prod(jnp.full(x[0].shape, c, F32), x[0])
    return fast_two_sum(p, e + c * x[1])


def ds_inverse(x):
    first = 1.0 / x[0]
    p, e = two_prod(first, x[0])
    rest = ((1.0 - p) - e) - first * x[1]
    return fast_two_sum(first, first * rest)


def spread(x, right):
    beside = right(x)
    return x + beside, beside - x


def stress(here, below, bulk, mu):
    (p0, m0), (p1, m1) = here
    (n0, o0), (n1, o1) = below
    exx, eyy = n0 - p0, o1 + m1
    gxy = (o0 + m0) + (n1 - p1)
    mean = bulk * (exx + eyy)
    apart = mu * (exx - eyy)
    return mean + apart, mean - apart, mu * gxy


def forces(before, s, left):
    pxx, pyy, pxy = before
    xx, yy, xy = s
    dxx = pxx - xx
    sxy = pxy + xy
    dxy = pxy - xy
    syy = pyy + yy
    return left(dxx + sxy) + (dxx - sxy), left(dxy + syy) + (dxy - syy)


def apply(k, v, strips, moduli, partial, mask, tiles, right, left):
    groups = tiles // TILE
    sub = iota(strips.shape[2:], 0)
    up = lambda x: pltpu.roll(x, TILE - 1, 0)
    down = lambda x: pltpu.roll(x, 1, 0)
    tile = lambda c, t: v[k, c, TILE * t : TILE * (t + 1), :]
    modulus = lambda g: (moduli[0, g], moduli[1, g])

    top, bottom = ([strips[s, c] for c in range(2)] for s in range(2))
    above = [jnp.where(sub == 0, pltpu.roll(top[c], 5, 0), down(tile(c, tiles - 1))) for c in range(2)]
    below = [jnp.where(sub == TILE - 1, pltpu.roll(bottom[c], 3, 0), up(tile(c, 0))) for c in range(2)]

    for s, old in enumerate((top, bottom)):
        here = [spread(x, right) for x in old]
        after = [(up(p), up(m)) for p, m in here]
        t = stress(here, after, *modulus(groups + 1 + s))
        new = forces(tuple(down(x) for x in t), t, left)
        for c in range(2):
            strips[s, c] = new[c] * mask if s else new[c]

    own = cross = None
    old = [tile(c, 0) for c in range(2)]
    here = [spread(x, right) for x in old]
    before = stress([spread(x, right) for x in above], here, *modulus(groups))
    for t in range(tiles):
        ahead = [tile(c, t + 1) for c in range(2)] if t + 1 < tiles else below
        after = [spread(x, right) for x in ahead]
        s = stress(here, after, *modulus(t // TILE))
        new = forces(before, s, left)
        square = old[0] * old[0] + old[1] * old[1]
        mixed = old[0] * new[0] + old[1] * new[1]
        own = square if own is None else own + square
        cross = mixed if cross is None else cross + mixed
        for c in range(2):
            v[k + 1, c, TILE * t : TILE * (t + 1), :] = new[c]
        before, here, old = s, after, ahead
    partial[2 * k] = own
    partial[2 * k + 1] = cross


def moment_rows(partial, keep):
    row = iota((2 * ITERS, LANES), 0)
    result = jnp.zeros((2 * ITERS, LANES), F32)
    for index in range(2 * ITERS):
        part = jnp.where(keep, partial[index], 0.0)
        folded = part[:, :LANES]
        for start in range(LANES, part.shape[1], LANES):
            folded = folded + part[:, start : start + LANES]
        total = jnp.sum(folded, axis=0, keepdims=True)
        result = jnp.where(row == index, total, result)
    return result


def fill_moduli(moduli, c, groups, first, last, edge):
    sub = iota(edge.shape, 0)
    low = sub < HALO
    above, below = edge[1:2, :], edge[0:1, :]
    moduli[c, groups] = jnp.where(sub == 0, above, pltpu.roll(moduli[c, groups - 1], 1, 0))
    moduli[c, groups + 1] = jnp.where(low, above, first)
    moduli[c, groups + 2] = jnp.where(low, last, below)


def fill_strips(strips, c, halo, first, last):
    low = iota(halo.shape, 0) < HALO
    strips[0, c] = pltpu.roll(jnp.where(low, first, halo), HALO, 0)
    strips[1, c] = pltpu.roll(jnp.where(low, halo, last), HALO, 0)


def prepare(table, load, material, u, moduli, *rest, gx):
    *packets, kinds_buffer, lines, sems = rest
    rows, cols = material.shape[1:]
    height, width = load.shape[2:]
    groups = rows // TILE
    columns = [slice(start, start + LANES) for start in range(0, width, LANES)]
    ends = [slice(0, TILE), slice(height - TILE, height)]
    first = pltpu.make_async_copy(material.at[0], kinds_buffer, sems.at[0, 0])
    first.start()
    copies = []
    for i, at in enumerate(ends + [slice(TILE, height - TILE)]):
        copies.append([])
        for l, lanes in enumerate(columns):
            copy = pltpu.make_async_copy(load.at[0, :, at, lanes], u.at[:, l, at, :], sems.at[i + 1, l])
            copy.start()
            copies[i].append(copy)
    first.wait()
    grid = (cols, width)
    expand = iota(grid, 1) // TILE == iota(grid, 0)
    kinds = jnp.dot(
        kinds_buffer[...].astype(F32).astype(jnp.bfloat16),
        expand.astype(F32).astype(jnp.bfloat16),
        preferred_element_type=F32,
    )
    bulk = jnp.zeros((rows, width), F32)
    shear = bulk
    for k in range(CLASSES):
        mu = 0.25 * table[1, k]
        here = kinds == float(k)
        bulk = jnp.where(here, 0.25 * table[0, k] + mu, bulk)
        shear = jnp.where(here, mu, shear)
    for c, values in enumerate((bulk, shear)):
        for l, lanes in enumerate(columns):
            lines[c, l] = values[:, lanes]
            for g in range(groups):
                moduli[c, g, :, lanes] = lines[c, l, pl.ds(g, TILE, stride=groups), :]
    place = lax.axis_index("gx")
    for copy in copies[0] + copies[1]:
        copy.wait()

    def fill(packet, down):
        for c in range(2):
            for l, lanes in enumerate(columns):
                packet[c, :, lanes] = jnp.where(down, u[c, l, ends[1], :], u[c, l, ends[0], :])
            row = jnp.where(down, moduli[c, groups - 1, TILE - 1 :, :], moduli[c, 0, 0:1, :])
            packet[2, c : c + 1, :] = row
        packet[2, 2:, :] = jnp.zeros((TILE - 2, width), F32)

    if gx == 2:
        fill(packets[0], place == 0)
    else:
        fill(packets[0], True)
        fill(packets[1], False)
    for copy in copies[2]:
        copy.wait()


def block(u, group_moduli, above, below, v, packet, strips, moduli, partial, *, gx):
    rows, width = v.shape[2:]
    tiles = rows // TILE
    columns = [slice(start, start + LANES) for start in range(0, width, LANES)]
    groups = tiles // TILE
    place = lax.axis_index("gx")
    has_above = place > 0
    has_below = place < gx - 1
    sub = iota((TILE, width), 0)
    low = sub < HALO

    halo, edge = [], []
    for c in range(2):
        under = jnp.where(has_below, below[c], 0.0)
        over = jnp.where(has_above, above[c], 0.0)
        halo.append(jnp.where(low, under, over))
        ends = (
            jnp.concatenate([u[c, l, at, :] for l in range(len(columns))], axis=1)
            for at in (slice(0, TILE), slice(rows - TILE, rows))
        )
        fill_strips(strips, c, halo[c], *ends)
        for t in range(tiles):
            for l, lanes in enumerate(columns):
                v[0, c, TILE * t : TILE * (t + 1), lanes] = u[c, l, pl.ds(t, TILE, stride=tiles), :]
        for g in range(groups):
            moduli[c, g] = group_moduli[c, g]
        under = jnp.where(has_below, below[2, c : c + 1, :], 0.0)
        over = jnp.where(has_above, above[2, c : c + 1, :], 0.0)
        edge.append(jnp.where(sub == 0, under, over))
        ends = moduli[c, 0, 0:1, :], moduli[c, groups - 1, TILE - 1 :, :]
        fill_moduli(moduli, c, groups, *ends, edge[c])
    mask = jnp.where(low, 1.0, jnp.where(has_below, 1.0, 0.0))
    right = lambda x: pltpu.roll(x, width - 1, 1)
    left = lambda x: pltpu.roll(x, 1, 1)

    lane = iota((TILE, LANES), 1)
    packet_rows = packet.shape[0]
    for group in range(packet_rows // TILE - 1):
        result = jnp.zeros((TILE, LANES), F32)
        for part in range(4):
            slot = 4 * group + part
            for c in range(2):
                if slot < tiles:
                    pick = lambda s: v[0, c, TILE * slot : TILE * (slot + 1), s]
                elif slot == tiles:
                    pick = lambda s: halo[c][:, s]
                elif slot <= tiles + groups:
                    pick = lambda s: moduli[c, slot - tiles - 1, :, s]
                elif slot == tiles + groups + 1:
                    pick = lambda s: edge[c][:, s]
                else:
                    continue
                offset = 32 * part + STRIP * c
                first = pick(slice(0, LANES))
                first = pltpu.roll(first, offset, 1) if offset else first
                final = pltpu.roll(pick(slice(width - LANES, width)), (offset + STRIP) % LANES, 1)
                result = jnp.where((lane >= offset) & (lane < offset + TILE), first, result)
                result = jnp.where((lane >= offset + TILE) & (lane < offset + STRIP), final, result)
        packet[TILE * group : TILE * (group + 1), :] = result

    @pl.loop(0, ITERS)
    def _(k):
        apply(k, v, strips, moduli, partial, mask, tiles, right, left)

    lane = iota((TILE, width), 1)
    keep = (lane >= HALO) & (lane < width - HALO)
    packet[packet_rows - TILE :, :] = moment_rows(partial, keep)


def interfaces(*refs, gx, gy, sources):
    packets = refs[:gy]
    v, moments, strips, moduli, partial = refs[gy:]
    tiles = v.shape[2] // TILE
    groups = tiles // TILE
    mine = lax.axis_index("gy")
    has_below = lax.axis_index("gx") < gx - 1
    lines = packets[0].shape[0] // TILE - 1

    def sort(rows):
        arrived = [p[rows, :] for p in packets]
        result = []
        for q in range(gy):
            chosen = arrived[0]
            for k in range(1, gy):
                chosen = jnp.where(sources(mine, k) == q, arrived[k], chosen)
            result.append(chosen)
        return result

    lane = iota((TILE, LANES), 1)
    sub = iota((TILE, LANES), 0)
    halo, edge = [None] * 2, [None] * 2
    for line in range(lines):
        pieces = sort(slice(TILE * line, TILE * (line + 1)))
        for part in range(4):
            slot = 4 * line + part
            for c in range(2):
                result = jnp.zeros((TILE, LANES), F32)
                for q in range(gy):
                    shift = (STRIP * q - 32 * part - STRIP * c) % LANES
                    piece = pltpu.roll(pieces[q], shift, 1) if shift else pieces[q]
                    result = jnp.where((lane >= STRIP * q) & (lane < STRIP * (q + 1)), piece, result)
                if slot < tiles:
                    v[0, c, TILE * slot : TILE * (slot + 1), :] = result
                elif slot == tiles:
                    halo[c] = result
                elif slot <= tiles + groups:
                    moduli[c, slot - tiles - 1] = result
                elif slot == tiles + groups + 1:
                    edge[c] = result
    for c in range(2):
        first = last = halo[c]
        for r in range(HALO):
            row = TILE * r
            first = jnp.where(sub == r, v[0, c, row : row + 1, :], first)
            row = TILE * (tiles - r) - 1
            last = jnp.where(sub == TILE - 1 - r, v[0, c, row : row + 1, :], last)
        fill_strips(strips, c, halo[c], first, last)
        ends = moduli[c, 0, 0:1, :], moduli[c, groups - 1, TILE - 1 :, :]
        fill_moduli(moduli, c, groups, *ends, edge[c])
    mask = jnp.where(sub < HALO, 1.0, jnp.where(has_below, 1.0, 0.0))
    at_end = lane == STRIP * gy - 1
    at_start = lane == 0
    right = lambda x: jnp.where(at_end, 0.0, pltpu.roll(x, LANES - 1, 1))
    left = lambda x: jnp.where(at_start, 0.0, pltpu.roll(x, 1, 1))

    @pl.loop(0, ITERS)
    def _(k):
        apply(k, v, strips, moduli, partial, mask, tiles, right, left)

    column = lane % STRIP
    keep = ((column < HALO) | (column >= STRIP - HALO)) & (lane < STRIP * gy)
    high = moment_rows(partial, keep)
    rest = jnp.zeros_like(high)
    for piece in sort(slice(TILE * lines, TILE * (lines + 1))):
        high, e = two_sum(high, piece)
        rest = rest + e
    moments[0] = high
    moments[1] = rest


def coefficients(moments):
    shape = moments[0].shape
    take = lambda x, l: jnp.broadcast_to(x[l : l + 1, :], shape)
    s = {l: (take(moments[0], l), take(moments[1], l)) for l in range(2 * ITERS)}
    q = dict(s)
    zero = jnp.zeros(shape, F32)
    residual = [zero + 1.0]
    solution = []
    for k in range(ITERS):
        if k:
            beta = ds_neg(ds_mul(s[k], inverse))
            q = {l: ds_add(s[l], ds_mul(beta, q[l])) for l in range(k, 2 * ITERS - k)}
            direction = [r + beta[0] * p for r, p in zip(residual, direction + [zero])]
        else:
            direction = residual
        push = {l: ds_add(ds_scale(0.05, q[l]), q[l + 1]) for l in range(k, 2 * ITERS - 1 - k)}
        inverse = ds_inverse(push[k])
        alpha = ds_mul(s[k], inverse)
        s = {l: ds_add(s[l], ds_neg(ds_mul(alpha, push[l]))) for l in range(k + 1, 2 * ITERS - 1 - k)}
        solution = [x + alpha[0] * p for x, p in zip(solution + [zero], direction)]
        change = [0.05 * a + b for a, b in zip(direction + [zero], [zero] + direction)]
        residual = [r - alpha[0] * d for r, d in zip(residual + [zero], change)]
    return solution, residual


def combine(*refs, gx):
    gathered = refs[:gx]
    v, strips, *outs, buffer, sems = refs[gx:]
    rows, width = v.shape[2:]
    tiles = rows // TILE
    columns = [slice(start, start + LANES) for start in range(0, width, LANES)]
    total = (gathered[0][0], gathered[0][1])
    for other in gathered[1:]:
        total = ds_add(total, (other[0], other[1]))
    distance = LANES // 2
    while distance:
        total = ds_add(total, tuple(pltpu.roll(x, distance, 1) for x in total))
        distance //= 2
    weights = coefficients(total)
    mine = lax.axis_index("gy")
    lane = iota((TILE, LANES), 1)
    to_left = lax.rem(LANES - STRIP * mine, LANES)
    to_right = lax.rem(2 * LANES - STRIP - STRIP * mine, LANES)
    copies = []
    for c in range(2):
        for i, w in enumerate(weights):

            @pl.loop(0, tiles, unroll=2)
            def _(t):
                at = pl.ds(pl.multiple_of(TILE * t, TILE), TILE)
                edge = sum(w[k] * strips[k, c, at, :] for k in range(len(w)))
                for l, lanes in enumerate(columns):
                    value = sum(w[k] * v[k, c, at, lanes] for k in range(len(w)))
                    if l == 0:
                        value = jnp.where(lane < HALO, pltpu.roll(edge, to_left, 1), value)
                    if l + 1 == len(columns):
                        value = jnp.where(lane >= LANES - HALO, pltpu.roll(edge, to_right, 1), value)
                    buffer[i, c, l, pl.ds(t, TILE, stride=tiles), :] = value

            for l, lanes in enumerate(columns):
                copy = pltpu.make_async_copy(buffer.at[i, c, l], outs[i].at[0, c, :, lanes], sems.at[i, c, l])
                copy.start()
                copies.append(copy)
    for copy in copies:
        copy.wait()


def routes(n):
    if n & (n - 1) == 0:
        return [[(i, i ^ k) for i in range(n)] for k in range(1, n)]
    return [[(i, (i + k) % n) for i in range(n)] for k in range(1, n)]


def source_of(n):
    if n & (n - 1) == 0:
        return lambda mine, k: mine ^ k
    return lambda mine, k: lax.rem(mine - k + n, n)


def on_device(load, material, lame_table):
    gx, gy = lax.axis_size("gx"), lax.axis_size("gy")
    rows, width = load.shape[2:]
    tiles = rows // TILE
    groups = tiles // TILE
    lines = width // LANES
    tile_rows, tile_cols = material.shape[1:]
    assert rows == TILE * TILE * groups and width % LANES == 0 and STRIP * gy <= LANES
    vmem = pl.BlockSpec(memory_space=pltpu.VMEM)
    hbm = pl.BlockSpec(memory_space=pltpu.HBM)
    shape = lambda *dims: pltpu.VMEM(dims, F32)
    params = pltpu.CompilerParams(vmem_limit_bytes=VMEM_LIMIT)
    pin = lambda x: pltpu.with_memory_space_constraint(x, pltpu.VMEM)
    far = lambda x: pltpu.with_memory_space_constraint(x, pltpu.HBM)
    work = lambda lanes: [
        pltpu.VMEM((2, 2, TILE, lanes), F32),
        pltpu.VMEM((2, groups + 3, TILE, lanes), F32),
        pltpu.VMEM((2 * ITERS, TILE, lanes), F32),
    ]

    packets = 1 if gx == 2 else 2
    u, moduli, *sent = pl.pallas_call(
        functools.partial(prepare, gx=gx),
        in_specs=[pl.BlockSpec(memory_space=pltpu.SMEM), hbm, hbm],
        out_specs=[vmem] * (2 + packets),
        out_shape=[shape(2, lines, rows, LANES), shape(2, groups, TILE, width)] + [shape(3, TILE, width)] * packets,
        scratch_shapes=[
            pltpu.VMEM((tile_rows, tile_cols), jnp.int32),
            pltpu.VMEM((2, lines, tile_rows, LANES), F32),
            pltpu.SemaphoreType.DMA((4, lines)),
        ],
        compiler_params=params,
        name="prepare",
    )(far(lame_table), far(load), far(material))

    if gx == 2:
        above = below = lax.ppermute(sent[0], "gx", [(0, 1), (1, 0)])
    else:
        above = lax.ppermute(sent[0], "gx", [(i, i + 1) for i in range(gx - 1)])
        below = lax.ppermute(sent[1], "gx", [(i + 1, i) for i in range(gx - 1)])

    slots = tiles + groups + 2
    packet_rows = TILE * (-(-slots // 4) + 1)
    v, packet = pl.pallas_call(
        functools.partial(block, gx=gx),
        in_specs=[vmem] * 4,
        out_specs=[vmem] * 2,
        out_shape=[shape(ITERS + 1, 2, rows, width), shape(packet_rows, LANES)],
        scratch_shapes=work(width),
        compiler_params=params,
        name="block",
    )(pin(u), pin(moduli), pin(above), pin(below))

    arrived = [packet] + [lax.ppermute(packet, "gy", route) for route in routes(gy)]
    strips, moments = pl.pallas_call(
        functools.partial(interfaces, gx=gx, gy=gy, sources=source_of(gy)),
        in_specs=[vmem] * gy,
        out_specs=[vmem] * 2,
        out_shape=[shape(ITERS + 1, 2, rows, LANES), shape(2, 2 * ITERS, LANES)],
        scratch_shapes=work(LANES),
        compiler_params=params,
        name="interfaces",
    )(*map(pin, arrived))

    gathered = [moments] + [lax.ppermute(moments, "gx", route) for route in routes(gx)]
    return pl.pallas_call(
        functools.partial(combine, gx=gx),
        in_specs=[vmem] * (gx + 2),
        out_specs=[hbm] * 2,
        out_shape=[jax.ShapeDtypeStruct(load.shape, F32)] * 2,
        scratch_shapes=[pltpu.VMEM((2, 2, lines, rows, LANES), F32), pltpu.SemaphoreType.DMA((2, 2, lines))],
        compiler_params=params,
        name="combine",
    )(*map(pin, gathered), pin(v), pin(strips))


def solution(mesh):
    return jax.shard_map(
        on_device,
        mesh=mesh,
        in_specs=(P("samp", None, "gx", "gy"), P("samp", "gx", "gy"), P()),
        out_specs=(P("samp", None, "gx", "gy"), P("samp", None, "gx", "gy")),
        check_vma=False,
    )
```

```python
import functools

import jax
import jax.numpy as jnp
from jax import lax
from jax.experimental import pallas as pl
from jax.experimental.pallas import tpu as pltpu
from jax.sharding import PartitionSpec as P

TILE = 8
CLASSES = 8
ITERS = 4
HALO = ITERS
LANES = 128
STRIP = 2 * TILE
VMEM_LIMIT = 16 << 20
F32 = jnp.float32


def iota(shape, dim):
    return lax.broadcasted_iota(jnp.int32, shape, dim)


def fast_two_sum(a, b):
    s = a + b
    return s, b - (s - a)


def two_sum(a, b):
    s = a + b
    t = s - a
    return s, (a - (s - t)) + (b - t)


def split(a):
    t = 4097.0 * a
    high = t - (t - a)
    return high, a - high


def two_prod(a, b):
    p = a * b
    ah, al = split(a)
    bh, bl = split(b)
    return p, ((ah * bh - p) + ah * bl + al * bh) + al * bl


def ds_add(x, y):
    s, e = two_sum(x[0], y[0])
    return fast_two_sum(s, e + (x[1] + y[1]))


def ds_mul(x, y):
    p, e = two_prod(x[0], y[0])
    return fast_two_sum(p, e + (x[0] * y[1] + x[1] * y[0]))


def ds_neg(x):
    return -x[0], -x[1]


def ds_scale(c, x):
    p, e = two_prod(jnp.full(x[0].shape, c, F32), x[0])
    return fast_two_sum(p, e + c * x[1])


def ds_inverse(x):
    first = 1.0 / x[0]
    p, e = two_prod(first, x[0])
    rest = ((1.0 - p) - e) - first * x[1]
    return fast_two_sum(first, first * rest)


def stress(here, below, bulk, mu):
    sums, gaps = [], []
    for (x, right), (y, beside) in zip(here, below):
        sums.append((x + right, y + beside))
        gaps.append((right - x, beside - y))
    exx = sums[0][1] - sums[0][0]
    eyy = gaps[1][1] + gaps[1][0]
    gxy = (gaps[0][1] + gaps[0][0]) + (sums[1][1] - sums[1][0])
    mean = bulk * (exx + eyy)
    apart = mu * (exx - eyy)
    return mean + apart, mean - apart, mu * gxy


def forces(before, s):
    pxx, pyy, pxy = before
    xx, yy, xy = s
    dxx = pxx - xx
    sxy = pxy + xy
    dxy = pxy - xy
    syy = pyy + yy
    return (dxx + sxy, dxx - sxy), (dxy + syy, dxy - syy)


def basis(v, strips, beside, push, moduli, partial, mask, right, left, clear):
    tiles = v.shape[2]
    groups = tiles // TILE
    sub = iota(strips.shape[2:], 0)
    up = lambda x: pltpu.roll(x, TILE - 1, 0)
    down = lambda x: pltpu.roll(x, 1, 0)
    modulus = lambda g: (moduli[0, g], moduli[1, g])

    for c in range(2):
        for t in range(tiles):
            beside[c, t] = right(v[0, c, t])
        for s in range(2):
            beside[c, tiles + s] = right(strips[s, c])

    @pl.loop(0, ITERS)
    def _(k):
        last = jnp.maximum(k - 1, 0)
        tile = lambda c, t: (v[k, c, t], beside[c, t])
        top, bottom = ([(strips[s, c], beside[c, tiles + s]) for c in range(2)] for s in range(2))
        for s, here in enumerate((top, bottom)):
            t = stress(here, [(up(x), up(y)) for x, y in here], *modulus(groups + 1 + s))
            for c, (x, y) in enumerate(forces(tuple(down(x) for x in t), t)):
                push[0, c, tiles + s], push[1, c, tiles + s] = (x * mask, y * mask) if s else (x, y)
        above, below = [], []
        for c in range(2):
            join = lambda x, y: jnp.where(sub == 0, pltpu.roll(x, 5, 0), down(y))
            above.append(tuple(map(join, top[c], tile(c, tiles - 1))))
            join = lambda x, y: jnp.where(sub == TILE - 1, pltpu.roll(x, 3, 0), up(y))
            below.append(tuple(map(join, bottom[c], tile(c, 0))))

        own = cross = None
        here = [tile(c, 0) for c in range(2)]
        before = stress(above, here, *modulus(groups))
        for t in range(tiles):
            after = [tile(c, t + 1) for c in range(2)] if t + 1 < tiles else below
            s = stress(here, after, *modulus(t // TILE))
            for c, (x, y) in enumerate(forces(before, s)):
                push[0, c, t], push[1, c, t] = x, y
            square = here[0][0] * here[0][0] + here[1][0] * here[1][0]
            mixed = v[last, 0, t] * here[0][0] + v[last, 1, t] * here[1][0]
            own = square if own is None else own + square
            cross = mixed if cross is None else cross + mixed
            before, here = s, after
        partial[2 * last + 1] = cross
        partial[2 * k] = own

        for t in range(tiles + 2):
            for c in range(2):
                x, y = push[0, c, t], push[1, c, t]
                beside[c, t] = clear(x + right(y))
                if t < tiles:
                    v[k + 1, c, t] = left(x) + y
                else:
                    strips[t - tiles, c] = left(x) + y

    cross = None
    for t in range(tiles):
        mixed = v[ITERS - 1, 0, t] * v[ITERS, 0, t] + v[ITERS - 1, 1, t] * v[ITERS, 1, t]
        cross = mixed if cross is None else cross + mixed
    partial[2 * ITERS - 1] = cross


def moment_rows(partial, keep):
    row = iota((2 * ITERS, LANES), 0)
    result = jnp.zeros((2 * ITERS, LANES), F32)
    for index in range(2 * ITERS):
        part = jnp.where(keep, partial[index], 0.0)
        folded = part[:, :LANES]
        for start in range(LANES, part.shape[1], LANES):
            folded = folded + part[:, start : start + LANES]
        total = jnp.sum(folded, axis=0, keepdims=True)
        result = jnp.where(row == index, total, result)
    return result


def fill_moduli(moduli, c, groups, first, last, edge):
    sub = iota(edge.shape, 0)
    low = sub < HALO
    above, below = edge[1:2, :], edge[0:1, :]
    moduli[c, groups] = jnp.where(sub == 0, above, pltpu.roll(moduli[c, groups - 1], 1, 0))
    moduli[c, groups + 1] = jnp.where(low, above, first)
    moduli[c, groups + 2] = jnp.where(low, last, below)


def fill_strips(strips, c, halo, v):
    sub = iota(halo.shape, 0)
    low = sub < HALO
    tiles = v.shape[2]
    first = last = halo
    for r in range(HALO):
        first = jnp.where(sub == r, v[0, c, r, 0:1, :], first)
        last = jnp.where(sub == TILE - 1 - r, v[0, c, tiles - 1 - r, TILE - 1 :, :], last)
    strips[0, c] = pltpu.roll(jnp.where(low, first, halo), HALO, 0)
    strips[1, c] = pltpu.roll(jnp.where(low, halo, last), HALO, 0)


def prepare(table, load, material, v, moduli, *rest, gx):
    *packets, kinds_buffer, lines, ends, scalars, sems = rest
    rows, cols = material.shape[1:]
    height, width = load.shape[2:]
    tiles = height // TILE
    groups = tiles // TILE
    columns = [slice(start, start + LANES) for start in range(0, width, LANES)]
    early = [pltpu.make_async_copy(material.at[0], kinds_buffer, sems.at[2, 0])]
    for i, at in enumerate((slice(0, TILE), slice(height - TILE, height))):
        early.append(pltpu.make_async_copy(load.at[0, :, at, :], ends.at[i], sems.at[2, i + 1]))
    early.append(pltpu.make_async_copy(table, scalars, sems.at[2, 3]))
    late = []
    for c in range(2):
        for s in range(TILE):
            at = slice(tiles * s, tiles * (s + 1))
            late.append(pltpu.make_async_copy(load.at[0, c, at, :], v.at[0, c, :, s, :], sems.at[c, s]))
    for copy in early + late:
        copy.start()
    early[0].wait()
    grid = (cols, width)
    expand = iota(grid, 1) // TILE == iota(grid, 0)
    kinds = jnp.dot(
        kinds_buffer[...].astype(F32).astype(jnp.bfloat16),
        expand.astype(F32).astype(jnp.bfloat16),
        preferred_element_type=F32,
    )
    early[3].wait()
    bulk = jnp.zeros((rows, width), F32)
    shear = bulk
    for k in range(CLASSES):
        mu = 0.25 * scalars[1, k]
        here = kinds == float(k)
        bulk = jnp.where(here, 0.25 * scalars[0, k] + mu, bulk)
        shear = jnp.where(here, mu, shear)
    for c, values in enumerate((bulk, shear)):
        for l, lanes in enumerate(columns):
            lines[c, l] = values[:, lanes]
            for g in range(groups):
                moduli[c, g, :, lanes] = lines[c, l, pl.ds(g, TILE, stride=groups), :]
    place = lax.axis_index("gx")
    for copy in early[1:3]:
        copy.wait()

    def fill(packet, down):
        for c in range(2):
            packet[c] = jnp.where(down, ends[1, c], ends[0, c])
            row = jnp.where(down, moduli[c, groups - 1, TILE - 1 :, :], moduli[c, 0, 0:1, :])
            packet[2, c : c + 1, :] = row
        packet[2, 2:, :] = jnp.zeros((TILE - 2, width), F32)

    if gx == 2:
        fill(packets[0], place == 0)
    else:
        fill(packets[0], True)
        fill(packets[1], False)
    for copy in late:
        copy.wait()


def block(v_in, group_moduli, above, below, v, packet, strips, beside, push, moduli, partial, *, gx):
    tiles, _, width = v.shape[2:]
    groups = tiles // TILE
    place = lax.axis_index("gx")
    has_above = place > 0
    has_below = place < gx - 1
    sub = iota((TILE, width), 0)
    low = sub < HALO

    halo, edge = [], []
    for c in range(2):
        under = jnp.where(has_below, below[c], 0.0)
        over = jnp.where(has_above, above[c], 0.0)
        halo.append(jnp.where(low, under, over))
        fill_strips(strips, c, halo[c], v)
        for g in range(groups):
            moduli[c, g] = group_moduli[c, g]
        under = jnp.where(has_below, below[2, c : c + 1, :], 0.0)
        over = jnp.where(has_above, above[2, c : c + 1, :], 0.0)
        edge.append(jnp.where(sub == 0, under, over))
        ends = moduli[c, 0, 0:1, :], moduli[c, groups - 1, TILE - 1 :, :]
        fill_moduli(moduli, c, groups, *ends, edge[c])
    mask = jnp.where(low, 1.0, jnp.where(has_below, 1.0, 0.0))
    right = lambda x: pltpu.roll(x, width - 1, 1)
    left = lambda x: pltpu.roll(x, 1, 1)

    lane = iota((TILE, LANES), 1)
    packet_rows = packet.shape[0]
    for group in range(packet_rows // TILE - 1):
        result = jnp.zeros((TILE, LANES), F32)
        for part in range(4):
            slot = 4 * group + part
            for c in range(2):
                if slot < tiles:
                    pick = lambda s: v[0, c, slot, :, s]
                elif slot == tiles:
                    pick = lambda s: halo[c][:, s]
                elif slot <= tiles + groups:
                    pick = lambda s: moduli[c, slot - tiles - 1, :, s]
                elif slot == tiles + groups + 1:
                    pick = lambda s: edge[c][:, s]
                else:
                    continue
                offset = 32 * part + STRIP * c
                first = pick(slice(0, LANES))
                first = pltpu.roll(first, offset, 1) if offset else first
                final = pltpu.roll(pick(slice(width - LANES, width)), (offset + STRIP) % LANES, 1)
                result = jnp.where((lane >= offset) & (lane < offset + TILE), first, result)
                result = jnp.where((lane >= offset + TILE) & (lane < offset + STRIP), final, result)
        packet[TILE * group : TILE * (group + 1), :] = result

    basis(v, strips, beside, push, moduli, partial, mask, right, left, lambda x: x)

    lane = iota((TILE, width), 1)
    keep = (lane >= HALO) & (lane < width - HALO)
    packet[packet_rows - TILE :, :] = moment_rows(partial, keep)


def interfaces(*refs, gx, gy, sources):
    packets = refs[:gy]
    v, moments, strips, beside, push, moduli, partial = refs[gy:]
    tiles = v.shape[2]
    groups = tiles // TILE
    mine = lax.axis_index("gy")
    has_below = lax.axis_index("gx") < gx - 1
    lines = packets[0].shape[0] // TILE - 1

    def sort(rows):
        arrived = [p[rows, :] for p in packets]
        result = []
        for q in range(gy):
            chosen = arrived[0]
            for k in range(1, gy):
                chosen = jnp.where(sources(mine, k) == q, arrived[k], chosen)
            result.append(chosen)
        return result

    lane = iota((TILE, LANES), 1)
    sub = iota((TILE, LANES), 0)
    halo, edge = [None] * 2, [None] * 2
    for line in range(lines):
        pieces = sort(slice(TILE * line, TILE * (line + 1)))
        for part in range(4):
            slot = 4 * line + part
            for c in range(2):
                result = jnp.zeros((TILE, LANES), F32)
                for q in range(gy):
                    shift = (STRIP * q - 32 * part - STRIP * c) % LANES
                    piece = pltpu.roll(pieces[q], shift, 1) if shift else pieces[q]
                    result = jnp.where((lane >= STRIP * q) & (lane < STRIP * (q + 1)), piece, result)
                if slot < tiles:
                    v[0, c, slot] = result
                elif slot == tiles:
                    halo[c] = result
                elif slot <= tiles + groups:
                    moduli[c, slot - tiles - 1] = result
                elif slot == tiles + groups + 1:
                    edge[c] = result
    for c in range(2):
        fill_strips(strips, c, halo[c], v)
        ends = moduli[c, 0, 0:1, :], moduli[c, groups - 1, TILE - 1 :, :]
        fill_moduli(moduli, c, groups, *ends, edge[c])
    mask = jnp.where(sub < HALO, 1.0, jnp.where(has_below, 1.0, 0.0))
    at_end = lane == STRIP * gy - 1
    at_start = lane == 0
    clear = lambda x: jnp.where(at_end, 0.0, x)
    right = lambda x: clear(pltpu.roll(x, LANES - 1, 1))
    left = lambda x: jnp.where(at_start, 0.0, pltpu.roll(x, 1, 1))

    basis(v, strips, beside, push, moduli, partial, mask, right, left, clear)

    column = lane % STRIP
    keep = ((column < HALO) | (column >= STRIP - HALO)) & (lane < STRIP * gy)
    high = moment_rows(partial, keep)
    rest = jnp.zeros_like(high)
    for piece in sort(slice(TILE * lines, TILE * (lines + 1))):
        high, e = two_sum(high, piece)
        rest = rest + e
    moments[0] = high
    moments[1] = rest


def coefficients(moments):
    shape = moments[0].shape
    take = lambda x, l: jnp.broadcast_to(x[l : l + 1, :], shape)
    s = {l: (take(moments[0], l), take(moments[1], l)) for l in range(2 * ITERS)}
    q = dict(s)
    zero = jnp.zeros(shape, F32)
    residual = [zero + 1.0]
    solution = []
    for k in range(ITERS):
        if k:
            beta = ds_neg(ds_mul(s[k], inverse))
            q = {l: ds_add(s[l], ds_mul(beta, q[l])) for l in range(k, 2 * ITERS - k)}
            direction = [r + beta[0] * p for r, p in zip(residual, direction + [zero])]
        else:
            direction = residual
        push = {l: ds_add(ds_scale(0.05, q[l]), q[l + 1]) for l in range(k, 2 * ITERS - 1 - k)}
        inverse = ds_inverse(push[k])
        alpha = ds_mul(s[k], inverse)
        s = {l: ds_add(s[l], ds_neg(ds_mul(alpha, push[l]))) for l in range(k + 1, 2 * ITERS - 1 - k)}
        solution = [x + alpha[0] * p for x, p in zip(solution + [zero], direction)]
        change = [0.05 * a + b for a, b in zip(direction + [zero], [zero] + direction)]
        residual = [r - alpha[0] * d for r, d in zip(residual + [zero], change)]
    return solution, residual


def combine(*refs, gx):
    gathered = refs[:gx]
    v, strips, *outs, buffer, sems = refs[gx:]
    tiles, _, width = v.shape[2:]
    columns = [slice(start, start + LANES) for start in range(0, width, LANES)]
    total = (gathered[0][0], gathered[0][1])
    for other in gathered[1:]:
        total = ds_add(total, (other[0], other[1]))
    for count, distance in ((8, 16), (16, 1)):
        terms = [total] + [tuple(pltpu.roll(x, distance * i, 1) for x in total) for i in range(1, count)]
        while len(terms) > 1:
            terms = [ds_add(a, b) for a, b in zip(terms[::2], terms[1::2])]
        total = terms[0]
    weights = coefficients(total)
    mine = lax.axis_index("gy")
    lane = iota((TILE, LANES), 1)
    to_left = lax.rem(LANES - STRIP * mine, LANES)
    to_right = lax.rem(2 * LANES - STRIP - STRIP * mine, LANES)
    copies = []
    for c in range(2):
        for i, w in enumerate(weights):

            weigh = lambda x: sum(a * b for a, b in zip(w, x))
            edges = [weigh([strips[k, c, t] for k in range(len(w))]) for t in range(tiles)]
            for t in range(tiles):
                for l, lanes in enumerate(columns):
                    value = weigh([v[k, c, t, :, lanes] for k in range(len(w))])
                    if l == 0:
                        value = jnp.where(lane < HALO, pltpu.roll(edges[t], to_left, 1), value)
                    if l + 1 == len(columns):
                        value = jnp.where(lane >= LANES - HALO, pltpu.roll(edges[t], to_right, 1), value)
                    buffer[i, c, t, :, lanes] = value

            for s in range(TILE):
                at = slice(tiles * s, tiles * (s + 1))
                copy = pltpu.make_async_copy(buffer.at[i, c, :, s, :], outs[i].at[0, c, at, :], sems.at[i, c, s])
                copy.start()
                copies.append(copy)
    for copy in copies:
        copy.wait()


def routes(n):
    if n & (n - 1) == 0:
        return [[(i, i ^ k) for i in range(n)] for k in range(1, n)]
    return [[(i, (i + k) % n) for i in range(n)] for k in range(1, n)]


def source_of(n):
    if n & (n - 1) == 0:
        return lambda mine, k: mine ^ k
    return lambda mine, k: lax.rem(mine - k + n, n)


def on_device(load, material, lame_table):
    gx, gy = lax.axis_size("gx"), lax.axis_size("gy")
    rows, width = load.shape[2:]
    tiles = rows // TILE
    groups = tiles // TILE
    lines = width // LANES
    dims = (ITERS + 1, 2, tiles, TILE)
    tile_rows, tile_cols = material.shape[1:]
    assert rows == TILE * TILE * groups and width % LANES == 0 and STRIP * gy <= LANES
    vmem = pl.BlockSpec(memory_space=pltpu.VMEM)
    hbm = pl.BlockSpec(memory_space=pltpu.HBM)
    shape = lambda *dims: pltpu.VMEM(dims, F32)
    params = pltpu.CompilerParams(vmem_limit_bytes=VMEM_LIMIT)
    pin = lambda x: pltpu.with_memory_space_constraint(x, pltpu.VMEM)
    far = lambda x: pltpu.with_memory_space_constraint(x, pltpu.HBM)
    work = lambda lanes: [
        pltpu.VMEM((2, 2, TILE, lanes), F32),
        pltpu.VMEM((2, tiles + 2, TILE, lanes), F32),
        pltpu.VMEM((2, 2, tiles + 2, TILE, lanes), F32),
        pltpu.VMEM((2, groups + 3, TILE, lanes), F32),
        pltpu.VMEM((2 * ITERS, TILE, lanes), F32),
    ]

    packets = 1 if gx == 2 else 2
    v, moduli, *sent = pl.pallas_call(
        functools.partial(prepare, gx=gx),
        in_specs=[hbm] * 3,
        out_specs=[vmem] * (2 + packets),
        out_shape=[shape(*dims, width), shape(2, groups, TILE, width)] + [shape(3, TILE, width)] * packets,
        scratch_shapes=[
            pltpu.VMEM((tile_rows, tile_cols), jnp.int32),
            pltpu.VMEM((2, lines, tile_rows, LANES), F32),
            pltpu.VMEM((2, 2, TILE, width), F32),
            pltpu.SMEM(lame_table.shape, F32),
            pltpu.SemaphoreType.DMA((3, TILE)),
        ],
        compiler_params=params,
        name="prepare",
    )(far(lame_table), far(load), far(material))

    if gx == 2:
        above = below = lax.ppermute(sent[0], "gx", [(0, 1), (1, 0)])
    else:
        above = lax.ppermute(sent[0], "gx", [(i, i + 1) for i in range(gx - 1)])
        below = lax.ppermute(sent[1], "gx", [(i + 1, i) for i in range(gx - 1)])

    slots = tiles + groups + 2
    packet_rows = TILE * (-(-slots // 4) + 1)
    v, packet = pl.pallas_call(
        functools.partial(block, gx=gx),
        in_specs=[vmem] * 4,
        out_specs=[vmem] * 2,
        out_shape=[shape(*dims, width), shape(packet_rows, LANES)],
        input_output_aliases={0: 0},
        scratch_shapes=work(width),
        compiler_params=params,
        name="block",
    )(pin(v), pin(moduli), pin(above), pin(below))

    arrived = [packet] + [lax.ppermute(packet, "gy", route) for route in routes(gy)]
    strips, moments = pl.pallas_call(
        functools.partial(interfaces, gx=gx, gy=gy, sources=source_of(gy)),
        in_specs=[vmem] * gy,
        out_specs=[vmem] * 2,
        out_shape=[shape(*dims, LANES), shape(2, 2 * ITERS, LANES)],
        scratch_shapes=work(LANES),
        compiler_params=params,
        name="interfaces",
    )(*map(pin, arrived))

    gathered = [moments] + [lax.ppermute(moments, "gx", route) for route in routes(gx)]
    return pl.pallas_call(
        functools.partial(combine, gx=gx),
        in_specs=[vmem] * (gx + 2),
        out_specs=[hbm] * 2,
        out_shape=[jax.ShapeDtypeStruct(load.shape, F32)] * 2,
        scratch_shapes=[pltpu.VMEM((2, *dims[1:], width), F32), pltpu.SemaphoreType.DMA((2, 2, TILE))],
        compiler_params=params,
        name="combine",
    )(*map(pin, gathered), pin(v), pin(strips))


def solution(mesh):
    return jax.shard_map(
        on_device,
        mesh=mesh,
        in_specs=(P("samp", None, "gx", "gy"), P("samp", "gx", "gy"), P()),
        out_specs=(P("samp", None, "gx", "gy"), P("samp", None, "gx", "gy")),
        check_vma=False,
    )
```

```python
import functools

import jax
import jax.numpy as jnp
from jax import lax
from jax.experimental import pallas as pl
from jax.experimental.pallas import tpu as pltpu
from jax.sharding import PartitionSpec as P

TILE = 8
CLASSES = 8
ITERS = 4
HALO = ITERS
LANES = 128
STRIP = 2 * TILE
VMEM_LIMIT = 16 << 20
F32 = jnp.float32


def iota(shape, dim):
    return lax.broadcasted_iota(jnp.int32, shape, dim)


def fast_two_sum(a, b):
    s = a + b
    return s, b - (s - a)


def two_sum(a, b):
    s = a + b
    t = s - a
    return s, (a - (s - t)) + (b - t)


def split(a):
    t = 4097.0 * a
    high = t - (t - a)
    return high, a - high


def two_prod(a, b):
    p = a * b
    ah, al = split(a)
    bh, bl = split(b)
    return p, ((ah * bh - p) + ah * bl + al * bh) + al * bl


def ds_add(x, y):
    s, e = two_sum(x[0], y[0])
    return fast_two_sum(s, e + (x[1] + y[1]))


def ds_mul(x, y):
    p, e = two_prod(x[0], y[0])
    return fast_two_sum(p, e + (x[0] * y[1] + x[1] * y[0]))


def ds_neg(x):
    return -x[0], -x[1]


def ds_scale(c, x):
    p, e = two_prod(jnp.full(x[0].shape, c, F32), x[0])
    return fast_two_sum(p, e + c * x[1])


def ds_inverse(x):
    first = 1.0 / x[0]
    p, e = two_prod(first, x[0])
    rest = ((1.0 - p) - e) - first * x[1]
    return fast_two_sum(first, first * rest)


def stress(here, below, bulk, mu):
    sums, gaps = [], []
    for (x, right), (y, beside) in zip(here, below):
        sums.append((x + right, y + beside))
        gaps.append((right - x, beside - y))
    exx = sums[0][1] - sums[0][0]
    eyy = gaps[1][1] + gaps[1][0]
    gxy = (gaps[0][1] + gaps[0][0]) + (sums[1][1] - sums[1][0])
    mean = bulk * (exx + eyy)
    apart = mu * (exx - eyy)
    return (mean + apart, mean - apart, mu * gxy), (exx, eyy, gxy)


def forces(before, s):
    pxx, pyy, pxy = before
    xx, yy, xy = s
    dxx = pxx - xx
    sxy = pxy + xy
    dxy = pxy - xy
    syy = pyy + yy
    return (dxx + sxy, dxx - sxy), (dxy + syy, dxy - syy)


def total(terms):
    return functools.reduce(lambda a, b: a + b, terms)


def dot(x, y):
    return total([a * b for a, b in zip(x, y)])


def basis(v, strips, beside, push, moduli, partial, mask, right, left, clear):
    tiles = v.shape[2]
    groups = tiles // TILE
    up = lambda x: pltpu.roll(x, TILE - 1, 0)
    down = lambda x: pltpu.roll(x, 1, 0)

    for c in range(2):
        for s in range(2):
            beside[c, tiles + s] = right(strips[s, c])

    def cells(k, final, at):
        modulus = lambda g: (moduli[0, g, :, at], moduli[1, g, :, at])
        tile = lambda c, t: (v[k, c, t, :, at], beside[c, t, :, at])
        ends = [[(strips[s, c, :, at], beside[c, tiles + s, :, at]) for c in range(2)] for s in range(2)]
        sub = iota(ends[0][0][0].shape, 0)
        for s, here in enumerate([] if final else ends):
            t, _ = stress(here, [(up(x), up(y)) for x, y in here], *modulus(groups + 1 + s))
            for c, (x, y) in enumerate(forces(tuple(down(x) for x in t), t)):
                push[0, c, tiles + s, :, at] = x * mask[:, at] if s else x
                push[1, c, tiles + s, :, at] = y * mask[:, at] if s else y
        above, below = [], []
        for c in range(2):
            join = lambda x, y: jnp.where(sub == 0, pltpu.roll(x, 5, 0), down(y))
            above.append(tuple(map(join, ends[0][c], tile(c, tiles - 1))))
            join = lambda x, y: jnp.where(sub == TILE - 1, pltpu.roll(x, 3, 0), up(y))
            below.append(tuple(map(join, ends[1][c], tile(c, 0))))

        own, cross, energy = [], [], []
        grow = lambda sums, x: sums.append(sums.pop() + x if sums else x)
        last = max(k - 1, 0) if final else jnp.maximum(k - 1, 0)
        here = [tile(c, 0) for c in range(2)]
        before, _ = stress(above, here, *modulus(groups))
        for t in range(tiles):
            after = [tile(c, t + 1) for c in range(2)] if t + 1 < tiles else below
            s, strain = stress(here, after, *modulus(t // TILE))
            for c, (x, y) in enumerate(forces(before, s)):
                push[0, c, t, :, at], push[1, c, t, :, at] = x, y
            values = [x for x, _ in here]
            grow(own, dot(values, values))
            grow(cross, dot([v[last, c, t, :, at] for c in range(2)], values))
            if final:
                grow(energy, dot(strain, s))
            before, here = s, after
        partial[2 * last + 1, :, at] = cross[0]
        partial[2 * k, :, at] = own[0]
        if final:
            partial[2 * k + 1, :, at] = energy[0]

    columns = [slice(start, start + LANES) for start in range(0, v.shape[4], LANES)]

    @pl.loop(0, ITERS - 1)
    def _(k):
        for at in columns:
            cells(k, False, at)
        for t in range(tiles + 2):
            for c in range(2):
                x, y = push[0, c, t], push[1, c, t]
                beside[c, t] = clear(x + right(y))
                if t < tiles:
                    v[k + 1, c, t] = left(x) + y
                else:
                    strips[t - tiles, c] = left(x) + y

    for at in columns:
        cells(ITERS - 1, True, at)


def finish(v_in, push, v, *, masked):
    tiles = v.shape[2]
    at_start = iota(v.shape[3:], 1) == 0
    for t in range(tiles):
        for c in range(2):
            x = pltpu.roll(push[0, c, t], 1, 1)
            v[ITERS, c, t] = (jnp.where(at_start, 0.0, x) if masked else x) + push[1, c, t]


def moment_rows(partial, keep):
    row = iota((2 * ITERS, LANES), 0)
    result = jnp.zeros((2 * ITERS, LANES), F32)
    for index in range(2 * ITERS):
        part = jnp.where(keep, partial[index], 0.0)
        folded = part[:, :LANES]
        for start in range(LANES, part.shape[1], LANES):
            folded = folded + part[:, start : start + LANES]
        total = jnp.sum(folded, axis=0, keepdims=True)
        result = jnp.where(row == index, total, result)
    return result


def fill_moduli(moduli, c, groups, first, last, edge):
    sub = iota(edge.shape, 0)
    low = sub < HALO
    above, below = edge[1:2, :], edge[0:1, :]
    moduli[c, groups] = jnp.where(sub == 0, above, pltpu.roll(moduli[c, groups - 1], 1, 0))
    moduli[c, groups + 1] = jnp.where(low, above, first)
    moduli[c, groups + 2] = jnp.where(low, last, below)


def fill_strips(strips, c, halo, v):
    sub = iota(halo.shape, 0)
    low = sub < HALO
    tiles = v.shape[2]
    first = last = halo
    for r in range(HALO):
        first = jnp.where(sub == r, v[0, c, r, 0:1, :], first)
        last = jnp.where(sub == TILE - 1 - r, v[0, c, tiles - 1 - r, TILE - 1 :, :], last)
    strips[0, c] = pltpu.roll(jnp.where(low, first, halo), HALO, 0)
    strips[1, c] = pltpu.roll(jnp.where(low, halo, last), HALO, 0)


def prepare(table, load, material, v, moduli, *rest, gx):
    *packets, kinds_buffer, lines, ends, scalars, sems = rest
    rows, cols = material.shape[1:]
    height, width = load.shape[2:]
    tiles = height // TILE
    groups = tiles // TILE
    columns = [slice(start, start + LANES) for start in range(0, width, LANES)]
    early = [pltpu.make_async_copy(material.at[0], kinds_buffer, sems.at[2, 0])]
    for i, at in enumerate((slice(0, TILE), slice(height - TILE, height))):
        early.append(pltpu.make_async_copy(load.at[0, :, at, :], ends.at[i], sems.at[2, i + 1]))
    early.append(pltpu.make_async_copy(table, scalars, sems.at[2, 3]))
    late = []
    for c in range(2):
        for s in range(TILE):
            at = slice(tiles * s, tiles * (s + 1))
            late.append(pltpu.make_async_copy(load.at[0, c, at, :], v.at[0, c, :, s, :], sems.at[c, s]))
    for copy in early + late:
        copy.start()
    early[0].wait()
    grid = (cols, width)
    expand = iota(grid, 1) // TILE == iota(grid, 0)
    kinds = jnp.dot(
        kinds_buffer[...].astype(F32).astype(jnp.bfloat16),
        expand.astype(F32).astype(jnp.bfloat16),
        preferred_element_type=F32,
    )
    early[3].wait()
    bulk = jnp.zeros((rows, width), F32)
    shear = bulk
    for k in range(CLASSES):
        mu = 0.25 * scalars[1, k]
        here = kinds == float(k)
        bulk = jnp.where(here, 0.25 * scalars[0, k] + mu, bulk)
        shear = jnp.where(here, mu, shear)
    for c, values in enumerate((bulk, shear)):
        for l, lanes in enumerate(columns):
            lines[c, l] = values[:, lanes]
            for g in range(groups):
                moduli[c, g, :, lanes] = lines[c, l, pl.ds(g, TILE, stride=groups), :]
    place = lax.axis_index("gx")
    for copy in early[1:3]:
        copy.wait()

    def fill(packet, down):
        for c in range(2):
            packet[c] = jnp.where(down, ends[1, c], ends[0, c])
            row = jnp.where(down, moduli[c, groups - 1, TILE - 1 :, :], moduli[c, 0, 0:1, :])
            packet[2, c : c + 1, :] = row
        packet[2, 2:, :] = jnp.zeros((TILE - 2, width), F32)

    if gx == 2:
        fill(packets[0], place == 0)
    else:
        fill(packets[0], True)
        fill(packets[1], False)
    for copy in late:
        copy.wait()


def pack(packet, lines, pick, width):
    lane = iota((TILE, LANES), 1)
    for line in lines:
        result = jnp.zeros((TILE, LANES), F32)
        for part in range(4):
            for c in range(2):
                offset = 32 * part + STRIP * c
                first = pick(4 * line + part, c, slice(0, LANES))
                if first is None:
                    continue
                first = pltpu.roll(first, offset, 1) if offset else first
                final = pick(4 * line + part, c, slice(width - LANES, width))
                final = pltpu.roll(final, (offset + STRIP) % LANES, 1)
                result = jnp.where((lane >= offset) & (lane < offset + TILE), first, result)
                result = jnp.where((lane >= offset + TILE) & (lane < offset + STRIP), final, result)
        packet[TILE * line : TILE * (line + 1), :] = result


def early(v, packet, beside):
    tiles, _, width = v.shape[2:]
    pack(packet, range(tiles // 4), lambda slot, c, at: v[0, c, slot, :, at], width)
    for c in range(2):
        for t in range(tiles):
            beside[c, t] = pltpu.roll(v[0, c, t], width - 1, 1)


def block(v_in, packet_in, beside_in, group_moduli, above, below, v, packet, beside, push, strips, moduli, partial, *, gx):
    tiles, _, width = v.shape[2:]
    groups = tiles // TILE
    place = lax.axis_index("gx")
    has_above = place > 0
    has_below = place < gx - 1
    sub = iota((TILE, width), 0)
    low = sub < HALO

    halo, edge = [], []
    for c in range(2):
        under = jnp.where(has_below, below[c], 0.0)
        over = jnp.where(has_above, above[c], 0.0)
        halo.append(jnp.where(low, under, over))
        fill_strips(strips, c, halo[c], v)
        for g in range(groups):
            moduli[c, g] = group_moduli[c, g]
        under = jnp.where(has_below, below[2, c : c + 1, :], 0.0)
        over = jnp.where(has_above, above[2, c : c + 1, :], 0.0)
        edge.append(jnp.where(sub == 0, under, over))
        ends = moduli[c, 0, 0:1, :], moduli[c, groups - 1, TILE - 1 :, :]
        fill_moduli(moduli, c, groups, *ends, edge[c])
    mask = jnp.where(low, 1.0, jnp.where(has_below, 1.0, 0.0))
    right = lambda x: pltpu.roll(x, width - 1, 1)
    left = lambda x: pltpu.roll(x, 1, 1)

    def pick(slot, c, at):
        if slot == tiles:
            return halo[c][:, at]
        if slot <= tiles + groups:
            return moduli[c, slot - tiles - 1, :, at]
        return edge[c][:, at] if slot == tiles + groups + 1 else None

    pack(packet, range(tiles // 4, packet.shape[0] // TILE - 1), pick, width)
    basis(v, strips, beside, push, moduli, partial, mask, right, left, lambda x: x)

    lane = iota((TILE, width), 1)
    keep = (lane >= HALO) & (lane < width - HALO)
    packet[packet.shape[0] - TILE :, :] = moment_rows(partial, keep)


def interfaces(*refs, gx, gy, sources):
    packets = refs[:gy]
    v, moments, push, strips, beside, moduli, partial = refs[gy:]
    tiles = v.shape[2]
    groups = tiles // TILE
    mine = lax.axis_index("gy")
    has_below = lax.axis_index("gx") < gx - 1
    lines = packets[0].shape[0] // TILE - 1

    def sort(rows):
        arrived = [p[rows, :] for p in packets]
        result = []
        for q in range(gy):
            chosen = arrived[0]
            for k in range(1, gy):
                chosen = jnp.where(sources(mine, k) == q, arrived[k], chosen)
            result.append(chosen)
        return result

    lane = iota((TILE, LANES), 1)
    sub = iota((TILE, LANES), 0)
    halo, edge = [None] * 2, [None] * 2
    for line in range(lines):
        pieces = sort(slice(TILE * line, TILE * (line + 1)))
        for part in range(4):
            slot = 4 * line + part
            for c in range(2):
                result = jnp.zeros((TILE, LANES), F32)
                for q in range(gy):
                    shift = (STRIP * q - 32 * part - STRIP * c) % LANES
                    piece = pltpu.roll(pieces[q], shift, 1) if shift else pieces[q]
                    result = jnp.where((lane >= STRIP * q) & (lane < STRIP * (q + 1)), piece, result)
                if slot < tiles:
                    v[0, c, slot] = result
                elif slot == tiles:
                    halo[c] = result
                elif slot <= tiles + groups:
                    moduli[c, slot - tiles - 1] = result
                elif slot == tiles + groups + 1:
                    edge[c] = result
    for c in range(2):
        fill_strips(strips, c, halo[c], v)
        ends = moduli[c, 0, 0:1, :], moduli[c, groups - 1, TILE - 1 :, :]
        fill_moduli(moduli, c, groups, *ends, edge[c])
    mask = jnp.where(sub < HALO, 1.0, jnp.where(has_below, 1.0, 0.0))
    at_end = lane == STRIP * gy - 1
    at_start = lane == 0
    clear = lambda x: jnp.where(at_end, 0.0, x)
    right = lambda x: clear(pltpu.roll(x, LANES - 1, 1))
    left = lambda x: jnp.where(at_start, 0.0, pltpu.roll(x, 1, 1))

    for c in range(2):
        for t in range(tiles):
            beside[c, t] = right(v[0, c, t])
    basis(v, strips, beside, push, moduli, partial, mask, right, left, clear)

    column = lane % STRIP
    keep = ((column < HALO) | (column >= STRIP - HALO)) & (lane < STRIP * gy)
    high = moment_rows(partial, keep)
    rest = jnp.zeros_like(high)
    for piece in sort(slice(TILE * lines, TILE * (lines + 1))):
        high, e = two_sum(high, piece)
        rest = rest + e
    moments[0] = high
    moments[1] = rest


def coefficients(moments):
    shape = moments[0].shape
    take = lambda x, l: jnp.broadcast_to(x[l : l + 1, :], shape)
    s = {l: (take(moments[0], l), take(moments[1], l)) for l in range(2 * ITERS)}
    q = dict(s)
    zero = jnp.zeros(shape, F32)
    residual = [zero + 1.0]
    solution = []
    for k in range(ITERS):
        if k:
            beta = ds_neg(ds_mul(s[k], inverse))
            q = {l: ds_add(s[l], ds_mul(beta, q[l])) for l in range(k, 2 * ITERS - k)}
            direction = [r + beta[0] * p for r, p in zip(residual, direction + [zero])]
        else:
            direction = residual
        push = {l: ds_add(ds_scale(0.05, q[l]), q[l + 1]) for l in range(k, 2 * ITERS - 1 - k)}
        inverse = ds_inverse(push[k])
        alpha = ds_mul(s[k], inverse)
        s = {l: ds_add(s[l], ds_neg(ds_mul(alpha, push[l]))) for l in range(k + 1, 2 * ITERS - 1 - k)}
        solution = [x + alpha[0] * p for x, p in zip(solution + [zero], direction)]
        change = [0.05 * a + b for a, b in zip(direction + [zero], [zero] + direction)]
        residual = [r - alpha[0] * d for r, d in zip(residual + [zero], change)]
    return solution, residual


def combine(*refs, gx):
    gathered = refs[:gx]
    v, strips, *outs, buffer, sems = refs[gx:]
    tiles, _, width = v.shape[2:]
    columns = [slice(start, start + LANES) for start in range(0, width, LANES)]
    moments = (gathered[0][0], gathered[0][1])
    for other in gathered[1:]:
        moments = ds_add(moments, (other[0], other[1]))
    for count, distance in ((8, 16), (16, 1)):
        terms = [moments] + [tuple(pltpu.roll(x, distance * i, 1) for x in moments) for i in range(1, count)]
        while len(terms) > 1:
            terms = [ds_add(a, b) for a, b in zip(terms[::2], terms[1::2])]
        moments = terms[0]
    weights = coefficients(moments)
    mine = lax.axis_index("gy")
    lane = iota((TILE, LANES), 1)
    to_left = lax.rem(LANES - STRIP * mine, LANES)
    to_right = lax.rem(2 * LANES - STRIP - STRIP * mine, LANES)
    copies = []
    for c in range(2):
        for i, w in enumerate(weights):

            weigh = lambda x: dot(w, x)
            edges = [weigh([strips[k, c, t] for k in range(len(w))]) for t in range(tiles)]
            for t in range(tiles):
                for l, lanes in enumerate(columns):
                    value = weigh([v[k, c, t, :, lanes] for k in range(len(w))])
                    if l == 0:
                        value = jnp.where(lane < HALO, pltpu.roll(edges[t], to_left, 1), value)
                    if l + 1 == len(columns):
                        value = jnp.where(lane >= LANES - HALO, pltpu.roll(edges[t], to_right, 1), value)
                    buffer[i, c, t, :, lanes] = value

            for s in range(TILE):
                at = slice(tiles * s, tiles * (s + 1))
                copy = pltpu.make_async_copy(buffer.at[i, c, :, s, :], outs[i].at[0, c, at, :], sems.at[i, c, s])
                copy.start()
                copies.append(copy)
    for copy in copies:
        copy.wait()


def routes(n):
    if n & (n - 1) == 0:
        return [[(i, i ^ k) for i in range(n)] for k in range(1, n)]
    return [[(i, (i + k) % n) for i in range(n)] for k in range(1, n)]


def source_of(n):
    if n & (n - 1) == 0:
        return lambda mine, k: mine ^ k
    return lambda mine, k: lax.rem(mine - k + n, n)


def on_device(load, material, lame_table):
    gx, gy = lax.axis_size("gx"), lax.axis_size("gy")
    rows, width = load.shape[2:]
    tiles = rows // TILE
    groups = tiles // TILE
    lines = width // LANES
    dims = (ITERS + 1, 2, tiles, TILE)
    tile_rows, tile_cols = material.shape[1:]
    assert rows == TILE * TILE * groups and width % LANES == 0 and STRIP * gy <= LANES
    vmem = pl.BlockSpec(memory_space=pltpu.VMEM)
    hbm = pl.BlockSpec(memory_space=pltpu.HBM)
    shape = lambda *dims: pltpu.VMEM(dims, F32)
    params = pltpu.CompilerParams(vmem_limit_bytes=VMEM_LIMIT)
    pin = lambda x: pltpu.with_memory_space_constraint(x, pltpu.VMEM)
    far = lambda x: pltpu.with_memory_space_constraint(x, pltpu.HBM)
    strips_of = lambda lanes: pltpu.VMEM((2, 2, TILE, lanes), F32)
    beside_of = lambda lanes: pltpu.VMEM((2, tiles + 2, TILE, lanes), F32)
    push_of = lambda lanes: pltpu.VMEM((2, 2, tiles + 2, TILE, lanes), F32)
    work = lambda lanes: [
        pltpu.VMEM((2, groups + 3, TILE, lanes), F32),
        pltpu.VMEM((2 * ITERS, TILE, lanes), F32),
    ]

    def finished(v, push, masked):
        return pl.pallas_call(
            functools.partial(finish, masked=masked),
            in_specs=[vmem] * 2,
            out_specs=vmem,
            out_shape=pltpu.VMEM(v.shape, F32),
            input_output_aliases={0: 0},
            compiler_params=params,
            name="finish",
        )(pin(v), pin(push))

    packets = 1 if gx == 2 else 2
    v, moduli, *sent = pl.pallas_call(
        functools.partial(prepare, gx=gx),
        in_specs=[hbm] * 3,
        out_specs=[vmem] * (2 + packets),
        out_shape=[shape(*dims, width), shape(2, groups, TILE, width)] + [shape(3, TILE, width)] * packets,
        scratch_shapes=[
            pltpu.VMEM((tile_rows, tile_cols), jnp.int32),
            pltpu.VMEM((2, lines, tile_rows, LANES), F32),
            pltpu.VMEM((2, 2, TILE, width), F32),
            pltpu.SMEM(lame_table.shape, F32),
            pltpu.SemaphoreType.DMA((3, TILE)),
        ],
        compiler_params=params,
        name="prepare",
    )(far(lame_table), far(load), far(material))

    if gx == 2:
        above = below = lax.ppermute(sent[0], "gx", [(0, 1), (1, 0)])
    else:
        above = lax.ppermute(sent[0], "gx", [(i, i + 1) for i in range(gx - 1)])
        below = lax.ppermute(sent[1], "gx", [(i + 1, i) for i in range(gx - 1)])

    slots = tiles + groups + 2
    packet_rows = TILE * (-(-slots // 4) + 1)
    packet, beside = pl.pallas_call(
        early,
        in_specs=[vmem],
        out_specs=[vmem] * 2,
        out_shape=[shape(packet_rows, LANES), beside_of(width)],
        compiler_params=params,
        name="early",
    )(pin(v))
    v, packet, _, push = pl.pallas_call(
        functools.partial(block, gx=gx),
        in_specs=[vmem] * 6,
        out_specs=[vmem] * 4,
        out_shape=[shape(*dims, width), shape(packet_rows, LANES), beside_of(width), push_of(width)],
        scratch_shapes=[strips_of(width)] + work(width),
        input_output_aliases={0: 0, 1: 1, 2: 2},
        compiler_params=params,
        name="block",
    )(*map(pin, (v, packet, beside, moduli, above, below)))

    arrived = [packet] + [lax.ppermute(packet, "gy", route) for route in routes(gy)]
    v = finished(v, push, False)
    strips, moments, push = pl.pallas_call(
        functools.partial(interfaces, gx=gx, gy=gy, sources=source_of(gy)),
        in_specs=[vmem] * gy,
        out_specs=[vmem] * 3,
        out_shape=[shape(*dims, LANES), shape(2, 2 * ITERS, LANES), push_of(LANES)],
        scratch_shapes=[strips_of(LANES), beside_of(LANES)] + work(LANES),
        compiler_params=params,
        name="interfaces",
    )(*map(pin, arrived))

    gathered = [moments] + [lax.ppermute(moments, "gx", route) for route in routes(gx)]
    strips = finished(strips, push, True)
    return pl.pallas_call(
        functools.partial(combine, gx=gx),
        in_specs=[vmem] * (gx + 2),
        out_specs=[hbm] * 2,
        out_shape=[jax.ShapeDtypeStruct(load.shape, F32)] * 2,
        scratch_shapes=[pltpu.VMEM((2, *dims[1:], width), F32), pltpu.SemaphoreType.DMA((2, 2, TILE))],
        compiler_params=params,
        name="combine",
    )(*map(pin, gathered), pin(v), pin(strips))


def solution(mesh):
    return jax.shard_map(
        on_device,
        mesh=mesh,
        in_specs=(P("samp", None, "gx", "gy"), P("samp", "gx", "gy"), P()),
        out_specs=(P("samp", None, "gx", "gy"), P("samp", None, "gx", "gy")),
        check_vma=False,
    )
```

```python
import functools

import jax
import jax.numpy as jnp
from jax import lax
from jax.experimental import pallas as pl
from jax.experimental.pallas import tpu as pltpu
from jax.sharding import PartitionSpec as P

TILE = 8
CLASSES = 8
ITERS = 4
HALO = ITERS
LANES = 128
STRIP = 2 * TILE
VMEM_LIMIT = 16 << 20
F32 = jnp.float32


def iota(shape, dim):
    return lax.broadcasted_iota(jnp.int32, shape, dim)


def fast_two_sum(a, b):
    s = a + b
    return s, b - (s - a)


def two_sum(a, b):
    s = a + b
    t = s - a
    return s, (a - (s - t)) + (b - t)


def split(a):
    t = 4097.0 * a
    high = t - (t - a)
    return high, a - high


def two_prod(a, b):
    p = a * b
    ah, al = split(a)
    bh, bl = split(b)
    return p, ((ah * bh - p) + ah * bl + al * bh) + al * bl


def ds_add(x, y):
    s, e = two_sum(x[0], y[0])
    return fast_two_sum(s, e + (x[1] + y[1]))


def ds_mul(x, y):
    p, e = two_prod(x[0], y[0])
    return fast_two_sum(p, e + (x[0] * y[1] + x[1] * y[0]))


def ds_neg(x):
    return -x[0], -x[1]


def ds_scale(c, x):
    p, e = two_prod(jnp.full(x[0].shape, c, F32), x[0])
    return fast_two_sum(p, e + c * x[1])


def ds_inverse(x):
    first = 1.0 / x[0]
    p, e = two_prod(first, x[0])
    rest = ((1.0 - p) - e) - first * x[1]
    return fast_two_sum(first, first * rest)


def stress(here, below, bulk, mu):
    sums, gaps = [], []
    for (x, right), (y, beside) in zip(here, below):
        sums.append((x + right, y + beside))
        gaps.append((right - x, beside - y))
    exx = sums[0][1] - sums[0][0]
    eyy = gaps[1][1] + gaps[1][0]
    gxy = (gaps[0][1] + gaps[0][0]) + (sums[1][1] - sums[1][0])
    mean = bulk * (exx + eyy)
    apart = mu * (exx - eyy)
    return (mean + apart, mean - apart, mu * gxy), (exx, eyy, gxy)


def forces(before, s):
    pxx, pyy, pxy = before
    xx, yy, xy = s
    dxx = pxx - xx
    sxy = pxy + xy
    dxy = pxy - xy
    syy = pyy + yy
    return (dxx + sxy, dxx - sxy), (dxy + syy, dxy - syy)


def total(terms):
    return functools.reduce(lambda a, b: a + b, terms)


def dot(x, y):
    return total([a * b for a, b in zip(x, y)])


def basis(v, strips, beside, push, moduli, partial, mask, right, left, clear):
    tiles = v.shape[2]
    groups = tiles // TILE
    up = lambda x: pltpu.roll(x, TILE - 1, 0)
    down = lambda x: pltpu.roll(x, 1, 0)

    for c in range(2):
        for s in range(2):
            beside[c, tiles + s] = right(strips[s, c])

    def cells(k, final, at):
        modulus = lambda g: (moduli[0, g, :, at], moduli[1, g, :, at])
        tile = lambda c, t: (v[k, c, t, :, at], beside[c, t, :, at])
        ends = [[(strips[s, c, :, at], beside[c, tiles + s, :, at]) for c in range(2)] for s in range(2)]
        sub = iota(ends[0][0][0].shape, 0)
        for s, here in enumerate([] if final else ends):
            t, _ = stress(here, [(up(x), up(y)) for x, y in here], *modulus(groups + 1 + s))
            for c, (x, y) in enumerate(forces(tuple(down(x) for x in t), t)):
                push[0, c, tiles + s, :, at] = x * mask[:, at] if s else x
                push[1, c, tiles + s, :, at] = y * mask[:, at] if s else y
        above, below = [], []
        for c in range(2):
            join = lambda x, y: jnp.where(sub == 0, pltpu.roll(x, 5, 0), down(y))
            above.append(tuple(map(join, ends[0][c], tile(c, tiles - 1))))
            join = lambda x, y: jnp.where(sub == TILE - 1, pltpu.roll(x, 3, 0), up(y))
            below.append(tuple(map(join, ends[1][c], tile(c, 0))))

        own, cross, energy = [], [], []
        grow = lambda sums, x: sums.append(sums.pop() + x if sums else x)
        last = max(k - 1, 0) if final else jnp.maximum(k - 1, 0)
        here = [tile(c, 0) for c in range(2)]
        before, _ = stress(above, here, *modulus(groups))
        for t in range(tiles):
            after = [tile(c, t + 1) for c in range(2)] if t + 1 < tiles else below
            s, strain = stress(here, after, *modulus(t // TILE))
            for c, (x, y) in enumerate(forces(before, s)):
                push[0, c, t, :, at], push[1, c, t, :, at] = x, y
            values = [x for x, _ in here]
            grow(own, dot(values, values))
            grow(cross, dot([v[last, c, t, :, at] for c in range(2)], values))
            if final:
                grow(energy, dot(strain, s))
            before, here = s, after
        partial[2 * last + 1, :, at] = cross[0]
        partial[2 * k, :, at] = own[0]
        if final:
            partial[2 * k + 1, :, at] = energy[0]

    columns = [slice(start, start + LANES) for start in range(0, v.shape[4], LANES)]

    @pl.loop(0, ITERS - 1)
    def _(k):
        for at in columns:
            cells(k, False, at)
        for t in range(tiles + 2):
            for c in range(2):
                x, y = push[0, c, t], push[1, c, t]
                beside[c, t] = clear(x + right(y))
                if t < tiles:
                    v[k + 1, c, t] = left(x) + y
                else:
                    strips[t - tiles, c] = left(x) + y

    for at in columns:
        cells(ITERS - 1, True, at)


def finish(v_in, push, v):
    for t in range(v.shape[2]):
        for c in range(2):
            v[ITERS, c, t] = pltpu.roll(push[0, c, t], 1, 1) + push[1, c, t]


def merge(v_in, strips, strips_push, v, ends):
    tiles, _, width = v.shape[2:]
    mine = lax.axis_index("gy")
    to_left = lax.rem(LANES - STRIP * mine, LANES)
    to_right = lax.rem(2 * LANES - STRIP - STRIP * mine, LANES)
    lane = iota((TILE, LANES), 1)

    @pl.loop(0, tiles, unroll=4)
    def _(t):
        for c in range(2):
            x = pltpu.roll(strips_push[0, c, t], 1, 1)
            last = jnp.where(lane == 0, 0.0, x) + strips_push[1, c, t]
            for k in range(ITERS):
                edge = strips[k + 1, c, t] if k + 1 < ITERS else last
                ends[0, k, c, t] = pltpu.roll(edge, to_left, 1)
                ends[1, k, c, t] = pltpu.roll(edge, to_right, 1)

    @pl.loop(0, tiles, unroll=4)
    def _(t):
        for k in range(ITERS):
            for c in range(2):
                for side, start in enumerate((0, width - LANES)):
                    at = slice(start, start + LANES)
                    inside = lane < LANES - HALO if side else lane >= HALO
                    v[k + 1, c, t, :, at] = jnp.where(inside, v[k + 1, c, t, :, at], ends[side, k, c, t])


def moment_rows(partial, keep):
    row = iota((2 * ITERS, LANES), 0)
    result = jnp.zeros((2 * ITERS, LANES), F32)
    for index in range(2 * ITERS):
        part = jnp.where(keep, partial[index], 0.0)
        folded = part[:, :LANES]
        for start in range(LANES, part.shape[1], LANES):
            folded = folded + part[:, start : start + LANES]
        total = jnp.sum(folded, axis=0, keepdims=True)
        result = jnp.where(row == index, total, result)
    return result


def fill_moduli(moduli, c, groups, first, last, edge):
    sub = iota(edge.shape, 0)
    low = sub < HALO
    above, below = edge[1:2, :], edge[0:1, :]
    moduli[c, groups] = jnp.where(sub == 0, above, pltpu.roll(moduli[c, groups - 1], 1, 0))
    moduli[c, groups + 1] = jnp.where(low, above, first)
    moduli[c, groups + 2] = jnp.where(low, last, below)


def fill_strips(strips, c, halo, v):
    sub = iota(halo.shape, 0)
    low = sub < HALO
    tiles = v.shape[2]
    first = last = halo
    for r in range(HALO):
        first = jnp.where(sub == r, v[0, c, r, 0:1, :], first)
        last = jnp.where(sub == TILE - 1 - r, v[0, c, tiles - 1 - r, TILE - 1 :, :], last)
    strips[0, c] = pltpu.roll(jnp.where(low, first, halo), HALO, 0)
    strips[1, c] = pltpu.roll(jnp.where(low, halo, last), HALO, 0)


def prepare(table, load, material, v, moduli, *rest, gx):
    *packets, kinds_buffer, lines, ends, scalars, sems = rest
    rows, cols = material.shape[1:]
    height, width = load.shape[2:]
    tiles = height // TILE
    groups = tiles // TILE
    columns = [slice(start, start + LANES) for start in range(0, width, LANES)]
    early = [pltpu.make_async_copy(material.at[0], kinds_buffer, sems.at[2, 0])]
    for i, at in enumerate((slice(0, TILE), slice(height - TILE, height))):
        early.append(pltpu.make_async_copy(load.at[0, :, at, :], ends.at[i], sems.at[2, i + 1]))
    early.append(pltpu.make_async_copy(table, scalars, sems.at[2, 3]))
    late = []
    for c in range(2):
        for s in range(TILE):
            at = slice(tiles * s, tiles * (s + 1))
            late.append(pltpu.make_async_copy(load.at[0, c, at, :], v.at[0, c, :, s, :], sems.at[c, s]))
    for copy in early + late:
        copy.start()
    early[0].wait()
    grid = (cols, width)
    expand = iota(grid, 1) // TILE == iota(grid, 0)
    kinds = jnp.dot(
        kinds_buffer[...].astype(F32).astype(jnp.bfloat16),
        expand.astype(F32).astype(jnp.bfloat16),
        preferred_element_type=F32,
    )
    early[3].wait()
    bulk = jnp.zeros((rows, width), F32)
    shear = bulk
    for k in range(CLASSES):
        mu = 0.25 * scalars[1, k]
        here = kinds == float(k)
        bulk = jnp.where(here, 0.25 * scalars[0, k] + mu, bulk)
        shear = jnp.where(here, mu, shear)
    for c, values in enumerate((bulk, shear)):
        for l, lanes in enumerate(columns):
            lines[c, l] = values[:, lanes]
            for g in range(groups):
                moduli[c, g, :, lanes] = lines[c, l, pl.ds(g, TILE, stride=groups), :]
    place = lax.axis_index("gx")
    for copy in early[1:3]:
        copy.wait()

    def fill(packet, down):
        for c in range(2):
            packet[c] = jnp.where(down, ends[1, c], ends[0, c])
            row = jnp.where(down, moduli[c, groups - 1, TILE - 1 :, :], moduli[c, 0, 0:1, :])
            packet[2, c : c + 1, :] = row
        packet[2, 2:, :] = jnp.zeros((TILE - 2, width), F32)

    if gx == 2:
        fill(packets[0], place == 0)
    else:
        fill(packets[0], True)
        fill(packets[1], False)
    for copy in late:
        copy.wait()


def pack(packet, lines, pick, width):
    lane = iota((TILE, LANES), 1)
    for line in lines:
        result = jnp.zeros((TILE, LANES), F32)
        for part in range(4):
            for c in range(2):
                offset = 32 * part + STRIP * c
                first = pick(4 * line + part, c, slice(0, LANES))
                if first is None:
                    continue
                first = pltpu.roll(first, offset, 1) if offset else first
                final = pick(4 * line + part, c, slice(width - LANES, width))
                final = pltpu.roll(final, (offset + STRIP) % LANES, 1)
                result = jnp.where((lane >= offset) & (lane < offset + TILE), first, result)
                result = jnp.where((lane >= offset + TILE) & (lane < offset + STRIP), final, result)
        packet[TILE * line : TILE * (line + 1), :] = result


def early(v, packet, beside):
    tiles, _, width = v.shape[2:]
    pack(packet, range(tiles // 4), lambda slot, c, at: v[0, c, slot, :, at], width)
    for c in range(2):
        for t in range(tiles):
            beside[c, t] = pltpu.roll(v[0, c, t], width - 1, 1)


def block(v_in, packet_in, beside_in, group_moduli, above, below, v, packet, beside, push, strips, moduli, partial, *, gx):
    tiles, _, width = v.shape[2:]
    groups = tiles // TILE
    place = lax.axis_index("gx")
    has_above = place > 0
    has_below = place < gx - 1
    sub = iota((TILE, width), 0)
    low = sub < HALO

    halo, edge = [], []
    for c in range(2):
        under = jnp.where(has_below, below[c], 0.0)
        over = jnp.where(has_above, above[c], 0.0)
        halo.append(jnp.where(low, under, over))
        fill_strips(strips, c, halo[c], v)
        for g in range(groups):
            moduli[c, g] = group_moduli[c, g]
        under = jnp.where(has_below, below[2, c : c + 1, :], 0.0)
        over = jnp.where(has_above, above[2, c : c + 1, :], 0.0)
        edge.append(jnp.where(sub == 0, under, over))
        ends = moduli[c, 0, 0:1, :], moduli[c, groups - 1, TILE - 1 :, :]
        fill_moduli(moduli, c, groups, *ends, edge[c])
    mask = jnp.where(low, 1.0, jnp.where(has_below, 1.0, 0.0))
    right = lambda x: pltpu.roll(x, width - 1, 1)
    left = lambda x: pltpu.roll(x, 1, 1)

    def pick(slot, c, at):
        if slot == tiles:
            return halo[c][:, at]
        if slot <= tiles + groups:
            return moduli[c, slot - tiles - 1, :, at]
        return edge[c][:, at] if slot == tiles + groups + 1 else None

    pack(packet, range(tiles // 4, packet.shape[0] // TILE - 1), pick, width)
    basis(v, strips, beside, push, moduli, partial, mask, right, left, lambda x: x)

    lane = iota((TILE, width), 1)
    keep = (lane >= HALO) & (lane < width - HALO)
    packet[packet.shape[0] - TILE :, :] = moment_rows(partial, keep)


def interfaces(*refs, gx, gy, sources):
    packets = refs[:gy]
    _, v, moments, push, _, strips, beside, moduli, partial = refs[gy:]
    tiles = v.shape[2]
    groups = tiles // TILE
    mine = lax.axis_index("gy")
    has_below = lax.axis_index("gx") < gx - 1
    lines = packets[0].shape[0] // TILE - 1

    def sort(rows):
        arrived = [p[rows, :] for p in packets]
        result = []
        for q in range(gy):
            chosen = arrived[0]
            for k in range(1, gy):
                chosen = jnp.where(sources(mine, k) == q, arrived[k], chosen)
            result.append(chosen)
        return result

    lane = iota((TILE, LANES), 1)
    sub = iota((TILE, LANES), 0)
    halo, edge = [None] * 2, [None] * 2
    for line in range(lines):
        pieces = sort(slice(TILE * line, TILE * (line + 1)))
        for part in range(4):
            slot = 4 * line + part
            for c in range(2):
                result = jnp.zeros((TILE, LANES), F32)
                for q in range(gy):
                    shift = (STRIP * q - 32 * part - STRIP * c) % LANES
                    piece = pltpu.roll(pieces[q], shift, 1) if shift else pieces[q]
                    result = jnp.where((lane >= STRIP * q) & (lane < STRIP * (q + 1)), piece, result)
                if slot < tiles:
                    v[0, c, slot] = result
                elif slot == tiles:
                    halo[c] = result
                elif slot <= tiles + groups:
                    moduli[c, slot - tiles - 1] = result
                elif slot == tiles + groups + 1:
                    edge[c] = result
    for c in range(2):
        fill_strips(strips, c, halo[c], v)
        ends = moduli[c, 0, 0:1, :], moduli[c, groups - 1, TILE - 1 :, :]
        fill_moduli(moduli, c, groups, *ends, edge[c])
    mask = jnp.where(sub < HALO, 1.0, jnp.where(has_below, 1.0, 0.0))
    at_end = lane == STRIP * gy - 1
    at_start = lane == 0
    clear = lambda x: jnp.where(at_end, 0.0, x)
    right = lambda x: clear(pltpu.roll(x, LANES - 1, 1))
    left = lambda x: jnp.where(at_start, 0.0, pltpu.roll(x, 1, 1))

    for c in range(2):
        for t in range(tiles):
            beside[c, t] = right(v[0, c, t])
    basis(v, strips, beside, push, moduli, partial, mask, right, left, clear)

    column = lane % STRIP
    keep = ((column < HALO) | (column >= STRIP - HALO)) & (lane < STRIP * gy)
    high = moment_rows(partial, keep)
    rest = jnp.zeros_like(high)
    for piece in sort(slice(TILE * lines, TILE * (lines + 1))):
        high, e = two_sum(high, piece)
        rest = rest + e
    moments[0] = high
    moments[1] = rest


def coefficients(moments):
    shape = moments[0].shape
    take = lambda x, l: jnp.broadcast_to(x[l : l + 1, :], shape)
    s = {l: (take(moments[0], l), take(moments[1], l)) for l in range(2 * ITERS)}
    q = dict(s)
    zero = jnp.zeros(shape, F32)
    residual = [zero + 1.0]
    solution = []
    for k in range(ITERS):
        if k:
            beta = ds_neg(ds_mul(s[k], inverse))
            q = {l: ds_add(s[l], ds_mul(beta, q[l])) for l in range(k, 2 * ITERS - k)}
            direction = [r + beta[0] * p for r, p in zip(residual, direction + [zero])]
        else:
            direction = residual
        push = {l: ds_add(ds_scale(0.05, q[l]), q[l + 1]) for l in range(k, 2 * ITERS - 1 - k)}
        inverse = ds_inverse(push[k])
        alpha = ds_mul(s[k], inverse)
        s = {l: ds_add(s[l], ds_neg(ds_mul(alpha, push[l]))) for l in range(k + 1, 2 * ITERS - 1 - k)}
        solution = [x + alpha[0] * p for x, p in zip(solution + [zero], direction)]
        change = [0.05 * a + b for a, b in zip(direction + [zero], [zero] + direction)]
        residual = [r - alpha[0] * d for r, d in zip(residual + [zero], change)]
    return solution, residual


def combine(*refs, gx):
    gathered = refs[:gx]
    v, *outs, buffer, sems = refs[gx:]
    tiles, _, width = v.shape[2:]
    columns = [slice(start, start + LANES) for start in range(0, width, LANES)]
    moments = (gathered[0][0], gathered[0][1])
    for other in gathered[1:]:
        moments = ds_add(moments, (other[0], other[1]))
    for count, distance in ((8, 16), (16, 1)):
        terms = [moments] + [tuple(pltpu.roll(x, distance * i, 1) for x in moments) for i in range(1, count)]
        while len(terms) > 1:
            terms = [ds_add(a, b) for a, b in zip(terms[::2], terms[1::2])]
        moments = terms[0]
    weights = coefficients(moments)
    copies = []
    for i, w in enumerate(weights):
        for c in range(2):
            for t in range(tiles):
                for lanes in columns:
                    buffer[i, c, t, :, lanes] = dot(w, [v[k, c, t, :, lanes] for k in range(len(w))])
        for s in range(TILE):
            at = slice(tiles * s, tiles * (s + 1))
            copy = pltpu.make_async_copy(buffer.at[i, :, :, s, :], outs[i].at[0, :, at, :], sems.at[i, 0, s])
            copy.start()
            copies.append(copy)
    for copy in copies:
        copy.wait()


def routes(n):
    if n & (n - 1) == 0:
        return [[(i, i ^ k) for i in range(n)] for k in range(1, n)]
    return [[(i, (i + k) % n) for i in range(n)] for k in range(1, n)]


def source_of(n):
    if n & (n - 1) == 0:
        return lambda mine, k: mine ^ k
    return lambda mine, k: lax.rem(mine - k + n, n)


def on_device(load, material, lame_table):
    gx, gy = lax.axis_size("gx"), lax.axis_size("gy")
    rows, width = load.shape[2:]
    tiles = rows // TILE
    groups = tiles // TILE
    lines = width // LANES
    dims = (ITERS + 1, 2, tiles, TILE)
    tile_rows, tile_cols = material.shape[1:]
    assert rows == TILE * TILE * groups and width % LANES == 0 and STRIP * gy <= LANES
    vmem = pl.BlockSpec(memory_space=pltpu.VMEM)
    hbm = pl.BlockSpec(memory_space=pltpu.HBM)
    shape = lambda *dims: pltpu.VMEM(dims, F32)
    params = pltpu.CompilerParams(vmem_limit_bytes=VMEM_LIMIT)
    pin = lambda x: pltpu.with_memory_space_constraint(x, pltpu.VMEM)
    far = lambda x: pltpu.with_memory_space_constraint(x, pltpu.HBM)
    strips_of = lambda lanes: pltpu.VMEM((2, 2, TILE, lanes), F32)
    beside_of = lambda lanes: pltpu.VMEM((2, tiles + 2, TILE, lanes), F32)
    push_of = lambda lanes: pltpu.VMEM((2, 2, tiles + 2, TILE, lanes), F32)
    work = lambda lanes: [
        pltpu.VMEM((2, groups + 3, TILE, lanes), F32),
        pltpu.VMEM((2 * ITERS, TILE, lanes), F32),
    ]

    packets = 1 if gx == 2 else 2
    v, moduli, *sent = pl.pallas_call(
        functools.partial(prepare, gx=gx),
        in_specs=[hbm] * 3,
        out_specs=[vmem] * (2 + packets),
        out_shape=[shape(*dims, width), shape(2, groups, TILE, width)] + [shape(3, TILE, width)] * packets,
        scratch_shapes=[
            pltpu.VMEM((tile_rows, tile_cols), jnp.int32),
            pltpu.VMEM((2, lines, tile_rows, LANES), F32),
            pltpu.VMEM((2, 2, TILE, width), F32),
            pltpu.SMEM(lame_table.shape, F32),
            pltpu.SemaphoreType.DMA((3, TILE)),
        ],
        compiler_params=params,
        name="prepare",
    )(far(lame_table), far(load), far(material))

    if gx == 2:
        above = below = lax.ppermute(sent[0], "gx", [(0, 1), (1, 0)])
    else:
        above = lax.ppermute(sent[0], "gx", [(i, i + 1) for i in range(gx - 1)])
        below = lax.ppermute(sent[1], "gx", [(i + 1, i) for i in range(gx - 1)])

    slots = tiles + groups + 2
    packet_rows = TILE * (-(-slots // 4) + 1)
    packet, beside = pl.pallas_call(
        early,
        in_specs=[vmem],
        out_specs=[vmem] * 2,
        out_shape=[shape(packet_rows, LANES), beside_of(width)],
        compiler_params=params,
        name="early",
    )(pin(v))
    v, packet, _, push = pl.pallas_call(
        functools.partial(block, gx=gx),
        in_specs=[vmem] * 6,
        out_specs=[vmem] * 4,
        out_shape=[shape(*dims, width), shape(packet_rows, LANES), beside_of(width), push_of(width)],
        scratch_shapes=[strips_of(width)] + work(width),
        input_output_aliases={0: 0, 1: 1, 2: 2},
        compiler_params=params,
        name="block",
    )(*map(pin, (v, packet, beside, moduli, above, below)))

    arrived = [packet] + [lax.ppermute(packet, "gy", route) for route in routes(gy)]
    v = pl.pallas_call(
        finish,
        in_specs=[vmem] * 2,
        out_specs=vmem,
        out_shape=pltpu.VMEM(v.shape, F32),
        input_output_aliases={0: 0},
        compiler_params=params,
        name="finish",
    )(pin(v), pin(push))
    strips, moments, strips_push, v = pl.pallas_call(
        functools.partial(interfaces, gx=gx, gy=gy, sources=source_of(gy)),
        in_specs=[vmem] * (gy + 1),
        out_specs=[vmem] * 4,
        out_shape=[shape(*dims, LANES), shape(2, 2 * ITERS, LANES), push_of(LANES), shape(*dims, width)],
        input_output_aliases={gy: 3},
        scratch_shapes=[strips_of(LANES), beside_of(LANES)] + work(LANES),
        compiler_params=params,
        name="interfaces",
    )(*map(pin, arrived), pin(v))

    gathered = [moments] + [lax.ppermute(moments, "gx", route) for route in routes(gx)]
    v = pl.pallas_call(
        merge,
        in_specs=[vmem] * 3,
        out_specs=vmem,
        out_shape=pltpu.VMEM(v.shape, F32),
        scratch_shapes=[pltpu.VMEM((2, ITERS, 2, tiles, TILE, LANES), F32)],
        input_output_aliases={0: 0},
        compiler_params=params,
        name="merge",
    )(*map(pin, (v, strips, strips_push)))
    return pl.pallas_call(
        functools.partial(combine, gx=gx),
        in_specs=[vmem] * (gx + 1),
        out_specs=[hbm] * 2,
        out_shape=[jax.ShapeDtypeStruct(load.shape, F32)] * 2,
        scratch_shapes=[pltpu.VMEM((2, *dims[1:], width), F32), pltpu.SemaphoreType.DMA((2, 2, TILE))],
        compiler_params=params,
        name="combine",
    )(*map(pin, gathered), pin(v))


def solution(mesh):
    return jax.shard_map(
        on_device,
        mesh=mesh,
        in_specs=(P("samp", None, "gx", "gy"), P("samp", "gx", "gy"), P()),
        out_specs=(P("samp", None, "gx", "gy"), P("samp", None, "gx", "gy")),
        check_vma=False,
    )
```

```python
import functools

import jax
import jax.numpy as jnp
from jax import lax
from jax.experimental import pallas as pl
from jax.experimental.pallas import tpu as pltpu
from jax.sharding import PartitionSpec as P

TILE = 8
CLASSES = 8
ITERS = 4
HALO = ITERS
LANES = 128
STRIP = 2 * TILE
VMEM_LIMIT = 16 << 20
F32 = jnp.float32


def iota(shape, dim):
    return lax.broadcasted_iota(jnp.int32, shape, dim)


def fast_two_sum(a, b):
    s = a + b
    return s, b - (s - a)


def two_sum(a, b):
    s = a + b
    t = s - a
    return s, (a - (s - t)) + (b - t)


def split(a):
    t = 4097.0 * a
    high = t - (t - a)
    return high, a - high


def two_prod(a, b):
    p = a * b
    ah, al = split(a)
    bh, bl = split(b)
    return p, ((ah * bh - p) + ah * bl + al * bh) + al * bl


def ds_add(x, y):
    s, e = two_sum(x[0], y[0])
    return fast_two_sum(s, e + (x[1] + y[1]))


def ds_mul(x, y):
    p, e = two_prod(x[0], y[0])
    return fast_two_sum(p, e + (x[0] * y[1] + x[1] * y[0]))


def ds_neg(x):
    return -x[0], -x[1]


def ds_scale(c, x):
    p, e = two_prod(jnp.full(x[0].shape, c, F32), x[0])
    return fast_two_sum(p, e + c * x[1])


def ds_inverse(x):
    first = 1.0 / x[0]
    p, e = two_prod(first, x[0])
    rest = ((1.0 - p) - e) - first * x[1]
    return fast_two_sum(first, first * rest)


def stress(here, below, bulk, mu):
    sums, gaps = [], []
    for (x, right), (y, beside) in zip(here, below):
        sums.append((x + right, y + beside))
        gaps.append((right - x, beside - y))
    exx = sums[0][1] - sums[0][0]
    eyy = gaps[1][1] + gaps[1][0]
    gxy = (gaps[0][1] + gaps[0][0]) + (sums[1][1] - sums[1][0])
    mean = bulk * (exx + eyy)
    apart = mu * (exx - eyy)
    return (mean + apart, mean - apart, mu * gxy), (exx, eyy, gxy)


def forces(before, s):
    pxx, pyy, pxy = before
    xx, yy, xy = s
    dxx = pxx - xx
    sxy = pxy + xy
    dxy = pxy - xy
    syy = pyy + yy
    return (dxx + sxy, dxx - sxy), (dxy + syy, dxy - syy)


def total(terms):
    return functools.reduce(lambda a, b: a + b, terms)


def dot(x, y):
    return total([a * b for a, b in zip(x, y)])


def up(x):
    return pltpu.roll(x, TILE - 1, 0)


def down(x):
    return pltpu.roll(x, 1, 0)


def lane_tiles(width):
    return [slice(start, start + LANES) for start in range(0, width, LANES)]


def inner_cells(k, v, beside, push, moduli, partial, at, above=None, below=None):
    tiles = v.shape[2]
    groups = tiles // TILE
    tile = lambda c, t: (v[k, c, t, :, at], beside[c, t, :, at])
    modulus = lambda g: (moduli[0, g, :, at], moduli[1, g, :, at])
    here = [tile(c, 0) for c in range(2)]
    before = stress(above, here, *modulus(groups))[0] if above else None
    own = energy = None
    for t in range(tiles):
        values = [x for x, _ in here]
        square = dot(values, values)
        own = square if own is None else own + square
        after = [tile(c, t + 1) for c in range(2)] if t + 1 < tiles else below
        if after:
            s, strain = stress(here, after, *modulus(t // TILE))
            work = dot(strain, s)
            energy = work if energy is None else energy + work
            if before:
                for c, (x, y) in enumerate(forces(before, s)):
                    push[0, c, t, :, at], push[1, c, t, :, at] = x, y
            before, here = s, after
    partial[2 * k, :, at] = own
    partial[2 * k + 1, :, at] = energy


def outer_tiles(k, v, strips, beside, at):
    tiles = v.shape[2]
    sub = iota((TILE, LANES), 0)
    above, below = [], []
    for c in range(2):
        first = v[k, c, 0, :, at], beside[c, 0, :, at]
        last = v[k, c, tiles - 1, :, at], beside[c, tiles - 1, :, at]
        top, bottom = ((strips[s, c, :, at], beside[c, tiles + s, :, at]) for s in range(2))
        above.append(tuple(jnp.where(sub == 0, pltpu.roll(x, 5, 0), down(y)) for x, y in zip(top, last)))
        below.append(tuple(jnp.where(sub == TILE - 1, pltpu.roll(x, 3, 0), up(y)) for x, y in zip(bottom, first)))
    return above, below


def strip_cells(strips, beside, push, moduli, mask, at):
    tiles = push.shape[2] - 2
    groups = tiles // TILE
    for s in range(2):
        here = [(strips[s, c, :, at], beside[c, tiles + s, :, at]) for c in range(2)]
        modulus = [moduli[c, groups + 1 + s, :, at] for c in range(2)]
        t, _ = stress(here, [(up(x), up(y)) for x, y in here], *modulus)
        for c, (x, y) in enumerate(forces(tuple(down(x) for x in t), t)):
            push[0, c, tiles + s, :, at] = x * mask[:, at] if s else x
            push[1, c, tiles + s, :, at] = y * mask[:, at] if s else y


def strip_neighbours(strips, beside, right):
    tiles = beside.shape[1] - 2
    for c in range(2):
        for s in range(2):
            beside[c, tiles + s] = right(strips[s, c])


def advance(k, v, strips, beside, push, right, left, clear):
    tiles = v.shape[2]
    for t in range(tiles + 2):
        for c in range(2):
            x, y = push[0, c, t], push[1, c, t]
            beside[c, t] = clear(x + right(y))
            if t < tiles:
                v[k + 1, c, t] = left(x) + y
            else:
                strips[t - tiles, c] = left(x) + y


def basis_pass(k, v, strips, beside, push, moduli, partial, mask):
    for at in lane_tiles(v.shape[4]):
        above, below = outer_tiles(k, v, strips, beside, at)
        inner_cells(k, v, beside, push, moduli, partial, at, above, below)
    for at in lane_tiles(v.shape[4]) if k + 1 < ITERS else []:
        strip_cells(strips, beside, push, moduli, mask, at)


def finish(v_in, push, v):
    for t in range(v.shape[2]):
        for c in range(2):
            v[ITERS, c, t] = pltpu.roll(push[0, c, t], 1, 1) + push[1, c, t]


def merge(v_in, strips, strips_push, v, ends):
    tiles, _, width = v.shape[2:]
    mine = lax.axis_index("gy")
    to_left = lax.rem(LANES - STRIP * mine, LANES)
    to_right = lax.rem(2 * LANES - STRIP - STRIP * mine, LANES)
    lane = iota((TILE, LANES), 1)

    @pl.loop(0, tiles, unroll=4)
    def _(t):
        for c in range(2):
            x = pltpu.roll(strips_push[0, c, t], 1, 1)
            last = jnp.where(lane == 0, 0.0, x) + strips_push[1, c, t]
            for k in range(ITERS):
                edge = strips[k + 1, c, t] if k + 1 < ITERS else last
                ends[0, k, c, t] = pltpu.roll(edge, to_left, 1)
                ends[1, k, c, t] = pltpu.roll(edge, to_right, 1)

    @pl.loop(0, tiles, unroll=4)
    def _(t):
        for k in range(ITERS):
            for c in range(2):
                for side, start in enumerate((0, width - LANES)):
                    at = slice(start, start + LANES)
                    inside = lane < LANES - HALO if side else lane >= HALO
                    v[k + 1, c, t, :, at] = jnp.where(inside, v[k + 1, c, t, :, at], ends[side, k, c, t])


def moment_rows(partial, keep):
    row = iota((2 * ITERS, LANES), 0)
    result = jnp.zeros((2 * ITERS, LANES), F32)
    for index in range(2 * ITERS):
        part = jnp.where(keep, partial[index], 0.0)
        folded = part[:, :LANES]
        for start in range(LANES, part.shape[1], LANES):
            folded = folded + part[:, start : start + LANES]
        total = jnp.sum(folded, axis=0, keepdims=True)
        result = jnp.where(row == index, total, result)
    return result


def fill_moduli(moduli, c, groups, first, last, edge):
    sub = iota(edge.shape, 0)
    low = sub < HALO
    above, below = edge[1:2, :], edge[0:1, :]
    moduli[c, groups] = jnp.where(sub == 0, above, pltpu.roll(moduli[c, groups - 1], 1, 0))
    moduli[c, groups + 1] = jnp.where(low, above, first)
    moduli[c, groups + 2] = jnp.where(low, last, below)


def fill_strips(strips, c, halo, v):
    sub = iota(halo.shape, 0)
    low = sub < HALO
    tiles = v.shape[2]
    first = last = halo
    for r in range(HALO):
        first = jnp.where(sub == r, v[0, c, r, 0:1, :], first)
        last = jnp.where(sub == TILE - 1 - r, v[0, c, tiles - 1 - r, TILE - 1 :, :], last)
    strips[0, c] = pltpu.roll(jnp.where(low, first, halo), HALO, 0)
    strips[1, c] = pltpu.roll(jnp.where(low, halo, last), HALO, 0)


def prepare(table, load, material, v, moduli, *rest, gx):
    *packets, kinds_buffer, lines, ends, scalars, sems = rest
    rows, cols = material.shape[1:]
    height, width = load.shape[2:]
    tiles = height // TILE
    groups = tiles // TILE
    columns = [slice(start, start + LANES) for start in range(0, width, LANES)]
    early = [pltpu.make_async_copy(material.at[0], kinds_buffer, sems.at[2, 0])]
    for i, at in enumerate((slice(0, TILE), slice(height - TILE, height))):
        early.append(pltpu.make_async_copy(load.at[0, :, at, :], ends.at[i], sems.at[2, i + 1]))
    early.append(pltpu.make_async_copy(table, scalars, sems.at[2, 3]))
    late = []
    for c in range(2):
        for s in range(TILE):
            at = slice(tiles * s, tiles * (s + 1))
            late.append(pltpu.make_async_copy(load.at[0, c, at, :], v.at[0, c, :, s, :], sems.at[c, s]))
    for copy in early + late:
        copy.start()
    early[0].wait()
    grid = (cols, width)
    expand = iota(grid, 1) // TILE == iota(grid, 0)
    kinds = jnp.dot(
        kinds_buffer[...].astype(F32).astype(jnp.bfloat16),
        expand.astype(F32).astype(jnp.bfloat16),
        preferred_element_type=F32,
    )
    early[3].wait()
    bulk = jnp.zeros((rows, width), F32)
    shear = bulk
    for k in range(CLASSES):
        mu = 0.25 * scalars[1, k]
        here = kinds == float(k)
        bulk = jnp.where(here, 0.25 * scalars[0, k] + mu, bulk)
        shear = jnp.where(here, mu, shear)
    for c, values in enumerate((bulk, shear)):
        for l, lanes in enumerate(columns):
            lines[c, l] = values[:, lanes]
            for g in range(groups):
                moduli[c, g, :, lanes] = lines[c, l, pl.ds(g, TILE, stride=groups), :]
    place = lax.axis_index("gx")
    for copy in early[1:3]:
        copy.wait()

    def fill(packet, down):
        for c in range(2):
            packet[c] = jnp.where(down, ends[1, c], ends[0, c])
            row = jnp.where(down, moduli[c, groups - 1, TILE - 1 :, :], moduli[c, 0, 0:1, :])
            packet[2, c : c + 1, :] = row
        packet[2, 2:, :] = jnp.zeros((TILE - 2, width), F32)

    if gx == 2:
        fill(packets[0], place == 0)
    else:
        fill(packets[0], True)
        fill(packets[1], False)
    for copy in late:
        copy.wait()


def pack(packet, lines, pick, width):
    lane = iota((TILE, LANES), 1)
    for line in lines:
        result = jnp.zeros((TILE, LANES), F32)
        for part in range(4):
            for c in range(2):
                offset = 32 * part + STRIP * c
                first = pick(4 * line + part, c, slice(0, LANES))
                if first is None:
                    continue
                first = pltpu.roll(first, offset, 1) if offset else first
                final = pick(4 * line + part, c, slice(width - LANES, width))
                final = pltpu.roll(final, (offset + STRIP) % LANES, 1)
                result = jnp.where((lane >= offset) & (lane < offset + TILE), first, result)
                result = jnp.where((lane >= offset + TILE) & (lane < offset + STRIP), final, result)
        packet[TILE * line : TILE * (line + 1), :] = result


def early(v, moduli, packet, beside, push, partial):
    tiles, _, width = v.shape[2:]
    for c in range(2):
        for t in range(tiles):
            beside[c, t] = pltpu.roll(v[0, c, t], width - 1, 1)
    pack(packet, range(tiles // 4), lambda slot, c, at: v[0, c, slot, :, at], width)
    for at in lane_tiles(width):
        inner_cells(0, v, beside, push, moduli, partial, at)


def block(*refs, gx):
    group_moduli, above, below, v, packet, beside, push, partial, strips, moduli = refs[5:]
    tiles, _, width = v.shape[2:]
    groups = tiles // TILE
    place = lax.axis_index("gx")
    has_above = place > 0
    has_below = place < gx - 1
    sub = iota((TILE, width), 0)
    low = sub < HALO

    halo, edge = [], []
    for c in range(2):
        under = jnp.where(has_below, below[c], 0.0)
        over = jnp.where(has_above, above[c], 0.0)
        halo.append(jnp.where(low, under, over))
        fill_strips(strips, c, halo[c], v)
        for g in range(groups):
            moduli[c, g] = group_moduli[c, g]
        under = jnp.where(has_below, below[2, c : c + 1, :], 0.0)
        over = jnp.where(has_above, above[2, c : c + 1, :], 0.0)
        edge.append(jnp.where(sub == 0, under, over))
        ends = moduli[c, 0, 0:1, :], moduli[c, groups - 1, TILE - 1 :, :]
        fill_moduli(moduli, c, groups, *ends, edge[c])
    mask = jnp.where(low, 1.0, jnp.where(has_below, 1.0, 0.0))
    right = lambda x: pltpu.roll(x, width - 1, 1)
    left = lambda x: pltpu.roll(x, 1, 1)

    def pick(slot, c, at):
        if slot == tiles:
            return halo[c][:, at]
        if slot <= tiles + groups:
            return moduli[c, slot - tiles - 1, :, at]
        return edge[c][:, at] if slot == tiles + groups + 1 else None

    pack(packet, range(tiles // 4, packet.shape[0] // TILE - 1), pick, width)
    strip_neighbours(strips, beside, right)
    for at in lane_tiles(width):
        strip_cells(strips, beside, push, moduli, mask, at)
        over, under = outer_tiles(0, v, strips, beside, at)
        tile = lambda t: [(v[0, c, t, :, at], beside[c, t, :, at]) for c in range(2)]
        modulus = lambda g: (moduli[0, g, :, at], moduli[1, g, :, at])
        last = groups - 1
        first_cells = stress(over, tile(0), *modulus(groups))[0], stress(tile(0), tile(1), *modulus(0))[0]
        final, strain = stress(tile(tiles - 1), under, *modulus(last))
        final_cells = stress(tile(tiles - 2), tile(tiles - 1), *modulus(last))[0], final
        for t, pair in ((0, first_cells), (tiles - 1, final_cells)):
            for c, (x, y) in enumerate(forces(*pair)):
                push[0, c, t, :, at], push[1, c, t, :, at] = x, y
        partial[1, :, at] = partial[1, :, at] + dot(strain, final)

    for k in range(ITERS - 1):
        advance(k, v, strips, beside, push, right, left, lambda x: x)
        basis_pass(k + 1, v, strips, beside, push, moduli, partial, mask)


    lane = iota((TILE, width), 1)
    keep = (lane >= HALO) & (lane < width - HALO)
    packet[packet.shape[0] - TILE :, :] = moment_rows(partial, keep)


def interfaces(*refs, gx, gy, sources):
    packets = refs[:gy]
    _, v, moments, push, _, strips, beside, moduli, partial = refs[gy:]
    tiles = v.shape[2]
    groups = tiles // TILE
    mine = lax.axis_index("gy")
    has_below = lax.axis_index("gx") < gx - 1
    lines = packets[0].shape[0] // TILE - 1

    def sort(rows):
        arrived = [p[rows, :] for p in packets]
        result = []
        for q in range(gy):
            chosen = arrived[0]
            for k in range(1, gy):
                chosen = jnp.where(sources(mine, k) == q, arrived[k], chosen)
            result.append(chosen)
        return result

    lane = iota((TILE, LANES), 1)
    sub = iota((TILE, LANES), 0)
    halo, edge = [None] * 2, [None] * 2
    for line in range(lines):
        pieces = sort(slice(TILE * line, TILE * (line + 1)))
        for part in range(4):
            slot = 4 * line + part
            for c in range(2):
                result = jnp.zeros((TILE, LANES), F32)
                for q in range(gy):
                    shift = (STRIP * q - 32 * part - STRIP * c) % LANES
                    piece = pltpu.roll(pieces[q], shift, 1) if shift else pieces[q]
                    result = jnp.where((lane >= STRIP * q) & (lane < STRIP * (q + 1)), piece, result)
                if slot < tiles:
                    v[0, c, slot] = result
                elif slot == tiles:
                    halo[c] = result
                elif slot <= tiles + groups:
                    moduli[c, slot - tiles - 1] = result
                elif slot == tiles + groups + 1:
                    edge[c] = result
    for c in range(2):
        fill_strips(strips, c, halo[c], v)
        ends = moduli[c, 0, 0:1, :], moduli[c, groups - 1, TILE - 1 :, :]
        fill_moduli(moduli, c, groups, *ends, edge[c])
    mask = jnp.where(sub < HALO, 1.0, jnp.where(has_below, 1.0, 0.0))
    at_end = lane == STRIP * gy - 1
    at_start = lane == 0
    clear = lambda x: jnp.where(at_end, 0.0, x)
    right = lambda x: clear(pltpu.roll(x, LANES - 1, 1))
    left = lambda x: jnp.where(at_start, 0.0, pltpu.roll(x, 1, 1))

    for c in range(2):
        for t in range(tiles):
            beside[c, t] = right(v[0, c, t])
    strip_neighbours(strips, beside, right)

    for k in range(ITERS - 1):
        basis_pass(k, v, strips, beside, push, moduli, partial, mask)
        advance(k, v, strips, beside, push, right, left, clear)
    basis_pass(ITERS - 1, v, strips, beside, push, moduli, partial, mask)

    column = lane % STRIP
    keep = ((column < HALO) | (column >= STRIP - HALO)) & (lane < STRIP * gy)
    high = moment_rows(partial, keep)
    rest = jnp.zeros_like(high)
    for piece in sort(slice(TILE * lines, TILE * (lines + 1))):
        high, e = two_sum(high, piece)
        rest = rest + e
    moments[0] = high
    moments[1] = rest


def coefficients(moments):
    shape = moments[0].shape
    take = lambda x, l: jnp.broadcast_to(x[l : l + 1, :], shape)
    s = {l: (take(moments[0], l), take(moments[1], l)) for l in range(2 * ITERS)}
    q = dict(s)
    zero = jnp.zeros(shape, F32)
    residual = [zero + 1.0]
    solution = []
    for k in range(ITERS):
        if k:
            beta = ds_neg(ds_mul(s[k], inverse))
            q = {l: ds_add(s[l], ds_mul(beta, q[l])) for l in range(k, 2 * ITERS - k)}
            direction = [r + beta[0] * p for r, p in zip(residual, direction + [zero])]
        else:
            direction = residual
        push = {l: ds_add(ds_scale(0.05, q[l]), q[l + 1]) for l in range(k, 2 * ITERS - 1 - k)}
        inverse = ds_inverse(push[k])
        alpha = ds_mul(s[k], inverse)
        s = {l: ds_add(s[l], ds_neg(ds_mul(alpha, push[l]))) for l in range(k + 1, 2 * ITERS - 1 - k)}
        solution = [x + alpha[0] * p for x, p in zip(solution + [zero], direction)]
        change = [0.05 * a + b for a, b in zip(direction + [zero], [zero] + direction)]
        residual = [r - alpha[0] * d for r, d in zip(residual + [zero], change)]
    return solution, residual


def combine(*refs, gx):
    gathered = refs[:gx]
    v, *outs, buffer, sems = refs[gx:]
    tiles, _, width = v.shape[2:]
    columns = [slice(start, start + LANES) for start in range(0, width, LANES)]
    moments = (gathered[0][0], gathered[0][1])
    for other in gathered[1:]:
        moments = ds_add(moments, (other[0], other[1]))
    for count, distance in ((8, 16), (16, 1)):
        terms = [moments] + [tuple(pltpu.roll(x, distance * i, 1) for x in moments) for i in range(1, count)]
        while len(terms) > 1:
            terms = [ds_add(a, b) for a, b in zip(terms[::2], terms[1::2])]
        moments = terms[0]
    weights = coefficients(moments)
    copies = []
    for i, w in enumerate(weights):
        for c in range(2):
            for t in range(tiles):
                for lanes in columns:
                    buffer[i, c, t, :, lanes] = dot(w, [v[k, c, t, :, lanes] for k in range(len(w))])
        for s in range(TILE):
            at = slice(tiles * s, tiles * (s + 1))
            copy = pltpu.make_async_copy(buffer.at[i, :, :, s, :], outs[i].at[0, :, at, :], sems.at[i, 0, s])
            copy.start()
            copies.append(copy)
    for copy in copies:
        copy.wait()


def routes(n):
    if n & (n - 1) == 0:
        return [[(i, i ^ k) for i in range(n)] for k in range(1, n)]
    return [[(i, (i + k) % n) for i in range(n)] for k in range(1, n)]


def source_of(n):
    if n & (n - 1) == 0:
        return lambda mine, k: mine ^ k
    return lambda mine, k: lax.rem(mine - k + n, n)


def on_device(load, material, lame_table):
    gx, gy = lax.axis_size("gx"), lax.axis_size("gy")
    rows, width = load.shape[2:]
    tiles = rows // TILE
    groups = tiles // TILE
    lines = width // LANES
    dims = (ITERS + 1, 2, tiles, TILE)
    tile_rows, tile_cols = material.shape[1:]
    assert rows == TILE * TILE * groups and width % LANES == 0 and STRIP * gy <= LANES
    vmem = pl.BlockSpec(memory_space=pltpu.VMEM)
    hbm = pl.BlockSpec(memory_space=pltpu.HBM)
    shape = lambda *dims: pltpu.VMEM(dims, F32)
    params = pltpu.CompilerParams(vmem_limit_bytes=VMEM_LIMIT)
    pin = lambda x: pltpu.with_memory_space_constraint(x, pltpu.VMEM)
    far = lambda x: pltpu.with_memory_space_constraint(x, pltpu.HBM)
    strips_of = lambda lanes: pltpu.VMEM((2, 2, TILE, lanes), F32)
    beside_of = lambda lanes: pltpu.VMEM((2, tiles + 2, TILE, lanes), F32)
    push_of = lambda lanes: pltpu.VMEM((2, 2, tiles + 2, TILE, lanes), F32)
    moduli_of = lambda lanes: pltpu.VMEM((2, groups + 3, TILE, lanes), F32)

    packets = 1 if gx == 2 else 2
    v, moduli, *sent = pl.pallas_call(
        functools.partial(prepare, gx=gx),
        in_specs=[hbm] * 3,
        out_specs=[vmem] * (2 + packets),
        out_shape=[shape(*dims, width), shape(2, groups, TILE, width)] + [shape(3, TILE, width)] * packets,
        scratch_shapes=[
            pltpu.VMEM((tile_rows, tile_cols), jnp.int32),
            pltpu.VMEM((2, lines, tile_rows, LANES), F32),
            pltpu.VMEM((2, 2, TILE, width), F32),
            pltpu.SMEM(lame_table.shape, F32),
            pltpu.SemaphoreType.DMA((3, TILE)),
        ],
        compiler_params=params,
        name="prepare",
    )(far(lame_table), far(load), far(material))

    if gx == 2:
        above = below = lax.ppermute(sent[0], "gx", [(0, 1), (1, 0)])
    else:
        above = lax.ppermute(sent[0], "gx", [(i, i + 1) for i in range(gx - 1)])
        below = lax.ppermute(sent[1], "gx", [(i + 1, i) for i in range(gx - 1)])

    slots = tiles + groups + 2
    packet_rows = TILE * (-(-slots // 4) + 1)
    partial_of = lambda lanes: pltpu.VMEM((2 * ITERS, TILE, lanes), F32)
    packet, beside, push, partial = pl.pallas_call(
        early,
        in_specs=[vmem] * 2,
        out_specs=[vmem] * 4,
        out_shape=[shape(packet_rows, LANES), beside_of(width), push_of(width), partial_of(width)],
        compiler_params=params,
        name="early",
    )(pin(v), pin(moduli))
    carried = v, packet, beside, push, partial
    v, packet, _, push, _ = pl.pallas_call(
        functools.partial(block, gx=gx),
        in_specs=[vmem] * 8,
        out_specs=[vmem] * 5,
        out_shape=[pltpu.VMEM(x.shape, F32) for x in carried],
        scratch_shapes=[strips_of(width), moduli_of(width)],
        input_output_aliases={i: i for i in range(5)},
        compiler_params=params,
        name="block",
    )(*map(pin, (*carried, moduli, above, below)))

    arrived = [packet] + [lax.ppermute(packet, "gy", route) for route in routes(gy)]
    v = pl.pallas_call(
        finish,
        in_specs=[vmem] * 2,
        out_specs=vmem,
        out_shape=pltpu.VMEM(v.shape, F32),
        input_output_aliases={0: 0},
        compiler_params=params,
        name="finish",
    )(pin(v), pin(push))
    strips, moments, strips_push, v = pl.pallas_call(
        functools.partial(interfaces, gx=gx, gy=gy, sources=source_of(gy)),
        in_specs=[vmem] * (gy + 1),
        out_specs=[vmem] * 4,
        out_shape=[shape(*dims, LANES), shape(2, 2 * ITERS, LANES), push_of(LANES), shape(*dims, width)],
        input_output_aliases={gy: 3},
        scratch_shapes=[strips_of(LANES), beside_of(LANES), moduli_of(LANES), partial_of(LANES)],
        compiler_params=params,
        name="interfaces",
    )(*map(pin, arrived), pin(v))

    gathered = [moments] + [lax.ppermute(moments, "gx", route) for route in routes(gx)]
    v = pl.pallas_call(
        merge,
        in_specs=[vmem] * 3,
        out_specs=vmem,
        out_shape=pltpu.VMEM(v.shape, F32),
        scratch_shapes=[pltpu.VMEM((2, ITERS, 2, tiles, TILE, LANES), F32)],
        input_output_aliases={0: 0},
        compiler_params=params,
        name="merge",
    )(*map(pin, (v, strips, strips_push)))
    return pl.pallas_call(
        functools.partial(combine, gx=gx),
        in_specs=[vmem] * (gx + 1),
        out_specs=[hbm] * 2,
        out_shape=[jax.ShapeDtypeStruct(load.shape, F32)] * 2,
        scratch_shapes=[pltpu.VMEM((2, *dims[1:], width), F32), pltpu.SemaphoreType.DMA((2, 2, TILE))],
        compiler_params=params,
        name="combine",
    )(*map(pin, gathered), pin(v))


def solution(mesh):
    return jax.shard_map(
        on_device,
        mesh=mesh,
        in_specs=(P("samp", None, "gx", "gy"), P("samp", "gx", "gy"), P()),
        out_specs=(P("samp", None, "gx", "gy"), P("samp", None, "gx", "gy")),
        check_vma=False,
    )
```

```python
import functools

import jax
import jax.numpy as jnp
from jax import lax
from jax.experimental import pallas as pl
from jax.experimental.pallas import tpu as pltpu
from jax.sharding import PartitionSpec as P

TILE = 8
CLASSES = 8
ITERS = 4
HALO = ITERS
LANES = 128
STRIP = 2 * TILE
VMEM_LIMIT = 16 << 20
F32 = jnp.float32


def iota(shape, dim):
    return lax.broadcasted_iota(jnp.int32, shape, dim)


def fast_two_sum(a, b):
    s = a + b
    return s, b - (s - a)


def two_sum(a, b):
    s = a + b
    t = s - a
    return s, (a - (s - t)) + (b - t)


def split(a):
    t = 4097.0 * a
    high = t - (t - a)
    return high, a - high


def two_prod(a, b):
    p = a * b
    ah, al = split(a)
    bh, bl = split(b)
    return p, ((ah * bh - p) + ah * bl + al * bh) + al * bl


def ds_add(x, y):
    s, e = two_sum(x[0], y[0])
    return fast_two_sum(s, e + (x[1] + y[1]))


def ds_mul(x, y):
    p, e = two_prod(x[0], y[0])
    return fast_two_sum(p, e + (x[0] * y[1] + x[1] * y[0]))


def ds_neg(x):
    return -x[0], -x[1]


def ds_scale(c, x):
    p, e = two_prod(jnp.full(x[0].shape, c, F32), x[0])
    return fast_two_sum(p, e + c * x[1])


def ds_inverse(x):
    first = 1.0 / x[0]
    p, e = two_prod(first, x[0])
    rest = ((1.0 - p) - e) - first * x[1]
    return fast_two_sum(first, first * rest)


def stress(here, below, bulk, mu):
    sums, gaps = [], []
    for (x, right), (y, beside) in zip(here, below):
        sums.append((x + right, y + beside))
        gaps.append((right - x, beside - y))
    exx = sums[0][1] - sums[0][0]
    eyy = gaps[1][1] + gaps[1][0]
    gxy = (gaps[0][1] + gaps[0][0]) + (sums[1][1] - sums[1][0])
    mean = bulk * (exx + eyy)
    apart = mu * (exx - eyy)
    return (mean + apart, mean - apart, mu * gxy), (exx, eyy, gxy)


def forces(before, s):
    pxx, pyy, pxy = before
    xx, yy, xy = s
    dxx = pxx - xx
    sxy = pxy + xy
    dxy = pxy - xy
    syy = pyy + yy
    return (dxx + sxy, dxx - sxy), (dxy + syy, dxy - syy)


def total(terms):
    return functools.reduce(lambda a, b: a + b, terms)


def dot(x, y):
    return total([a * b for a, b in zip(x, y)])


def up(x):
    return pltpu.roll(x, TILE - 1, 0)


def down(x):
    return pltpu.roll(x, 1, 0)


def lane_tiles(width):
    return [slice(start, start + LANES) for start in range(0, width, LANES)]


def cells(k, v, beside, push, moduli, partial, at, span, squares, works, outer=(None, None), more=False):
    tiles = v.shape[2]
    groups = tiles // TILE

    def nodes(t):
        if 0 <= t < tiles:
            return [(v[k, c, t, :, at], beside[c, t, :, at]) for c in range(2)]
        return outer[t > 0]

    first, last = span
    here = nodes(first)
    before = None
    own = [partial[2 * k, :, at]] if more else []
    energy = [partial[2 * k + 1, :, at]] if more else []
    for t in range(first, last):
        after = nodes(t + 1)
        g = groups if t < 0 else t // TILE
        s, strain = stress(here, after, moduli[0, g, :, at], moduli[1, g, :, at])
        if t in works:
            energy = [total(energy + [dot(strain, s)])]
        for node, tile in ((t, here), (t + 1, after)):
            if node in squares and (node == t or node == last):
                values = [x for x, _ in tile]
                own = [total(own + [dot(values, values)])]
        if before:
            for c, (x, y) in enumerate(forces(before, s)):
                push[0, c, t, :, at], push[1, c, t, :, at] = x, y
        before, here = s, after
    if squares:
        partial[2 * k, :, at] = own[0]
    if works:
        partial[2 * k + 1, :, at] = energy[0]


def outer_tiles(k, v, strips, beside, at):
    tiles = v.shape[2]
    sub = iota((TILE, LANES), 0)
    above, below = [], []
    for c in range(2):
        first = v[k, c, 0, :, at], beside[c, 0, :, at]
        last = v[k, c, tiles - 1, :, at], beside[c, tiles - 1, :, at]
        top, bottom = ((strips[s, c, :, at], beside[c, tiles + s, :, at]) for s in range(2))
        above.append(tuple(jnp.where(sub == 0, pltpu.roll(x, 5, 0), down(y)) for x, y in zip(top, last)))
        below.append(tuple(jnp.where(sub == TILE - 1, pltpu.roll(x, 3, 0), up(y)) for x, y in zip(bottom, first)))
    return above, below


def strip_cells(strips, beside, push, moduli, mask, at):
    tiles = push.shape[2] - 2
    groups = tiles // TILE
    for s in range(2):
        here = [(strips[s, c, :, at], beside[c, tiles + s, :, at]) for c in range(2)]
        modulus = [moduli[c, groups + 1 + s, :, at] for c in range(2)]
        t, _ = stress(here, [(up(x), up(y)) for x, y in here], *modulus)
        for c, (x, y) in enumerate(forces(tuple(down(x) for x in t), t)):
            push[0, c, tiles + s, :, at] = x * mask[:, at] if s else x
            push[1, c, tiles + s, :, at] = y * mask[:, at] if s else y


def strip_neighbours(strips, beside, right):
    tiles = beside.shape[1] - 2
    for c in range(2):
        for s in range(2):
            beside[c, tiles + s] = right(strips[s, c])


def advance(k, v, strips, beside, push, right, left, clear, which=None):
    tiles = v.shape[2]
    for t in which or range(tiles + 2):
        for c in range(2):
            x, y = push[0, c, t], push[1, c, t]
            beside[c, t] = clear(x + right(y))
            if t < tiles:
                v[k + 1, c, t] = left(x) + y
            else:
                strips[t - tiles, c] = left(x) + y


def basis_pass(k, v, strips, beside, push, moduli, partial, mask):
    for at in lane_tiles(v.shape[4]):
        outer = outer_tiles(k, v, strips, beside, at)
        every = range(v.shape[2])
        cells(k, v, beside, push, moduli, partial, at, (-1, len(every)), every, every, outer)
    for at in lane_tiles(v.shape[4]) if k + 1 < ITERS else []:
        strip_cells(strips, beside, push, moduli, mask, at)


def finish(v_in, push, v):
    for t in range(v.shape[2]):
        for c in range(2):
            v[ITERS, c, t] = pltpu.roll(push[0, c, t], 1, 1) + push[1, c, t]


def merge(v_in, strips, strips_push, v, ends):
    tiles, _, width = v.shape[2:]
    mine = lax.axis_index("gy")
    to_left = lax.rem(LANES - STRIP * mine, LANES)
    to_right = lax.rem(2 * LANES - STRIP - STRIP * mine, LANES)
    lane = iota((TILE, LANES), 1)

    @pl.loop(0, tiles, unroll=4)
    def _(t):
        for c in range(2):
            x = pltpu.roll(strips_push[0, c, t], 1, 1)
            last = jnp.where(lane == 0, 0.0, x) + strips_push[1, c, t]
            for k in range(ITERS):
                edge = strips[k + 1, c, t] if k + 1 < ITERS else last
                ends[0, k, c, t] = pltpu.roll(edge, to_left, 1)
                ends[1, k, c, t] = pltpu.roll(edge, to_right, 1)

    @pl.loop(0, tiles, unroll=4)
    def _(t):
        for k in range(ITERS):
            for c in range(2):
                for side, start in enumerate((0, width - LANES)):
                    at = slice(start, start + LANES)
                    inside = lane < LANES - HALO if side else lane >= HALO
                    v[k + 1, c, t, :, at] = jnp.where(inside, v[k + 1, c, t, :, at], ends[side, k, c, t])


def moment_rows(partial, keep):
    row = iota((2 * ITERS, LANES), 0)
    result = jnp.zeros((2 * ITERS, LANES), F32)
    for index in range(2 * ITERS):
        part = jnp.where(keep, partial[index], 0.0)
        folded = part[:, :LANES]
        for start in range(LANES, part.shape[1], LANES):
            folded = folded + part[:, start : start + LANES]
        total = jnp.sum(folded, axis=0, keepdims=True)
        result = jnp.where(row == index, total, result)
    return result


def fill_moduli(moduli, c, groups, first, last, edge):
    sub = iota(edge.shape, 0)
    low = sub < HALO
    above, below = edge[1:2, :], edge[0:1, :]
    moduli[c, groups] = jnp.where(sub == 0, above, pltpu.roll(moduli[c, groups - 1], 1, 0))
    moduli[c, groups + 1] = jnp.where(low, above, first)
    moduli[c, groups + 2] = jnp.where(low, last, below)


def fill_strips(strips, c, halo, v):
    sub = iota(halo.shape, 0)
    low = sub < HALO
    tiles = v.shape[2]
    first = last = halo
    for r in range(HALO):
        first = jnp.where(sub == r, v[0, c, r, 0:1, :], first)
        last = jnp.where(sub == TILE - 1 - r, v[0, c, tiles - 1 - r, TILE - 1 :, :], last)
    strips[0, c] = pltpu.roll(jnp.where(low, first, halo), HALO, 0)
    strips[1, c] = pltpu.roll(jnp.where(low, halo, last), HALO, 0)


def prepare(table, load, material, v, moduli, *rest, gx):
    *packets, kinds_buffer, lines, ends, scalars, sems = rest
    rows, cols = material.shape[1:]
    height, width = load.shape[2:]
    tiles = height // TILE
    groups = tiles // TILE
    columns = [slice(start, start + LANES) for start in range(0, width, LANES)]
    early = [pltpu.make_async_copy(material.at[0], kinds_buffer, sems.at[2, 0])]
    for i, at in enumerate((slice(0, TILE), slice(height - TILE, height))):
        early.append(pltpu.make_async_copy(load.at[0, :, at, :], ends.at[i], sems.at[2, i + 1]))
    early.append(pltpu.make_async_copy(table, scalars, sems.at[2, 3]))
    late = []
    for c in range(2):
        for s in range(TILE):
            at = slice(tiles * s, tiles * (s + 1))
            late.append(pltpu.make_async_copy(load.at[0, c, at, :], v.at[0, c, :, s, :], sems.at[c, s]))
    for copy in early + late:
        copy.start()
    early[0].wait()
    grid = (cols, width)
    expand = iota(grid, 1) // TILE == iota(grid, 0)
    kinds = jnp.dot(
        kinds_buffer[...].astype(F32).astype(jnp.bfloat16),
        expand.astype(F32).astype(jnp.bfloat16),
        preferred_element_type=F32,
    )
    early[3].wait()
    bulk = jnp.zeros((rows, width), F32)
    shear = bulk
    for k in range(CLASSES):
        mu = 0.25 * scalars[1, k]
        here = kinds == float(k)
        bulk = jnp.where(here, 0.25 * scalars[0, k] + mu, bulk)
        shear = jnp.where(here, mu, shear)
    for c, values in enumerate((bulk, shear)):
        for l, lanes in enumerate(columns):
            lines[c, l] = values[:, lanes]
            for g in range(groups):
                moduli[c, g, :, lanes] = lines[c, l, pl.ds(g, TILE, stride=groups), :]
    place = lax.axis_index("gx")
    for copy in early[1:3]:
        copy.wait()

    def fill(packet, down):
        for c in range(2):
            packet[c] = jnp.where(down, ends[1, c], ends[0, c])
            row = jnp.where(down, moduli[c, groups - 1, TILE - 1 :, :], moduli[c, 0, 0:1, :])
            packet[2, c : c + 1, :] = row
        packet[2, 2:, :] = jnp.zeros((TILE - 2, width), F32)

    if gx == 2:
        fill(packets[0], place == 0)
    else:
        fill(packets[0], True)
        fill(packets[1], False)
    for copy in late:
        copy.wait()


def pack(packet, lines, pick, width):
    lane = iota((TILE, LANES), 1)
    for line in lines:
        result = jnp.zeros((TILE, LANES), F32)
        for part in range(4):
            for c in range(2):
                offset = 32 * part + STRIP * c
                first = pick(4 * line + part, c, slice(0, LANES))
                if first is None:
                    continue
                first = pltpu.roll(first, offset, 1) if offset else first
                final = pick(4 * line + part, c, slice(width - LANES, width))
                final = pltpu.roll(final, (offset + STRIP) % LANES, 1)
                result = jnp.where((lane >= offset) & (lane < offset + TILE), first, result)
                result = jnp.where((lane >= offset + TILE) & (lane < offset + STRIP), final, result)
        packet[TILE * line : TILE * (line + 1), :] = result


def early(v_in, moduli, v, packet, beside, push, partial):
    tiles, _, width = v.shape[2:]
    for c in range(2):
        for t in range(tiles):
            beside[c, t] = pltpu.roll(v[0, c, t], width - 1, 1)
    pack(packet, range(tiles // 4), lambda slot, c, at: v[0, c, slot, :, at], width)
    right = lambda x: pltpu.roll(x, width - 1, 1)
    left = lambda x: pltpu.roll(x, 1, 1)
    for at in lane_tiles(width):
        cells(0, v, beside, push, moduli, partial, at, (0, tiles - 1), range(tiles), range(tiles - 1))
    inner = range(2, tiles - 2)
    advance(0, v, None, beside, push, right, left, lambda x: x, inner)
    for at in lane_tiles(width):
        cells(1, v, beside, push, moduli, partial, at, (2, tiles - 3), inner, range(2, tiles - 3))


def block(*refs, gx):
    group_moduli, above, below, v, packet, beside, push, partial, strips, moduli = refs[5:]
    tiles, _, width = v.shape[2:]
    groups = tiles // TILE
    place = lax.axis_index("gx")
    has_above = place > 0
    has_below = place < gx - 1
    sub = iota((TILE, width), 0)
    low = sub < HALO

    halo, edge = [], []
    for c in range(2):
        under = jnp.where(has_below, below[c], 0.0)
        over = jnp.where(has_above, above[c], 0.0)
        halo.append(jnp.where(low, under, over))
        fill_strips(strips, c, halo[c], v)
        for g in range(groups):
            moduli[c, g] = group_moduli[c, g]
        under = jnp.where(has_below, below[2, c : c + 1, :], 0.0)
        over = jnp.where(has_above, above[2, c : c + 1, :], 0.0)
        edge.append(jnp.where(sub == 0, under, over))
        ends = moduli[c, 0, 0:1, :], moduli[c, groups - 1, TILE - 1 :, :]
        fill_moduli(moduli, c, groups, *ends, edge[c])
    mask = jnp.where(low, 1.0, jnp.where(has_below, 1.0, 0.0))
    right = lambda x: pltpu.roll(x, width - 1, 1)
    left = lambda x: pltpu.roll(x, 1, 1)

    def pick(slot, c, at):
        if slot == tiles:
            return halo[c][:, at]
        if slot <= tiles + groups:
            return moduli[c, slot - tiles - 1, :, at]
        return edge[c][:, at] if slot == tiles + groups + 1 else None

    pack(packet, range(tiles // 4, packet.shape[0] // TILE - 1), pick, width)
    strip_neighbours(strips, beside, right)
    edges = [0, 1, tiles - 2, tiles - 1]
    same = lambda x: x
    for k in range(ITERS):
        if k < 2:
            for at in lane_tiles(width):
                strip_cells(strips, beside, push, moduli, mask, at)
                outer = outer_tiles(k, v, strips, beside, at)
                part = functools.partial(cells, k, v, beside, push, moduli, partial, at, outer=outer, more=True)
                part((-1, 1 + 2 * k), edges[: 2 * k], edges[: 2 * k])
                part((tiles - 2 - 2 * k, tiles), edges[2:] * k, range(tiles - 1 - 2 * k, tiles))
        else:
            basis_pass(k, v, strips, beside, push, moduli, partial, mask)
        if k + 1 < ITERS:
            which = None if k else edges + [tiles, tiles + 1]
            advance(k, v, strips, beside, push, right, left, same, which)

    lane = iota((TILE, width), 1)
    keep = (lane >= HALO) & (lane < width - HALO)
    packet[packet.shape[0] - TILE :, :] = moment_rows(partial, keep)


def interfaces(*refs, gx, gy, sources):
    packets = refs[:gy]
    _, v, moments, push, _, strips, beside, moduli, partial = refs[gy:]
    tiles = v.shape[2]
    groups = tiles // TILE
    mine = lax.axis_index("gy")
    has_below = lax.axis_index("gx") < gx - 1
    lines = packets[0].shape[0] // TILE - 1

    def sort(rows):
        arrived = [p[rows, :] for p in packets]
        result = []
        for q in range(gy):
            chosen = arrived[0]
            for k in range(1, gy):
                chosen = jnp.where(sources(mine, k) == q, arrived[k], chosen)
            result.append(chosen)
        return result

    lane = iota((TILE, LANES), 1)
    sub = iota((TILE, LANES), 0)
    halo, edge = [None] * 2, [None] * 2
    for line in range(lines):
        pieces = sort(slice(TILE * line, TILE * (line + 1)))
        for part in range(4):
            slot = 4 * line + part
            for c in range(2):
                result = jnp.zeros((TILE, LANES), F32)
                for q in range(gy):
                    shift = (STRIP * q - 32 * part - STRIP * c) % LANES
                    piece = pltpu.roll(pieces[q], shift, 1) if shift else pieces[q]
                    result = jnp.where((lane >= STRIP * q) & (lane < STRIP * (q + 1)), piece, result)
                if slot < tiles:
                    v[0, c, slot] = result
                elif slot == tiles:
                    halo[c] = result
                elif slot <= tiles + groups:
                    moduli[c, slot - tiles - 1] = result
                elif slot == tiles + groups + 1:
                    edge[c] = result
    for c in range(2):
        fill_strips(strips, c, halo[c], v)
        ends = moduli[c, 0, 0:1, :], moduli[c, groups - 1, TILE - 1 :, :]
        fill_moduli(moduli, c, groups, *ends, edge[c])
    mask = jnp.where(sub < HALO, 1.0, jnp.where(has_below, 1.0, 0.0))
    at_end = lane == STRIP * gy - 1
    at_start = lane == 0
    clear = lambda x: jnp.where(at_end, 0.0, x)
    right = lambda x: clear(pltpu.roll(x, LANES - 1, 1))
    left = lambda x: jnp.where(at_start, 0.0, pltpu.roll(x, 1, 1))

    for c in range(2):
        for t in range(tiles):
            beside[c, t] = right(v[0, c, t])
    strip_neighbours(strips, beside, right)

    for k in range(ITERS - 1):
        basis_pass(k, v, strips, beside, push, moduli, partial, mask)
        advance(k, v, strips, beside, push, right, left, clear)
    basis_pass(ITERS - 1, v, strips, beside, push, moduli, partial, mask)

    column = lane % STRIP
    keep = ((column < HALO) | (column >= STRIP - HALO)) & (lane < STRIP * gy)
    high = moment_rows(partial, keep)
    rest = jnp.zeros_like(high)
    for piece in sort(slice(TILE * lines, TILE * (lines + 1))):
        high, e = two_sum(high, piece)
        rest = rest + e
    moments[0] = high
    moments[1] = rest


def coefficients(moments):
    shape = moments[0].shape
    take = lambda x, l: jnp.broadcast_to(x[l : l + 1, :], shape)
    s = {l: (take(moments[0], l), take(moments[1], l)) for l in range(2 * ITERS)}
    q = dict(s)
    zero = jnp.zeros(shape, F32)
    residual = [zero + 1.0]
    solution = []
    for k in range(ITERS):
        if k:
            beta = ds_neg(ds_mul(s[k], inverse))
            q = {l: ds_add(s[l], ds_mul(beta, q[l])) for l in range(k, 2 * ITERS - k)}
            direction = [r + beta[0] * p for r, p in zip(residual, direction + [zero])]
        else:
            direction = residual
        push = {l: ds_add(ds_scale(0.05, q[l]), q[l + 1]) for l in range(k, 2 * ITERS - 1 - k)}
        inverse = ds_inverse(push[k])
        alpha = ds_mul(s[k], inverse)
        s = {l: ds_add(s[l], ds_neg(ds_mul(alpha, push[l]))) for l in range(k + 1, 2 * ITERS - 1 - k)}
        solution = [x + alpha[0] * p for x, p in zip(solution + [zero], direction)]
        change = [0.05 * a + b for a, b in zip(direction + [zero], [zero] + direction)]
        residual = [r - alpha[0] * d for r, d in zip(residual + [zero], change)]
    return solution, residual


def combine(*refs, gx):
    gathered = refs[:gx]
    v, *outs, buffer, sems = refs[gx:]
    tiles, _, width = v.shape[2:]
    columns = [slice(start, start + LANES) for start in range(0, width, LANES)]
    moments = (gathered[0][0], gathered[0][1])
    for other in gathered[1:]:
        moments = ds_add(moments, (other[0], other[1]))
    for count, distance in ((8, 16), (16, 1)):
        terms = [moments] + [tuple(pltpu.roll(x, distance * i, 1) for x in moments) for i in range(1, count)]
        while len(terms) > 1:
            terms = [ds_add(a, b) for a, b in zip(terms[::2], terms[1::2])]
        moments = terms[0]
    weights = coefficients(moments)
    copies = []
    for i, w in enumerate(weights):
        for c in range(2):
            for t in range(tiles):
                for lanes in columns:
                    buffer[i, c, t, :, lanes] = dot(w, [v[k, c, t, :, lanes] for k in range(len(w))])
        for s in range(TILE):
            at = slice(tiles * s, tiles * (s + 1))
            copy = pltpu.make_async_copy(buffer.at[i, :, :, s, :], outs[i].at[0, :, at, :], sems.at[i, 0, s])
            copy.start()
            copies.append(copy)
    for copy in copies:
        copy.wait()


def routes(n):
    if n & (n - 1) == 0:
        return [[(i, i ^ k) for i in range(n)] for k in range(1, n)]
    return [[(i, (i + k) % n) for i in range(n)] for k in range(1, n)]


def source_of(n):
    if n & (n - 1) == 0:
        return lambda mine, k: mine ^ k
    return lambda mine, k: lax.rem(mine - k + n, n)


def on_device(load, material, lame_table):
    gx, gy = lax.axis_size("gx"), lax.axis_size("gy")
    rows, width = load.shape[2:]
    tiles = rows // TILE
    groups = tiles // TILE
    lines = width // LANES
    dims = (ITERS + 1, 2, tiles, TILE)
    tile_rows, tile_cols = material.shape[1:]
    assert rows == TILE * TILE * groups and width % LANES == 0 and STRIP * gy <= LANES
    vmem = pl.BlockSpec(memory_space=pltpu.VMEM)
    hbm = pl.BlockSpec(memory_space=pltpu.HBM)
    shape = lambda *dims: pltpu.VMEM(dims, F32)
    params = pltpu.CompilerParams(vmem_limit_bytes=VMEM_LIMIT)
    pin = lambda x: pltpu.with_memory_space_constraint(x, pltpu.VMEM)
    far = lambda x: pltpu.with_memory_space_constraint(x, pltpu.HBM)
    strips_of = lambda lanes: pltpu.VMEM((2, 2, TILE, lanes), F32)
    beside_of = lambda lanes: pltpu.VMEM((2, tiles + 2, TILE, lanes), F32)
    push_of = lambda lanes: pltpu.VMEM((2, 2, tiles + 2, TILE, lanes), F32)
    moduli_of = lambda lanes: pltpu.VMEM((2, groups + 3, TILE, lanes), F32)

    packets = 1 if gx == 2 else 2
    v, moduli, *sent = pl.pallas_call(
        functools.partial(prepare, gx=gx),
        in_specs=[hbm] * 3,
        out_specs=[vmem] * (2 + packets),
        out_shape=[shape(*dims, width), shape(2, groups, TILE, width)] + [shape(3, TILE, width)] * packets,
        scratch_shapes=[
            pltpu.VMEM((tile_rows, tile_cols), jnp.int32),
            pltpu.VMEM((2, lines, tile_rows, LANES), F32),
            pltpu.VMEM((2, 2, TILE, width), F32),
            pltpu.SMEM(lame_table.shape, F32),
            pltpu.SemaphoreType.DMA((3, TILE)),
        ],
        compiler_params=params,
        name="prepare",
    )(far(lame_table), far(load), far(material))

    if gx == 2:
        above = below = lax.ppermute(sent[0], "gx", [(0, 1), (1, 0)])
    else:
        above = lax.ppermute(sent[0], "gx", [(i, i + 1) for i in range(gx - 1)])
        below = lax.ppermute(sent[1], "gx", [(i + 1, i) for i in range(gx - 1)])

    slots = tiles + groups + 2
    packet_rows = TILE * (-(-slots // 4) + 1)
    partial_of = lambda lanes: pltpu.VMEM((2 * ITERS, TILE, lanes), F32)
    carried = pl.pallas_call(
        early,
        in_specs=[vmem] * 2,
        out_specs=[vmem] * 5,
        input_output_aliases={0: 0},
        out_shape=[shape(*dims, width), shape(packet_rows, LANES), beside_of(width), push_of(width), partial_of(width)],
        compiler_params=params,
        name="early",
    )(pin(v), pin(moduli))
    v, packet, _, push, _ = pl.pallas_call(
        functools.partial(block, gx=gx),
        in_specs=[vmem] * 8,
        out_specs=[vmem] * 5,
        out_shape=[pltpu.VMEM(x.shape, F32) for x in carried],
        scratch_shapes=[strips_of(width), moduli_of(width)],
        input_output_aliases={i: i for i in range(5)},
        compiler_params=params,
        name="block",
    )(*map(pin, (*carried, moduli, above, below)))

    arrived = [packet] + [lax.ppermute(packet, "gy", route) for route in routes(gy)]
    v = pl.pallas_call(
        finish,
        in_specs=[vmem] * 2,
        out_specs=vmem,
        out_shape=pltpu.VMEM(v.shape, F32),
        input_output_aliases={0: 0},
        compiler_params=params,
        name="finish",
    )(pin(v), pin(push))
    strips, moments, strips_push, v = pl.pallas_call(
        functools.partial(interfaces, gx=gx, gy=gy, sources=source_of(gy)),
        in_specs=[vmem] * (gy + 1),
        out_specs=[vmem] * 4,
        out_shape=[shape(*dims, LANES), shape(2, 2 * ITERS, LANES), push_of(LANES), shape(*dims, width)],
        input_output_aliases={gy: 3},
        scratch_shapes=[strips_of(LANES), beside_of(LANES), moduli_of(LANES), partial_of(LANES)],
        compiler_params=params,
        name="interfaces",
    )(*map(pin, arrived), pin(v))

    gathered = [moments] + [lax.ppermute(moments, "gx", route) for route in routes(gx)]
    v = pl.pallas_call(
        merge,
        in_specs=[vmem] * 3,
        out_specs=vmem,
        out_shape=pltpu.VMEM(v.shape, F32),
        scratch_shapes=[pltpu.VMEM((2, ITERS, 2, tiles, TILE, LANES), F32)],
        input_output_aliases={0: 0},
        compiler_params=params,
        name="merge",
    )(*map(pin, (v, strips, strips_push)))
    return pl.pallas_call(
        functools.partial(combine, gx=gx),
        in_specs=[vmem] * (gx + 1),
        out_specs=[hbm] * 2,
        out_shape=[jax.ShapeDtypeStruct(load.shape, F32)] * 2,
        scratch_shapes=[pltpu.VMEM((2, *dims[1:], width), F32), pltpu.SemaphoreType.DMA((2, 2, TILE))],
        compiler_params=params,
        name="combine",
    )(*map(pin, gathered), pin(v))


def solution(mesh):
    return jax.shard_map(
        on_device,
        mesh=mesh,
        in_specs=(P("samp", None, "gx", "gy"), P("samp", "gx", "gy"), P()),
        out_specs=(P("samp", None, "gx", "gy"), P("samp", None, "gx", "gy")),
        check_vma=False,
    )
```

```python
import functools

import jax
import jax.numpy as jnp
from jax import lax
from jax.experimental import pallas as pl
from jax.experimental.pallas import tpu as pltpu
from jax.sharding import PartitionSpec as P

TILE = 8
CLASSES = 8
ITERS = 4
HALO = ITERS
LANES = 128
STRIP = 2 * TILE
VMEM_LIMIT = 16 << 20
F32 = jnp.float32


def iota(shape, dim):
    return lax.broadcasted_iota(jnp.int32, shape, dim)


def fast_two_sum(a, b):
    s = a + b
    return s, b - (s - a)


def two_sum(a, b):
    s = a + b
    t = s - a
    return s, (a - (s - t)) + (b - t)


def split(a):
    t = 4097.0 * a
    high = t - (t - a)
    return high, a - high


def two_prod(a, b):
    p = a * b
    ah, al = split(a)
    bh, bl = split(b)
    return p, ((ah * bh - p) + ah * bl + al * bh) + al * bl


def ds_add(x, y):
    s, e = two_sum(x[0], y[0])
    return fast_two_sum(s, e + (x[1] + y[1]))


def loose_add(x, y):
    s, e = two_sum(x[0], y[0])
    return s, e + (x[1] + y[1])


def ds_mul(x, y):
    p, e = two_prod(x[0], y[0])
    return p, e + (x[0] * y[1] + x[1] * y[0])


def ds_neg(x):
    return -x[0], -x[1]


def ds_scale(c, x):
    p, e = two_prod(jnp.full(x[0].shape, c, F32), x[0])
    return p, e + c * x[1]


def ds_inverse(x):
    first = 1.0 / x[0]
    p, e = two_prod(first, x[0])
    rest = ((1.0 - p) - e) - first * x[1]
    return first, first * rest


def stress(here, below, bulk, mu):
    sums, gaps = [], []
    for (x, right), (y, beside) in zip(here, below):
        sums.append((x + right, y + beside))
        gaps.append((right - x, beside - y))
    exx = sums[0][1] - sums[0][0]
    eyy = gaps[1][1] + gaps[1][0]
    gxy = (gaps[0][1] + gaps[0][0]) + (sums[1][1] - sums[1][0])
    mean = bulk * (exx + eyy)
    apart = mu * (exx - eyy)
    return (mean + apart, mean - apart, mu * gxy), (exx, eyy, gxy)


def forces(before, s):
    pxx, pyy, pxy = before
    xx, yy, xy = s
    dxx = pxx - xx
    sxy = pxy + xy
    dxy = pxy - xy
    syy = pyy + yy
    return (dxx + sxy, dxx - sxy), (dxy + syy, dxy - syy)


def total(terms):
    return functools.reduce(lambda a, b: a + b, terms)


def dot(x, y):
    return total([a * b for a, b in zip(x, y)])


def up(x):
    return pltpu.roll(x, TILE - 1, 0)


def down(x):
    return pltpu.roll(x, 1, 0)


def lane_tiles(width):
    return [slice(start, start + LANES) for start in range(0, width, LANES)]


def cells(k, v, beside, push, moduli, partial, at, span, squares, works, outer=(None, None), more=False):
    tiles = v.shape[2]
    groups = tiles // TILE

    def nodes(t):
        if 0 <= t < tiles:
            return [(v[k, c, t, :, at], beside[c, t, :, at]) for c in range(2)]
        return outer[t > 0]

    first, last = span
    here = nodes(first)
    before = None
    own = [partial[2 * k, :, at]] if more else []
    energy = [partial[2 * k + 1, :, at]] if more else []
    for t in range(first, last):
        after = nodes(t + 1)
        g = groups if t < 0 else t // TILE
        s, strain = stress(here, after, moduli[0, g, :, at], moduli[1, g, :, at])
        if t in works:
            energy = [total(energy + [dot(strain, s)])]
        for node, tile in ((t, here), (t + 1, after)):
            if node in squares and (node == t or node == last):
                values = [x for x, _ in tile]
                own = [total(own + [dot(values, values)])]
        if before:
            for c, (x, y) in enumerate(forces(before, s)):
                push[0, c, t, :, at], push[1, c, t, :, at] = x, y
        before, here = s, after
    if squares:
        partial[2 * k, :, at] = own[0]
    if works:
        partial[2 * k + 1, :, at] = energy[0]


def outer_tiles(k, v, strips, beside, at):
    tiles = v.shape[2]
    sub = iota((TILE, LANES), 0)
    above, below = [], []
    for c in range(2):
        first = v[k, c, 0, :, at], beside[c, 0, :, at]
        last = v[k, c, tiles - 1, :, at], beside[c, tiles - 1, :, at]
        top, bottom = ((strips[s, c, :, at], beside[c, tiles + s, :, at]) for s in range(2))
        above.append(tuple(jnp.where(sub == 0, pltpu.roll(x, 5, 0), down(y)) for x, y in zip(top, last)))
        below.append(tuple(jnp.where(sub == TILE - 1, pltpu.roll(x, 3, 0), up(y)) for x, y in zip(bottom, first)))
    return above, below


def strip_cells(strips, beside, push, moduli, mask, at):
    tiles = push.shape[2] - 2
    groups = tiles // TILE
    for s in range(2):
        here = [(strips[s, c, :, at], beside[c, tiles + s, :, at]) for c in range(2)]
        modulus = [moduli[c, groups + 1 + s, :, at] for c in range(2)]
        t, _ = stress(here, [(up(x), up(y)) for x, y in here], *modulus)
        for c, (x, y) in enumerate(forces(tuple(down(x) for x in t), t)):
            push[0, c, tiles + s, :, at] = x * mask[:, at] if s else x
            push[1, c, tiles + s, :, at] = y * mask[:, at] if s else y


def strip_neighbours(strips, beside, right):
    tiles = beside.shape[1] - 2
    for c in range(2):
        for s in range(2):
            beside[c, tiles + s] = right(strips[s, c])


def advance(k, v, strips, beside, push, right, left, clear, which=None):
    tiles = v.shape[2]
    for t in which or range(tiles + 2):
        for c in range(2):
            x, y = push[0, c, t], push[1, c, t]
            beside[c, t] = clear(x + right(y))
            if t < tiles:
                v[k + 1, c, t] = left(x) + y
            else:
                strips[t - tiles, c] = left(x) + y


def basis_pass(k, v, strips, beside, push, moduli, partial, mask):
    for at in lane_tiles(v.shape[4]):
        outer = outer_tiles(k, v, strips, beside, at)
        every = range(v.shape[2])
        cells(k, v, beside, push, moduli, partial, at, (-1, len(every)), every, every, outer)
    for at in lane_tiles(v.shape[4]) if k + 1 < ITERS else []:
        strip_cells(strips, beside, push, moduli, mask, at)


def finish(v_in, push, v):
    for t in range(v.shape[2]):
        for c in range(2):
            v[ITERS, c, t] = pltpu.roll(push[0, c, t], 1, 1) + push[1, c, t]


def merge(v_in, strips, strips_push, v, ends):
    tiles, _, width = v.shape[2:]
    mine = lax.axis_index("gy")
    to_left = lax.rem(LANES - STRIP * mine, LANES)
    to_right = lax.rem(2 * LANES - STRIP - STRIP * mine, LANES)
    lane = iota((TILE, LANES), 1)

    @pl.loop(0, tiles, unroll=4)
    def _(t):
        for c in range(2):
            x = pltpu.roll(strips_push[0, c, t], 1, 1)
            last = jnp.where(lane == 0, 0.0, x) + strips_push[1, c, t]
            for k in range(ITERS):
                edge = strips[k + 1, c, t] if k + 1 < ITERS else last
                ends[0, k, c, t] = pltpu.roll(edge, to_left, 1)
                ends[1, k, c, t] = pltpu.roll(edge, to_right, 1)

    @pl.loop(0, tiles, unroll=4)
    def _(t):
        for k in range(ITERS):
            for c in range(2):
                for side, start in enumerate((0, width - LANES)):
                    at = slice(start, start + LANES)
                    inside = lane < LANES - HALO if side else lane >= HALO
                    v[k + 1, c, t, :, at] = jnp.where(inside, v[k + 1, c, t, :, at], ends[side, k, c, t])


def moment_rows(partial, keep):
    row = iota((2 * ITERS, LANES), 0)
    result = jnp.zeros((2 * ITERS, LANES), F32)
    for index in range(2 * ITERS):
        part = jnp.where(keep, partial[index], 0.0)
        folded = part[:, :LANES]
        for start in range(LANES, part.shape[1], LANES):
            folded = folded + part[:, start : start + LANES]
        total = jnp.sum(folded, axis=0, keepdims=True)
        result = jnp.where(row == index, total, result)
    return result


def fill_moduli(moduli, c, groups, first, last, edge):
    sub = iota(edge.shape, 0)
    low = sub < HALO
    above, below = edge[1:2, :], edge[0:1, :]
    moduli[c, groups] = jnp.where(sub == 0, above, pltpu.roll(moduli[c, groups - 1], 1, 0))
    moduli[c, groups + 1] = jnp.where(low, above, first)
    moduli[c, groups + 2] = jnp.where(low, last, below)


def fill_strips(strips, c, halo, v):
    sub = iota(halo.shape, 0)
    low = sub < HALO
    tiles = v.shape[2]
    first = last = halo
    for r in range(HALO):
        first = jnp.where(sub == r, v[0, c, r, 0:1, :], first)
        last = jnp.where(sub == TILE - 1 - r, v[0, c, tiles - 1 - r, TILE - 1 :, :], last)
    strips[0, c] = pltpu.roll(jnp.where(low, first, halo), HALO, 0)
    strips[1, c] = pltpu.roll(jnp.where(low, halo, last), HALO, 0)


def prepare(table, load, material, v, moduli, *rest, gx):
    *packets, kinds_buffer, lines, ends, scalars, sems = rest
    rows, cols = material.shape[1:]
    height, width = load.shape[2:]
    tiles = height // TILE
    groups = tiles // TILE
    columns = [slice(start, start + LANES) for start in range(0, width, LANES)]
    early = [pltpu.make_async_copy(material.at[0], kinds_buffer, sems.at[2, 0])]
    for i, at in enumerate((slice(0, TILE), slice(height - TILE, height))):
        early.append(pltpu.make_async_copy(load.at[0, :, at, :], ends.at[i], sems.at[2, i + 1]))
    early.append(pltpu.make_async_copy(table, scalars, sems.at[2, 3]))
    late = []
    for c in range(2):
        for s in range(TILE):
            at = slice(tiles * s, tiles * (s + 1))
            late.append(pltpu.make_async_copy(load.at[0, c, at, :], v.at[0, c, :, s, :], sems.at[c, s]))
    for copy in early + late:
        copy.start()
    early[0].wait()
    grid = (cols, width)
    expand = iota(grid, 1) // TILE == iota(grid, 0)
    kinds = jnp.dot(
        kinds_buffer[...].astype(F32).astype(jnp.bfloat16),
        expand.astype(F32).astype(jnp.bfloat16),
        preferred_element_type=F32,
    )
    early[3].wait()
    bulk = jnp.zeros((rows, width), F32)
    shear = bulk
    for k in range(CLASSES):
        mu = 0.25 * scalars[1, k]
        here = kinds == float(k)
        bulk = jnp.where(here, 0.25 * scalars[0, k] + mu, bulk)
        shear = jnp.where(here, mu, shear)
    for c, values in enumerate((bulk, shear)):
        for l, lanes in enumerate(columns):
            lines[c, l] = values[:, lanes]
            for g in range(groups):
                moduli[c, g, :, lanes] = lines[c, l, pl.ds(g, TILE, stride=groups), :]
    place = lax.axis_index("gx")
    for copy in early[1:3]:
        copy.wait()

    def fill(packet, down):
        for c in range(2):
            packet[c] = jnp.where(down, ends[1, c], ends[0, c])
            row = jnp.where(down, moduli[c, groups - 1, TILE - 1 :, :], moduli[c, 0, 0:1, :])
            packet[2, c : c + 1, :] = row
        packet[2, 2:, :] = jnp.zeros((TILE - 2, width), F32)

    if gx == 2:
        fill(packets[0], place == 0)
    else:
        fill(packets[0], True)
        fill(packets[1], False)
    for copy in late:
        copy.wait()


def pack(packet, lines, pick, width):
    lane = iota((TILE, LANES), 1)
    for line in lines:
        result = jnp.zeros((TILE, LANES), F32)
        for part in range(4):
            for c in range(2):
                offset = 32 * part + STRIP * c
                first = pick(4 * line + part, c, slice(0, LANES))
                if first is None:
                    continue
                first = pltpu.roll(first, offset, 1) if offset else first
                final = pick(4 * line + part, c, slice(width - LANES, width))
                final = pltpu.roll(final, (offset + STRIP) % LANES, 1)
                result = jnp.where((lane >= offset) & (lane < offset + TILE), first, result)
                result = jnp.where((lane >= offset + TILE) & (lane < offset + STRIP), final, result)
        packet[TILE * line : TILE * (line + 1), :] = result


def early(v_in, moduli, v, packet, beside, push, partial):
    tiles, _, width = v.shape[2:]
    for c in range(2):
        for t in range(tiles):
            beside[c, t] = pltpu.roll(v[0, c, t], width - 1, 1)
    pack(packet, range(tiles // 4), lambda slot, c, at: v[0, c, slot, :, at], width)
    right = lambda x: pltpu.roll(x, width - 1, 1)
    left = lambda x: pltpu.roll(x, 1, 1)
    for at in lane_tiles(width):
        cells(0, v, beside, push, moduli, partial, at, (0, tiles - 1), range(tiles), range(tiles - 1))
    inner = range(2, tiles - 2)
    advance(0, v, None, beside, push, right, left, lambda x: x, inner)
    for at in lane_tiles(width):
        cells(1, v, beside, push, moduli, partial, at, (2, tiles - 3), inner, range(2, tiles - 3))


def block(*refs, gx):
    group_moduli, above, below, v, packet, beside, push, partial, strips, moduli = refs[5:]
    tiles, _, width = v.shape[2:]
    groups = tiles // TILE
    place = lax.axis_index("gx")
    has_above = place > 0
    has_below = place < gx - 1
    sub = iota((TILE, width), 0)
    low = sub < HALO

    halo, edge = [], []
    for c in range(2):
        under = jnp.where(has_below, below[c], 0.0)
        over = jnp.where(has_above, above[c], 0.0)
        halo.append(jnp.where(low, under, over))
        fill_strips(strips, c, halo[c], v)
        for g in range(groups):
            moduli[c, g] = group_moduli[c, g]
        under = jnp.where(has_below, below[2, c : c + 1, :], 0.0)
        over = jnp.where(has_above, above[2, c : c + 1, :], 0.0)
        edge.append(jnp.where(sub == 0, under, over))
        ends = moduli[c, 0, 0:1, :], moduli[c, groups - 1, TILE - 1 :, :]
        fill_moduli(moduli, c, groups, *ends, edge[c])
    mask = jnp.where(low, 1.0, jnp.where(has_below, 1.0, 0.0))
    right = lambda x: pltpu.roll(x, width - 1, 1)
    left = lambda x: pltpu.roll(x, 1, 1)

    def pick(slot, c, at):
        if slot == tiles:
            return halo[c][:, at]
        if slot <= tiles + groups:
            return moduli[c, slot - tiles - 1, :, at]
        return edge[c][:, at] if slot == tiles + groups + 1 else None

    pack(packet, range(tiles // 4, packet.shape[0] // TILE - 1), pick, width)
    strip_neighbours(strips, beside, right)
    edges = [0, 1, tiles - 2, tiles - 1]
    same = lambda x: x
    for k in range(ITERS):
        if k < 2:
            for at in lane_tiles(width):
                strip_cells(strips, beside, push, moduli, mask, at)
                outer = outer_tiles(k, v, strips, beside, at)
                part = functools.partial(cells, k, v, beside, push, moduli, partial, at, outer=outer, more=True)
                part((-1, 1 + 2 * k), edges[: 2 * k], edges[: 2 * k])
                part((tiles - 2 - 2 * k, tiles), edges[2:] * k, range(tiles - 1 - 2 * k, tiles))
        else:
            basis_pass(k, v, strips, beside, push, moduli, partial, mask)
        if k + 1 < ITERS:
            which = None if k else edges + [tiles, tiles + 1]
            advance(k, v, strips, beside, push, right, left, same, which)

    lane = iota((TILE, width), 1)
    keep = (lane >= HALO) & (lane < width - HALO)
    packet[packet.shape[0] - TILE :, :] = moment_rows(partial, keep)


def interfaces(*refs, gx, gy, sources):
    packets = refs[:gy]
    _, v, moments, push, _, strips, beside, moduli, partial = refs[gy:]
    tiles = v.shape[2]
    groups = tiles // TILE
    mine = lax.axis_index("gy")
    has_below = lax.axis_index("gx") < gx - 1
    lines = packets[0].shape[0] // TILE - 1

    def sort(rows):
        arrived = [p[rows, :] for p in packets]
        result = []
        for q in range(gy):
            chosen = arrived[0]
            for k in range(1, gy):
                chosen = jnp.where(sources(mine, k) == q, arrived[k], chosen)
            result.append(chosen)
        return result

    lane = iota((TILE, LANES), 1)
    sub = iota((TILE, LANES), 0)
    halo, edge = [None] * 2, [None] * 2
    for line in range(lines):
        pieces = sort(slice(TILE * line, TILE * (line + 1)))
        for part in range(4):
            slot = 4 * line + part
            for c in range(2):
                result = jnp.zeros((TILE, LANES), F32)
                for q in range(gy):
                    shift = (STRIP * q - 32 * part - STRIP * c) % LANES
                    piece = pltpu.roll(pieces[q], shift, 1) if shift else pieces[q]
                    result = jnp.where((lane >= STRIP * q) & (lane < STRIP * (q + 1)), piece, result)
                if slot < tiles:
                    v[0, c, slot] = result
                elif slot == tiles:
                    halo[c] = result
                elif slot <= tiles + groups:
                    moduli[c, slot - tiles - 1] = result
                elif slot == tiles + groups + 1:
                    edge[c] = result
    for c in range(2):
        fill_strips(strips, c, halo[c], v)
        ends = moduli[c, 0, 0:1, :], moduli[c, groups - 1, TILE - 1 :, :]
        fill_moduli(moduli, c, groups, *ends, edge[c])
    mask = jnp.where(sub < HALO, 1.0, jnp.where(has_below, 1.0, 0.0))
    at_end = lane == STRIP * gy - 1
    at_start = lane == 0
    clear = lambda x: jnp.where(at_end, 0.0, x)
    right = lambda x: clear(pltpu.roll(x, LANES - 1, 1))
    left = lambda x: jnp.where(at_start, 0.0, pltpu.roll(x, 1, 1))

    for c in range(2):
        for t in range(tiles):
            beside[c, t] = right(v[0, c, t])
    strip_neighbours(strips, beside, right)

    for k in range(ITERS - 1):
        basis_pass(k, v, strips, beside, push, moduli, partial, mask)
        advance(k, v, strips, beside, push, right, left, clear)
    basis_pass(ITERS - 1, v, strips, beside, push, moduli, partial, mask)

    column = lane % STRIP
    keep = ((column < HALO) | (column >= STRIP - HALO)) & (lane < STRIP * gy)
    high = moment_rows(partial, keep)
    rest = jnp.zeros_like(high)
    for piece in sort(slice(TILE * lines, TILE * (lines + 1))):
        high, e = two_sum(high, piece)
        rest = rest + e
    moments[0] = high
    moments[1] = rest


def coefficients(moments):
    shape = moments[0].shape
    take = lambda x, l: jnp.broadcast_to(x[l : l + 1, :], shape)
    s = {l: (take(moments[0], l), take(moments[1], l)) for l in range(2 * ITERS)}
    q = dict(s)
    zero = jnp.zeros(shape, F32)
    residual = [zero + 1.0]
    solution = []
    for k in range(ITERS):
        if k:
            beta = ds_neg(ds_mul(s[k], inverse))
            q = {l: ds_add(s[l], ds_mul(beta, q[l])) for l in range(k, 2 * ITERS - k)}
            direction = [r + beta[0] * p for r, p in zip(residual, direction + [zero])]
        else:
            direction = residual
        push = {l: ds_add(ds_scale(0.05, q[l]), q[l + 1]) for l in range(k, 2 * ITERS - 1 - k)}
        inverse = ds_inverse(push[k])
        alpha = ds_mul(s[k], inverse)
        s = {l: ds_add(s[l], ds_neg(ds_mul(alpha, push[l]))) for l in range(k + 1, 2 * ITERS - 1 - k)}
        solution = [x + alpha[0] * p for x, p in zip(solution + [zero], direction)]
        change = [0.05 * a + b for a, b in zip(direction + [zero], [zero] + direction)]
        residual = [r - alpha[0] * d for r, d in zip(residual + [zero], change)]
    return solution, residual


def combine(*refs, gx):
    gathered = refs[:gx]
    v, *outs, buffer, sems = refs[gx:]
    tiles, _, width = v.shape[2:]
    columns = [slice(start, start + LANES) for start in range(0, width, LANES)]
    moments = (gathered[0][0], gathered[0][1])
    for other in gathered[1:]:
        moments = ds_add(moments, (other[0], other[1]))
    for count, distance in ((8, 16), (16, 1)):
        terms = [moments] + [tuple(pltpu.roll(x, distance * i, 1) for x in moments) for i in range(1, count)]
        while len(terms) > 1:
            terms = [loose_add(a, b) for a, b in zip(terms[::2], terms[1::2])]
        moments = terms[0]
    moments = fast_two_sum(*moments)
    weights = coefficients(moments)
    copies = []
    for i, w in enumerate(weights):
        for c in range(2):
            for t in range(tiles):
                for lanes in columns:
                    buffer[i, c, t, :, lanes] = dot(w, [v[k, c, t, :, lanes] for k in range(len(w))])
        for s in range(TILE):
            at = slice(tiles * s, tiles * (s + 1))
            copy = pltpu.make_async_copy(buffer.at[i, :, :, s, :], outs[i].at[0, :, at, :], sems.at[i, 0, s])
            copy.start()
            copies.append(copy)
    for copy in copies:
        copy.wait()


def routes(n):
    if n & (n - 1) == 0:
        return [[(i, i ^ k) for i in range(n)] for k in range(1, n)]
    return [[(i, (i + k) % n) for i in range(n)] for k in range(1, n)]


def source_of(n):
    if n & (n - 1) == 0:
        return lambda mine, k: mine ^ k
    return lambda mine, k: lax.rem(mine - k + n, n)


def on_device(load, material, lame_table):
    gx, gy = lax.axis_size("gx"), lax.axis_size("gy")
    rows, width = load.shape[2:]
    tiles = rows // TILE
    groups = tiles // TILE
    lines = width // LANES
    dims = (ITERS + 1, 2, tiles, TILE)
    tile_rows, tile_cols = material.shape[1:]
    assert rows == TILE * TILE * groups and width % LANES == 0 and STRIP * gy <= LANES
    vmem = pl.BlockSpec(memory_space=pltpu.VMEM)
    hbm = pl.BlockSpec(memory_space=pltpu.HBM)
    shape = lambda *dims: pltpu.VMEM(dims, F32)
    params = pltpu.CompilerParams(vmem_limit_bytes=VMEM_LIMIT)
    pin = lambda x: pltpu.with_memory_space_constraint(x, pltpu.VMEM)
    far = lambda x: pltpu.with_memory_space_constraint(x, pltpu.HBM)
    strips_of = lambda lanes: pltpu.VMEM((2, 2, TILE, lanes), F32)
    beside_of = lambda lanes: pltpu.VMEM((2, tiles + 2, TILE, lanes), F32)
    push_of = lambda lanes: pltpu.VMEM((2, 2, tiles + 2, TILE, lanes), F32)
    moduli_of = lambda lanes: pltpu.VMEM((2, groups + 3, TILE, lanes), F32)

    packets = 1 if gx == 2 else 2
    v, moduli, *sent = pl.pallas_call(
        functools.partial(prepare, gx=gx),
        in_specs=[hbm] * 3,
        out_specs=[vmem] * (2 + packets),
        out_shape=[shape(*dims, width), shape(2, groups, TILE, width)] + [shape(3, TILE, width)] * packets,
        scratch_shapes=[
            pltpu.VMEM((tile_rows, tile_cols), jnp.int32),
            pltpu.VMEM((2, lines, tile_rows, LANES), F32),
            pltpu.VMEM((2, 2, TILE, width), F32),
            pltpu.SMEM(lame_table.shape, F32),
            pltpu.SemaphoreType.DMA((3, TILE)),
        ],
        compiler_params=params,
        name="prepare",
    )(far(lame_table), far(load), far(material))

    if gx == 2:
        above = below = lax.ppermute(sent[0], "gx", [(0, 1), (1, 0)])
    else:
        above = lax.ppermute(sent[0], "gx", [(i, i + 1) for i in range(gx - 1)])
        below = lax.ppermute(sent[1], "gx", [(i + 1, i) for i in range(gx - 1)])

    slots = tiles + groups + 2
    packet_rows = TILE * (-(-slots // 4) + 1)
    partial_of = lambda lanes: pltpu.VMEM((2 * ITERS, TILE, lanes), F32)
    carried = pl.pallas_call(
        early,
        in_specs=[vmem] * 2,
        out_specs=[vmem] * 5,
        input_output_aliases={0: 0},
        out_shape=[shape(*dims, width), shape(packet_rows, LANES), beside_of(width), push_of(width), partial_of(width)],
        compiler_params=params,
        name="early",
    )(pin(v), pin(moduli))
    v, packet, _, push, _ = pl.pallas_call(
        functools.partial(block, gx=gx),
        in_specs=[vmem] * 8,
        out_specs=[vmem] * 5,
        out_shape=[pltpu.VMEM(x.shape, F32) for x in carried],
        scratch_shapes=[strips_of(width), moduli_of(width)],
        input_output_aliases={i: i for i in range(5)},
        compiler_params=params,
        name="block",
    )(*map(pin, (*carried, moduli, above, below)))

    arrived = [packet] + [lax.ppermute(packet, "gy", route) for route in routes(gy)]
    v = pl.pallas_call(
        finish,
        in_specs=[vmem] * 2,
        out_specs=vmem,
        out_shape=pltpu.VMEM(v.shape, F32),
        input_output_aliases={0: 0},
        compiler_params=params,
        name="finish",
    )(pin(v), pin(push))
    strips, moments, strips_push, v = pl.pallas_call(
        functools.partial(interfaces, gx=gx, gy=gy, sources=source_of(gy)),
        in_specs=[vmem] * (gy + 1),
        out_specs=[vmem] * 4,
        out_shape=[shape(*dims, LANES), shape(2, 2 * ITERS, LANES), push_of(LANES), shape(*dims, width)],
        input_output_aliases={gy: 3},
        scratch_shapes=[strips_of(LANES), beside_of(LANES), moduli_of(LANES), partial_of(LANES)],
        compiler_params=params,
        name="interfaces",
    )(*map(pin, arrived), pin(v))

    gathered = [moments] + [lax.ppermute(moments, "gx", route) for route in routes(gx)]
    v = pl.pallas_call(
        merge,
        in_specs=[vmem] * 3,
        out_specs=vmem,
        out_shape=pltpu.VMEM(v.shape, F32),
        scratch_shapes=[pltpu.VMEM((2, ITERS, 2, tiles, TILE, LANES), F32)],
        input_output_aliases={0: 0},
        compiler_params=params,
        name="merge",
    )(*map(pin, (v, strips, strips_push)))
    return pl.pallas_call(
        functools.partial(combine, gx=gx),
        in_specs=[vmem] * (gx + 1),
        out_specs=[hbm] * 2,
        out_shape=[jax.ShapeDtypeStruct(load.shape, F32)] * 2,
        scratch_shapes=[pltpu.VMEM((2, *dims[1:], width), F32), pltpu.SemaphoreType.DMA((2, 2, TILE))],
        compiler_params=params,
        name="combine",
    )(*map(pin, gathered), pin(v))


def solution(mesh):
    return jax.shard_map(
        on_device,
        mesh=mesh,
        in_specs=(P("samp", None, "gx", "gy"), P("samp", "gx", "gy"), P()),
        out_specs=(P("samp", None, "gx", "gy"), P("samp", None, "gx", "gy")),
        check_vma=False,
    )
```
